256 devices in a mesh: gx: 32 (over z_hi, x, core), gy: 8 (over y, z_lo).
Axes of the slice: x: 4, y: 4, z: 8 (z_hi: 4, z_lo: 2; z = z_hi * 2 + z_lo), core: 2. Of those that a mesh axis runs over, the one named last changes fastest.
Arguments:
- voltage: float32 [256, 256, 128], P('gx', 'gy'), may hold values from -0.5 to 1.5
- potential: float32 [256, 256, 128], P('gx', 'gy'), may hold values from -6 to 6
- tissue: int32 [256, 256, 128], P('gx', 'gy'), may hold values 0 or 1
- gain: float32 [256, 256, 128], P('gx', 'gy'), may hold values from 0.25 to 1.75
- couplings: float32 [2, 9], replicated, may hold values from 0.05 to 0.5
- line_factor: float32 [256, 256], replicated, as said below
Outputs:
- new_voltage: float32 [256, 256, 128], P('gx', 'gy')
- new_potential: float32 [256, 256, 128], P('gx', 'gy')
The draws below stay inside these ranges and needn't reach their ends.
Inputs may be any that keep to these rules, and one draw needn't show every extreme that they name: line_factor is lower triangular with positive diagonal entries.
All inputs are finite; a program needn't handle non-finite values. No bound on the sum of `tissue` on one device may be relied on, other than what follows from the above.
Results may differ from the reference program's by a relative error of at most 0.0003.
Values sent between devices are 32-bit elements; how exact they have to be, the bound alone decides.
A program may use at most 64 MiB of HBM per device.

```python
import math
import jax
import jax.numpy as jnp
from jax import lax

NX = 128
NZ = 256
CHEB = 8
ITERS = 4
NY = 256


def draw_line_factor(key, part):
    diag_key = jax.random.fold_in(key, 11)
    rest_key = jax.random.fold_in(key, 12)
    diag_vals = jax.random.uniform(diag_key, (NZ,), jnp.float32, 1.0, 2.0)
    off_scale = 0.35
    lower = jnp.tril(jax.random.normal(rest_key, (NZ, NZ), jnp.float32), -1) * (off_scale / math.sqrt(NZ))
    return lower + jnp.diag(diag_vals)


def with_ends(array, own_key, least, top_value):
    shape = array.shape
    spot = [jax.random.randint(jax.random.fold_in(own_key, axis), (), 0, shape[axis]) for axis in range(len(shape))]
    array = array.at[tuple(spot)].set(least)
    longest = shape.index(max(shape))
    spot[longest] = (spot[longest] + 1) % shape[longest]
    return array.at[tuple(spot)].set(top_value)


def block_scale(own_key, shape, split, low, top_value):
    level, own = 1.0, jax.random.fold_in(own_key, 6)
    for axis_at, blocks in split:
        draws = jnp.exp(jax.random.uniform(jax.random.fold_in(own, axis_at), (blocks,), jnp.float32, low / len(split), top_value / len(split)))
        level = level * jnp.repeat(draws, shape[axis_at] // blocks).reshape([-1 if axis == axis_at else 1 for axis in range(len(shape))])
    return level


def bell_draw(stream_key, shape, width, reach, split=(), dtype=jnp.bfloat16):
    values = jax.random.normal(stream_key, shape, jnp.float32) * width
    if len(split) > 0:
        values = block_scale(stream_key, shape, split, -0.22, 0.18) * values
    return jnp.clip(values, min=-reach, max=reach).astype(dtype)


def setup_inputs(seed: int = 0) -> dict:
    splits = jax.random.split(jax.random.key(seed), 7)
    voltage = jnp.clip(-0.5 + 2.0 * jax.random.uniform(splits[0], (NZ, NY, NX), jnp.float32) ** block_scale(splits[0], (NZ, NY, NX), ((0, 32), (1, 8)), -0.2, 0.2), -0.5, 1.5)
    potential = bell_draw(splits[1], (NZ, NY, NX), 1.0, 6.0, ((0, 32), (1, 8)), jnp.float32)
    tissue = with_ends((jax.random.randint(splits[2], (NZ, NY, NX), 0, 4) < 3).astype(jnp.int32), jax.random.fold_in(splits[2], 1), 0, 1)
    gain = jnp.clip(1.0 + 0.15 * jax.random.normal(splits[3], (NZ, NY, NX), jnp.float32), 0.25, 1.75)
    couplings = jnp.clip(jnp.exp(jax.random.uniform(splits[4], (2, 9), jnp.float32, math.log(0.05), math.log(0.5))), 0.05, 0.5)
    line_factor = draw_line_factor(jax.random.fold_in(splits[6], 71), 0)
    return dict(voltage=voltage, potential=potential, tissue=tissue, gain=gain, couplings=couplings, line_factor=line_factor)


highest = lax.Precision.HIGHEST
time_step = 2.0
ionic_rate = 0.5
onset_level = 0.2
gain_top = 3.0625
neighbours = ((1, 0, 0, 0), (-1, 0, 0, 0), (0, 1, 0, 1), (0, -1, 0, 1), (0, 0, 1, 2), (0, 0, -1, 2),
              (1, 1, 0, 3), (-1, -1, 0, 3), (1, -1, 0, 4), (-1, 1, 0, 4), (1, 0, 1, 5), (-1, 0, -1, 5),
              (1, 0, -1, 6), (-1, 0, 1, 6), (0, 1, 1, 7), (0, -1, -1, 7), (0, 1, -1, 8), (0, -1, 1, 8))


def shifted(padded, move_z, move_y, move_x):
    extent_z, extent_y, extent_x = padded.shape
    return padded[1 + move_z:extent_z - 1 + move_z, 1 + move_y:extent_y - 1 + move_y, 1 + move_x:extent_x - 1 + move_x]


def fluxes(vector_pad, cond_pad, intra_coef, extra_coef):
    centre = shifted(vector_pad, 0, 0, 0)
    intra = jnp.zeros_like(centre)
    extra = jnp.zeros_like(centre)
    for move_z, move_y, move_x, column in neighbours:
        difference = centre - shifted(vector_pad, move_z, move_y, move_x)
        intra = intra + intra_coef[column] * shifted(cond_pad, move_z, move_y, move_x) * difference
        extra = extra + extra_coef[column] * difference
    return shifted(cond_pad, 0, 0, 0) * intra, extra


def along_lines(vector, line_factor):
    extent = vector.shape
    matrix = vector.reshape(extent[0], -1)
    first = jnp.dot(line_factor, matrix, precision=highest)
    second = jnp.dot(line_factor.T, first, precision=highest)
    return second.reshape(extent)


def reference(voltage, potential, tissue, gain, couplings, line_factor):
    mask_f = tissue.astype(jnp.float32)
    conduct = mask_f * gain
    cond_pad = jnp.pad(conduct, 1)
    intra_coef = couplings[0]
    extra_coef = couplings[1]
    volt_intra, volt_extra = fluxes(jnp.pad(voltage, 1), cond_pad, intra_coef, extra_coef)
    pot_intra, pot_extra = fluxes(jnp.pad(potential, 1), cond_pad, intra_coef, extra_coef)
    ionic = mask_f * voltage * (voltage - onset_level) * (voltage - 1.0)
    source = voltage - ionic_rate * ionic - time_step * pot_intra
    residual = source - (voltage + time_step * volt_intra)
    top_eig = 1.0 + time_step * 4.0 * gain_top * jnp.sum(intra_coef)
    centre_eig = (top_eig + 1.0) / 2.0
    half_width = (top_eig - 1.0) / 2.0
    spread_ratio = centre_eig / half_width
    weight_now = 1.0 / spread_ratio
    update = residual / centre_eig
    estimate = voltage
    for sweep in range(CHEB):
        estimate = estimate + update
        if sweep < CHEB - 1:
            upd_intra, upd_extra = fluxes(jnp.pad(update, 1), cond_pad, intra_coef, extra_coef)
            residual = residual - (update + time_step * upd_intra)
            weight_next = 1.0 / (2.0 * spread_ratio - weight_now)
            update = weight_next * weight_now * update + (2.0 * weight_next / half_width) * residual
            weight_now = weight_next
    est_intra, est_extra = fluxes(jnp.pad(estimate, 1), cond_pad, intra_coef, extra_coef)
    residual = -est_intra - (pot_intra + pot_extra)
    approx = potential
    smoothed = along_lines(residual, line_factor)
    search = smoothed
    energy = jnp.sum(residual * smoothed)
    for turn in range(ITERS):
        image_intra, image_extra = fluxes(jnp.pad(search, 1), cond_pad, intra_coef, extra_coef)
        image = image_intra + image_extra
        step_size = energy / jnp.sum(search * image)
        approx = approx + step_size * search
        if turn < ITERS - 1:
            residual = residual - step_size * image
            smoothed = along_lines(residual, line_factor)
            energy_new = jnp.sum(residual * smoothed)
            search = smoothed + (energy_new / energy) * search
            energy = energy_new
    return estimate, approx
```

```python
import jax
import jax.numpy as jnp
from jax import lax
from jax.experimental import pallas as pl
from jax.experimental.pallas import tpu as pltpu
from jax.sharding import PartitionSpec as P

CHEB = 8
SHIFT = 1.3
BASIS = 4
MESH = pl.DeviceIdType.MESH
HIGHEST = lax.Precision.HIGHEST
time_step = 2.0
ionic_rate = 0.5
onset_level = 0.2
gain_top = 3.0625

PLANES, ROWS, COLS = 8, 32, 128
HALO = 8
EXT_Z, EXT_Y = PLANES + 2 * HALO, ROWS + 2 * HALO
GX, GY = 32, 8
WHOLE_Z = GX * PLANES
WHOLE_Y = GY * ROWS
TILES = WHOLE_Z // 8
DIRECTIONS = tuple((a, b) for a in (-1, 0, 1) for b in (-1, 0, 1) if (a, b) != (0, 0))


def z_range(a, depth):
    if a == 0:
        return pl.ds(HALO, PLANES), pl.ds(HALO, PLANES)
    if a > 0:
        return pl.ds(HALO + PLANES - depth, depth), pl.ds(HALO - depth, depth)
    return pl.ds(HALO, depth), pl.ds(HALO + PLANES, depth)


def y_range(b):
    if b == 0:
        return pl.ds(HALO, ROWS), pl.ds(HALO, ROWS)
    if b > 0:
        return pl.ds(HALO + ROWS - 8, 8), pl.ds(0, 8)
    return pl.ds(HALO, 8), pl.ds(HALO + ROWS, 8)


def lane_shifts(v, first, last):
    up = jnp.where(last, 0.0, pltpu.roll(v, COLS - 1, 1))
    down = jnp.where(first, 0.0, pltpu.roll(v, 1, 1))
    return up, down


def stencil(minus, here, plus, k, first, last, swapped=False):
    rows = here.shape[0]
    lead, sub, lane = (k[1], k[0], k[2]) if swapped else (k[0], k[1], k[2])
    both, cross = k[3], k[4]
    lead_lane, lead_lane_cross = (k[7], k[8]) if swapped else (k[5], k[6])
    sub_lane, sub_lane_cross = (k[5], k[6]) if swapped else (k[7], k[8])
    right, left = lane_shifts(here, first, last)
    up = sub * here + both * plus + cross * minus + sub_lane * right + sub_lane_cross * left
    down = sub * here + both * minus + cross * plus + sub_lane * left + sub_lane_cross * right
    x_up = lane * here + lead_lane * plus + lead_lane_cross * minus
    x_down = lane * here + lead_lane * minus + lead_lane_cross * plus
    x_up = jnp.where(last, 0.0, pltpu.roll(x_up, COLS - 1, 1))
    x_down = jnp.where(first, 0.0, pltpu.roll(x_down, 1, 1))
    return lead * (plus + minus) + pltpu.roll(up, rows - 1, 0) + pltpu.roll(down, 1, 0) + x_up + x_down


def owner(row):
    chip_y = row // 64
    along = row % 64
    along = along + (chip_y % 2) * (63 - 2 * along)
    chip_z = along // 8
    spot = along % 8
    spot = spot + (chip_z % 2) * (7 - 2 * spot)
    return (chip_z // 2) * 8 + spot, chip_y * 2 + chip_z % 2


def own_row(gx, gy):
    chip_y = gy // 2
    chip_z = (gx // 8) * 2 + gy % 2
    spot = gx % 8
    spot = spot + (chip_z % 2) * (7 - 2 * spot)
    along = chip_z * 8 + spot
    return chip_y * 64 + along + (chip_y % 2) * (63 - 2 * along)


def kernel(
    coup, volt_in, pot_in, tissue_in, gain_in, factor_in, new_volt, new_pot,
    volt, pot, tissue, gain, factor,
    fields, resid, upd, diag, ionic_own, matrix,
    stage_cond, stage_res, stage_row,
    row_cond, row_res, lines, line_prev, line_next, cond_prev, cond_next,
    image, row_diag, back, part, gather_a, gather_b,
    s_fields, r_fields, s_cond, r_cond, s_resid, r_resid,
    s_rows, r_rows, s_edge, r_edge, s_back, r_back, s_sum, r_sum, s_local, s_take,
):
    gx = lax.axis_index("gx")
    gy = lax.axis_index("gy")
    row = own_row(gx, gy)
    own_gy = row // ROWS
    own_t = row % ROWS
    me_a = ((gx % 8) // 2) * 4 + gy // 2
    me_b = (gx // 8) * 4 + (gy % 2) * 2 + gx % 2

    def peer_a(p):
        return (gx // 8) * 8 + (p // 4) * 2 + gx % 2, (p % 4) * 2 + gy % 2

    def peer_b(p):
        return (p // 4) * 8 + ((gx % 8) // 2) * 2 + p % 2, (gy // 2) * 2 + (p % 4) // 2

    barrier = pltpu.get_barrier_semaphore()

    def greet(to):
        pl.semaphore_signal(barrier, inc=1, device_id=to, device_id_type=MESH)

    for a, b in DIRECTIONS:
        greet((lax.rem(gx + a + GX, GX), lax.rem(gy + b + GY, GY)))
    greet(owner(lax.rem(row + 1, WHOLE_Y)))
    greet(owner(lax.rem(row + WHOLE_Y - 1, WHOLE_Y)))

    def greet_sixteen(d, _):
        greet(peer_a(lax.rem(me_a + d, 16)))
        greet(peer_b(lax.rem(me_b + d, 16)))
        return 0

    lax.fori_loop(1, 16, greet_sixteen, 0)

    def greet_rows(t, _):
        to_gx, to_gy = owner(gy * ROWS + t)

        @pl.when(jnp.logical_not((to_gx == gx) & (to_gy == gy)))
        def _():
            greet((to_gx, to_gy))

        @pl.when(jnp.logical_not((t == gx) & (own_gy == gy)))
        def _():
            greet((t, own_gy))
        return 0

    lax.fori_loop(0, ROWS, greet_rows, 0)
    takes = [
        pltpu.make_async_copy(src, dst, s_take.at[n])
        for n, (src, dst) in enumerate(
            ((tissue_in, tissue), (gain_in, gain), (volt_in, volt), (pot_in, pot), (factor_in, factor)))
    ]
    for copy in takes:
        copy.start()
    for copy in takes:
        copy.wait()

    lane = lax.broadcasted_iota(jnp.int32, (1, COLS), 1)
    first, last = lane == 0, lane == COLS - 1
    k_in = [coup[0, n] for n in range(9)]
    k_ex = [coup[1, n] for n in range(9)]

    def neighbour(a, b):
        ok = (gx + a >= 0) & (gx + a < GX) & (gy + b >= 0) & (gy + b < GY)
        return ok, (gx + a, gy + b)

    def send_halo(ref, d, depth, sems_s, sems_r, stacked):
        a, b = DIRECTIONS[d]
        zs, zd = z_range(a, depth)
        ys, yd = y_range(b)
        src = ref.at[:, zs, ys, :] if stacked else ref.at[zs, ys, :]
        dst = ref.at[:, zd, yd, :] if stacked else ref.at[zd, yd, :]
        return pltpu.make_async_remote_copy(
            src_ref=src, dst_ref=dst, send_sem=sems_s.at[d], recv_sem=sems_r.at[d],
            device_id=(gx + a, gy + b), device_id_type=MESH)

    def each_halo(act, ref, depth, sems_s, sems_r, stacked, receive=False):
        for d, (a, b) in enumerate(DIRECTIONS):
            ok, _ = neighbour(-a, -b) if receive else neighbour(a, b)

            @pl.when(ok)
            def _():
                act(send_halo(ref, d, depth, sems_s, sems_r, stacked))

    def deep_conduct(d):
        a, b = DIRECTIONS[d]
        ys, yd = y_range(b)
        if a > 0:
            zs, zd = pl.ds(HALO, PLANES - 1), pl.ds(0, HALO - 1)
        else:
            zs, zd = pl.ds(HALO + 1, PLANES - 1), pl.ds(HALO + PLANES + 1, HALO - 1)
        return pltpu.make_async_remote_copy(
            src_ref=fields.at[2, zs, ys, :], dst_ref=fields.at[2, zd, yd, :],
            send_sem=s_cond.at[d], recv_sem=r_cond.at[d],
            device_id=(gx + a, gy + b), device_id_type=MESH)

    def each_deep(act, receive=False):
        for d, (a, b) in enumerate(DIRECTIONS):
            if a == 0:
                continue
            ok, _ = neighbour(-a, -b) if receive else neighbour(a, b)

            @pl.when(ok)
            def _():
                act(deep_conduct(d))

    def start(copy):
        copy.start()

    def wait_recv(copy):
        copy.wait_recv()

    def wait_send(copy):
        copy.wait_send()

    def scatter_rows(stage, rows_ref, n):
        def one(t, _):
            to_gx, to_gy = owner(gy * ROWS + t)
            mine = (to_gx == gx) & (to_gy == gy)

            @pl.when(mine)
            def _():
                pltpu.make_async_copy(stage.at[t], rows_ref.at[1 + gx], s_local.at[n]).start()

            @pl.when(jnp.logical_not(mine))
            def _():
                pltpu.make_async_remote_copy(
                    src_ref=stage.at[t], dst_ref=rows_ref.at[1 + gx],
                    send_sem=s_rows.at[n], recv_sem=r_rows.at[n],
                    device_id=(to_gx, to_gy), device_id_type=MESH).start()
            return 0

        lax.fori_loop(0, ROWS, one, 0)

    def wait_rows(stage, rows_ref, n):
        @pl.when(own_gy == gy)
        def _():
            pltpu.make_async_copy(stage.at[0], rows_ref.at[1], s_local.at[n]).wait()
            part_ref = rows_ref.at[pl.ds(1, TILES - 1)]
            pltpu.make_async_copy(part_ref, part_ref, r_rows.at[n]).wait()

        @pl.when(own_gy != gy)
        def _():
            part_ref = rows_ref.at[pl.ds(1, TILES)]
            pltpu.make_async_copy(part_ref, part_ref, r_rows.at[n]).wait()

    def wait_rows_sent(stage, n):
        @pl.when(own_gy == gy)
        def _():
            part_ref = stage.at[pl.ds(0, ROWS - 1)]
            pltpu.make_async_copy(part_ref, part_ref, s_rows.at[n]).wait()

        @pl.when(own_gy != gy)
        def _():
            pltpu.make_async_copy(stage, stage, s_rows.at[n]).wait()

    def send_back(k):
        def one(i, _):
            mine = (i == gx) & (own_gy == gy)

            @pl.when(mine)
            def _():
                pltpu.make_async_copy(lines.at[k, 1 + i], back.at[k, own_t], s_local.at[2 + k]).start()

            @pl.when(jnp.logical_not(mine))
            def _():
                pltpu.make_async_remote_copy(
                    src_ref=lines.at[k, 1 + i], dst_ref=back.at[k, own_t],
                    send_sem=s_back.at[k], recv_sem=r_back.at[k],
                    device_id=(i, own_gy), device_id_type=MESH).start()
            return 0

        lax.fori_loop(0, GX, one, 0)

    def wait_back(k):
        @pl.when(own_gy == gy)
        def _():
            pltpu.make_async_copy(lines.at[k, 1], back.at[k, 0], s_local.at[2 + k]).wait()
            got = back.at[k, pl.ds(0, ROWS - 1)]
            pltpu.make_async_copy(got, got, r_back.at[k]).wait()
            sent = lines.at[k, pl.ds(1, TILES - 1)]
            pltpu.make_async_copy(sent, sent, s_back.at[k]).wait()

        @pl.when(own_gy != gy)
        def _():
            pltpu.make_async_copy(back.at[k], back.at[k], r_back.at[k]).wait()
            sent = lines.at[k, pl.ds(1, TILES)]
            pltpu.make_async_copy(sent, sent, s_back.at[k]).wait()

    inner = pl.ds(1, TILES)

    def edge(src, dst, n, side):
        to_gx, to_gy = owner(row + (1 if side == 0 else -1))
        return pltpu.make_async_remote_copy(
            src_ref=src.at[inner], dst_ref=dst.at[inner],
            send_sem=s_edge.at[n, side], recv_sem=r_edge.at[n, side],
            device_id=(to_gx, to_gy), device_id_type=MESH)

    has_next, has_prev = row < WHOLE_Y - 1, row > 0

    def edges_start(src, prev, nxt, n):
        @pl.when(has_next)
        def _():
            edge(src, prev, n, 0).start()

        @pl.when(has_prev)
        def _():
            edge(src, nxt, n, 1).start()

    def edges_wait(src, prev, nxt, n):
        @pl.when(has_prev)
        def _():
            edge(src, prev, n, 0).wait_recv()

        @pl.when(has_next)
        def _():
            edge(src, nxt, n, 1).wait_recv()

    def edges_sent(src, prev, nxt, n):
        @pl.when(has_next)
        def _():
            edge(src, prev, n, 0).wait_send()

        @pl.when(has_prev)
        def _():
            edge(src, nxt, n, 1).wait_send()

    own_y = pl.ds(HALO, ROWS)
    mask = tissue[...].astype(jnp.float32)
    v = volt[...]
    conduct = mask * gain[...]
    own = (pl.ds(HALO, PLANES), own_y, slice(None))
    fields[0, *own] = v + pot[...]
    fields[1, *own] = pot[...]
    fields[2, *own] = conduct
    met = (gx >= 0) & (own_gy == gy)
    pl.semaphore_wait(barrier, 104 - 2 * met.astype(jnp.int32))
    each_halo(start, fields, 1, s_fields, r_fields, True)
    each_deep(start)
    ionic_own[...] = mask * v * (v - onset_level) * (v - 1.0)

    for d, (a, b) in enumerate(DIRECTIONS):
        ok, _ = neighbour(-a, -b)

        @pl.when(jnp.logical_not(ok))
        def _():
            zd = z_range(a, HALO)[1]
            yd = y_range(b)[1]
            shape = (zd.size, yd.size, COLS)
            for n in range(3):
                fields[n, zd, yd, :] = jnp.zeros(shape, jnp.float32)
            resid[zd, yd, :] = jnp.zeros(shape, jnp.float32)
    stage_cond[...] = jnp.swapaxes(conduct, 0, 1)
    tile = jnp.zeros((8, COLS), jnp.float32)
    for ref in (row_cond, row_res, cond_prev, cond_next):
        ref[0] = tile
        ref[TILES + 1] = tile
    for k in range(BASIS):
        for ref in (lines, line_prev, line_next):
            ref[k, 0] = tile
            ref[k, TILES + 1] = tile
    blank = jnp.zeros((TILES, 8, COLS), jnp.float32)

    @pl.when(jnp.logical_not(has_prev))
    def _():
        cond_prev[pl.ds(1, TILES)] = blank
        for k in range(BASIS):
            line_prev[k, pl.ds(1, TILES)] = blank

    @pl.when(jnp.logical_not(has_next))
    def _():
        cond_next[pl.ds(1, TILES)] = blank
        for k in range(BASIS):
            line_next[k, pl.ds(1, TILES)] = blank
    part[...] = jnp.zeros_like(part)

    whole = lax.dot_general(
        factor[...], factor[...], (((0,), (0,)), ((), ())), precision=HIGHEST,
        preferred_element_type=jnp.float32)
    in_sum = k_in[0]
    ex_sum = k_ex[0]
    for n in range(1, 9):
        in_sum = in_sum + k_in[n]
        ex_sum = ex_sum + k_ex[n]
    reach = jnp.max(jnp.sum(jnp.abs(whole), axis=1, keepdims=True), axis=0, keepdims=True)
    bound = reach * (4.0 * gain_top * in_sum + 4.0 * ex_sum)
    matrix[...] = whole * (1.0 / bound)
    eye = lax.broadcasted_iota(jnp.int32, whole.shape, 0) == lax.broadcasted_iota(jnp.int32, whole.shape, 1)
    mean = jnp.sum(jnp.sum(jnp.where(eye, whole, 0.0), axis=1, keepdims=True), axis=0, keepdims=True) / WHOLE_Z
    shift = SHIFT * mean * (2.0 * in_sum + 2.0 * ex_sum) / bound

    top = 1.0 + time_step * 4.0 * gain_top * in_sum
    ones = jnp.ones((1, COLS), jnp.float32)
    top = ones * top
    centre = (top + 1.0) / 2.0
    half = (top - 1.0) / 2.0
    ratio = centre / half
    weight = 1.0 / ratio

    each_halo(wait_recv, fields, 1, s_fields, r_fields, True, receive=True)

    def first_plane(z, _):
        s = stencil(fields[2, z - 1], fields[2, z], fields[2, z + 1], k_in, first, last)
        diag[z] = s
        w = [fields[2, z + n] * fields[0, z + n] for n in (-1, 0, 1)]
        c = fields[2, z]
        ki = c * (s * fields[0, z] - stencil(*w, k_in, first, last))
        r = -ionic_rate * ionic_own[z - HALO] - time_step * ki[HALO : HALO + ROWS]
        resid[z, own_y, :] = r
        return 0

    lax.fori_loop(HALO, HALO + PLANES, first_plane, 0)
    each_halo(start, resid, HALO, s_resid, r_resid, False)

    each_deep(wait_recv, receive=True)

    def diag_plane(z, _):
        diag[z] = stencil(fields[2, z - 1], fields[2, z], fields[2, z + 1], k_in, first, last)
        return 0

    lax.fori_loop(1, HALO, diag_plane, 0)
    lax.fori_loop(HALO + PLANES, EXT_Z - 1, diag_plane, 0)
    each_halo(wait_recv, resid, HALO, s_resid, r_resid, False, receive=True)

    scatter_rows(stage_cond, row_cond, 0)

    inv_centre = 1.0 / centre

    def first_update(z, _):
        upd[0, z] = resid[z] * inv_centre
        return 0

    lax.fori_loop(0, EXT_Z, first_update, 0)

    def add_update(slot):
        def one(z, _):
            fields[0, z] = fields[0, z] + upd[slot, z]
            return 0

        lax.fori_loop(HALO - 1, HALO + PLANES + 1, one, 0)
        new_volt[...] = new_volt[...] + upd[slot, pl.ds(HALO, PLANES), own_y, :]

    each_halo(wait_send, fields, 1, s_fields, r_fields, True)
    new_volt[...] = volt[...]
    add_update(0)

    def sweep(n, weight):
        old = lax.rem(n + 1, 2)
        new = lax.rem(n, 2)
        weight_next = 1.0 / (2.0 * ratio - weight)
        keep = weight_next * weight
        gain_r = 2.0 * weight_next / half

        def one(z, _):
            w = [fields[2, z + m] * upd[old, z + m] for m in (-1, 0, 1)]
            u = upd[old, z]
            c = fields[2, z]
            ki = c * (diag[z] * u - stencil(*w, k_in, first, last))
            r = resid[z] - (u + time_step * ki)
            resid[z] = r
            upd[new, z] = keep * u + gain_r * r
            return 0

        lax.fori_loop(n, EXT_Z - n, one, 0)
        add_update(new)
        return weight_next

    each_halo(wait_send, resid, HALO, s_resid, r_resid, False)
    lax.fori_loop(1, CHEB, sweep, weight)

    ex_total = 2.0 * ex_sum

    def elliptic_plane(z, _):
        c = fields[2, z]
        w = [fields[2, z + m] * fields[0, z + m] for m in (-1, 0, 1)]
        ki = c * (diag[z] * fields[0, z] - stencil(*w, k_in, first, last))
        p = [fields[1, z + m] for m in (-1, 0, 1)]
        ke = ex_total * p[1] - stencil(*p, k_ex, first, last)
        upd[0, z] = -ki - ke
        return 0

    lax.fori_loop(HALO, HALO + PLANES, elliptic_plane, 0)
    stage_res[...] = jnp.swapaxes(upd[0, pl.ds(HALO, PLANES), own_y, :], 0, 1)
    scatter_rows(stage_res, row_res, 1)

    wait_rows(stage_cond, row_cond, 0)
    edges_start(row_cond, cond_prev, cond_next, BASIS)
    wait_rows(stage_res, row_res, 1)

    def apply_matrix(src, k, shift=None):
        out = jnp.dot(matrix[...], src.reshape(WHOLE_Z, COLS), precision=HIGHEST,
                      preferred_element_type=jnp.float32)
        out = out.reshape(TILES, 8, COLS)
        if shift is not None:
            out = out - shift * lines[k - 1, inner]
        lines[k, inner] = out

    def product(e, a, b):
        total = jnp.sum(a * b, axis=0)
        part[pl.ds(e, 1), :] = jnp.sum(total, axis=0, keepdims=True)

    CHUNK = 8

    def chunk(ref, at):
        return ref[pl.ds(at, CHUNK + 2)].reshape((CHUNK + 2) * 8, COLS)

    def put(ref, at, value):
        ref[pl.ds(at, CHUNK)] = value[8 : 8 + CHUNK * 8].reshape(CHUNK, 8, COLS)

    def operate(k):
        def one(i, _):
            at = i * CHUNK
            c = [chunk(r, at) for r in (cond_prev, row_cond, cond_next)]
            s = [chunk(r, at) for r in (line_prev.at[k], lines.at[k], line_next.at[k])]
            w = [a * b for a, b in zip(c, s)]
            ki = c[1] * (chunk(row_diag, at) * s[1] - stencil(*w, k_in, first, last, True))
            ke = ex_total * s[1] - stencil(*s, k_ex, first, last, True)
            put(image.at[k], at, ki + ke)
            return 0

        lax.fori_loop(0, TILES // CHUNK, one, 0)

    def line_diag(i, _):
        at = i * CHUNK
        c = [chunk(r, at) for r in (cond_prev, row_cond, cond_next)]
        row_diag[pl.ds(at + 1, CHUNK)] = stencil(*c, k_in, first, last, True)[8 : 8 + CHUNK * 8].reshape(
            CHUNK, 8, COLS)
        return 0

    apply_matrix(row_res[inner], 0)
    edges_start(lines.at[0], line_prev.at[0], line_next.at[0], 0)
    send_back(0)
    product(0, lines[0, inner], row_res[inner])
    edges_wait(row_cond, cond_prev, cond_next, BASIS)
    row_diag[0] = tile
    row_diag[TILES + 1] = tile
    lax.fori_loop(0, TILES // CHUNK, line_diag, 0)

    at = BASIS
    for k in range(BASIS):
        edges_wait(lines.at[k], line_prev.at[k], line_next.at[k], k)
        operate(k)
        if k < BASIS - 1:
            apply_matrix(image[k], k + 1, shift)
            edges_start(lines.at[k + 1], line_prev.at[k + 1], line_next.at[k + 1], k + 1)
            send_back(k + 1)
            product(k + 1, lines[k + 1, inner], row_res[inner])
            for m in range(k + 1):
                product(at, lines[m, inner], image[k])
                at += 1
        else:
            for m in range(k):
                product(at, lines[k, inner], image[m])
                at += 1
            product(at, lines[k, inner], image[k])

    def sum_over(buf, n, me, peer):
        buf[me] = part[...]

        def one(d, _):
            to = lax.rem(me + d, 16)
            pltpu.make_async_remote_copy(
                src_ref=part, dst_ref=buf.at[me], send_sem=s_sum.at[n], recv_sem=r_sum.at[n],
                device_id=peer(to), device_id_type=MESH).start()
            return 0

        lax.fori_loop(1, 16, one, 0)
        got = buf.at[pl.ds(0, 15)]
        pltpu.make_async_copy(got, got, r_sum.at[n]).wait()
        pltpu.make_async_copy(got, got, s_sum.at[n]).wait()
        part[...] = jnp.sum(buf[...], axis=0)

    sum_over(gather_a, 0, me_a, peer_a)
    sum_over(gather_b, 1, me_b, peer_b)

    totals = jnp.broadcast_to(jnp.sum(part[...], axis=1, keepdims=True), (16, COLS))
    value = [totals[e : e + 1] for e in range(14)]
    rhs = value[:BASIS]
    gram = {}
    at = BASIS
    for k in range(BASIS - 1):
        for m in range(k + 1):
            gram[m, k] = value[at]
            at += 1
    for m in range(BASIS):
        gram[m, BASIS - 1] = value[at]
        at += 1

    low, pivot = {}, {}
    for j in range(BASIS):
        d = gram[j, j]
        for m in range(j):
            d = d - low[j, m] * low[j, m] * pivot[m]
        pivot[j] = d
        for i in range(j + 1, BASIS):
            e = gram[j, i]
            for m in range(j):
                e = e - low[i, m] * low[j, m] * pivot[m]
            low[i, j] = e / d
    sol = list(rhs)
    for i in range(BASIS):
        for m in range(i):
            sol[i] = sol[i] - low[i, m] * sol[m]
    sol = [a / pivot[i] for i, a in enumerate(sol)]
    for i in reversed(range(BASIS)):
        for m in range(i + 1, BASIS):
            sol[i] = sol[i] - low[m, i] * sol[m]

    for k in range(BASIS):
        wait_back(k)
    total = sol[0] * back[0]
    for k in range(1, BASIS):
        total = total + sol[k] * back[k]
    new_pot[...] = pot[...] + jnp.swapaxes(total, 0, 1)

    each_deep(wait_send)
    wait_rows_sent(stage_cond, 0)
    wait_rows_sent(stage_res, 1)
    edges_sent(row_cond, cond_prev, cond_next, BASIS)
    for k in range(BASIS):
        edges_sent(lines.at[k], line_prev.at[k], line_next.at[k], k)


def body(voltage, potential, tissue, gain, couplings, line_factor):
    f32 = jnp.float32
    block = jax.ShapeDtypeStruct((PLANES, ROWS, COLS), f32)
    vmem = pl.BlockSpec(memory_space=pltpu.VMEM)
    line = (TILES + 2, 8, COLS)
    dma = pltpu.SemaphoreType.DMA
    return pl.pallas_call(
        kernel,
        name="bidomain",
        out_shape=(block, block),
        in_specs=[pl.BlockSpec(memory_space=pltpu.SMEM)] + [pl.BlockSpec(memory_space=pl.ANY)] * 5,
        out_specs=(vmem, vmem),
        scratch_shapes=[
            pltpu.VMEM((PLANES, ROWS, COLS), f32),
            pltpu.VMEM((PLANES, ROWS, COLS), f32),
            pltpu.VMEM((PLANES, ROWS, COLS), jnp.int32),
            pltpu.VMEM((PLANES, ROWS, COLS), f32),
            pltpu.VMEM((WHOLE_Z, WHOLE_Z), f32),
            pltpu.VMEM((3, EXT_Z, EXT_Y, COLS), f32),
            pltpu.VMEM((EXT_Z, EXT_Y, COLS), f32),
            pltpu.VMEM((2, EXT_Z, EXT_Y, COLS), f32),
            pltpu.VMEM((EXT_Z, EXT_Y, COLS), f32),
            pltpu.VMEM((PLANES, ROWS, COLS), f32),
            pltpu.VMEM((WHOLE_Z, WHOLE_Z), f32),
            pltpu.VMEM((ROWS, PLANES, COLS), f32),
            pltpu.VMEM((ROWS, PLANES, COLS), f32),
            pltpu.VMEM((ROWS, PLANES, COLS), f32),
            pltpu.VMEM(line, f32),
            pltpu.VMEM(line, f32),
            pltpu.VMEM((BASIS, *line), f32),
            pltpu.VMEM((BASIS, *line), f32),
            pltpu.VMEM((BASIS, *line), f32),
            pltpu.VMEM(line, f32),
            pltpu.VMEM(line, f32),
            pltpu.VMEM((BASIS, TILES, 8, COLS), f32),
            pltpu.VMEM(line, f32),
            pltpu.VMEM((BASIS, ROWS, PLANES, COLS), f32),
            pltpu.VMEM((16, COLS), f32),
            pltpu.VMEM((16, 16, COLS), f32),
            pltpu.VMEM((16, 16, COLS), f32),
            dma((8,)), dma((8,)), dma((8,)), dma((8,)), dma((8,)), dma((8,)),
            dma((2,)), dma((2,)), dma((BASIS + 1, 2)), dma((BASIS + 1, 2)),
            dma((BASIS,)), dma((BASIS,)), dma((2,)), dma((2,)), dma((2 + BASIS,)), dma((5,)),
        ],
        compiler_params=pltpu.CompilerParams(
            collective_id=0, has_side_effects=True, vmem_limit_bytes=48 * 2**20),
    )(couplings, voltage, potential, tissue, gain, line_factor)


def solution(mesh):
    block = P("gx", "gy", None)
    return jax.shard_map(
        body, mesh=mesh, in_specs=(block, block, block, block, P(), P()),
        out_specs=(block, block), check_vma=False)
```

```python
import jax
import jax.numpy as jnp
from jax import lax
from jax.experimental import pallas as pl
from jax.experimental.pallas import tpu as pltpu
from jax.sharding import PartitionSpec as P

CHEB = 8
SHIFT = 1.3
BASIS = 4
MESH = pl.DeviceIdType.MESH
HIGHEST = lax.Precision.HIGHEST
time_step = 2.0
ionic_rate = 0.5
onset_level = 0.2
gain_top = 3.0625

PLANES, ROWS, COLS = 8, 32, 128
HALO = 8
EXT_Z, EXT_Y = PLANES + 2 * HALO, ROWS + 2 * HALO
GX, GY = 32, 8
WHOLE_Z = GX * PLANES
WHOLE_Y = GY * ROWS
TILES = WHOLE_Z // 8
DIRECTIONS = tuple((a, b) for a in (-1, 0, 1) for b in (-1, 0, 1) if (a, b) != (0, 0))


def z_range(a, depth):
    if a == 0:
        return pl.ds(HALO, PLANES), pl.ds(HALO, PLANES)
    if a > 0:
        return pl.ds(HALO + PLANES - depth, depth), pl.ds(HALO - depth, depth)
    return pl.ds(HALO, depth), pl.ds(HALO + PLANES, depth)


def y_range(b):
    if b == 0:
        return pl.ds(HALO, ROWS), pl.ds(HALO, ROWS)
    if b > 0:
        return pl.ds(HALO + ROWS - 8, 8), pl.ds(0, 8)
    return pl.ds(HALO, 8), pl.ds(HALO + ROWS, 8)


def lane_shifts(v, first, last):
    up = jnp.where(last, 0.0, pltpu.roll(v, COLS - 1, 1))
    down = jnp.where(first, 0.0, pltpu.roll(v, 1, 1))
    return up, down


def stencil(minus, here, plus, k, first, last, swapped=False):
    rows = here.shape[0]
    lead, sub, lane = (k[1], k[0], k[2]) if swapped else (k[0], k[1], k[2])
    both, cross = k[3], k[4]
    lead_lane, lead_lane_cross = (k[7], k[8]) if swapped else (k[5], k[6])
    sub_lane, sub_lane_cross = (k[5], k[6]) if swapped else (k[7], k[8])
    right, left = lane_shifts(here, first, last)
    up = sub * here + both * plus + cross * minus + sub_lane * right + sub_lane_cross * left
    down = sub * here + both * minus + cross * plus + sub_lane * left + sub_lane_cross * right
    x_up = lane * here + lead_lane * plus + lead_lane_cross * minus
    x_down = lane * here + lead_lane * minus + lead_lane_cross * plus
    x_up = jnp.where(last, 0.0, pltpu.roll(x_up, COLS - 1, 1))
    x_down = jnp.where(first, 0.0, pltpu.roll(x_down, 1, 1))
    return lead * (plus + minus) + pltpu.roll(up, rows - 1, 0) + pltpu.roll(down, 1, 0) + x_up + x_down


def owner(row):
    chip_y = row // 64
    along = row % 64
    along = along + (chip_y % 2) * (63 - 2 * along)
    chip_z = along // 8
    spot = along % 8
    spot = spot + (chip_z % 2) * (7 - 2 * spot)
    return (chip_z // 2) * 8 + spot, chip_y * 2 + chip_z % 2


def own_row(gx, gy):
    chip_y = gy // 2
    chip_z = (gx // 8) * 2 + gy % 2
    spot = gx % 8
    spot = spot + (chip_z % 2) * (7 - 2 * spot)
    along = chip_z * 8 + spot
    return chip_y * 64 + along + (chip_y % 2) * (63 - 2 * along)


def kernel(
    coup, volt_in, pot_in, tissue_in, gain_in, factor_in, new_volt, new_pot,
    volt, pot, tissue, gain, factor,
    fields, resid, upd, diag, estimate, own_term, matrix,
    stage_cond, stage_res,
    row_cond, row_res, lines, line_prev, line_next, cond_prev, cond_next,
    image, row_diag, back, part, gather_a, gather_b,
    s_fields, r_fields, s_cond, r_cond, s_pot, r_pot, s_resid, r_resid,
    s_rows, r_rows, s_edge, r_edge, s_back, r_back, s_sum, r_sum, s_take, far,
):
    gx = lax.axis_index("gx")
    gy = lax.axis_index("gy")
    row = own_row(gx, gy)
    own_gy = row // ROWS
    own_t = row % ROWS
    chip_z = (gx // 8) * 2 + gy % 2
    chip_y = gy // 2
    spot = gx % 8

    def at_z(z):
        return (z // 2) * 8 + spot, chip_y * 2 + z % 2

    def at_y(y):
        return gx, y * 2 + gy % 2

    barrier = pltpu.get_barrier_semaphore()

    def greet(sem, to):
        pl.semaphore_signal(sem, inc=1, device_id=to, device_id_type=MESH)

    for a, b in DIRECTIONS:
        greet(barrier, (lax.rem(gx + a + GX, GX), lax.rem(gy + b + GY, GY)))
    for d in range(1, 8):
        greet(barrier, at_z(lax.rem(chip_z + d, 8)))
        greet(barrier, ((gx // 8) * 8 + lax.rem(spot + d, 8), gy))
    for d in range(1, 4):
        greet(barrier, at_y(lax.rem(chip_y + d, 4)))
    takes = [
        pltpu.make_async_copy(src, dst, s_take.at[n])
        for n, (src, dst) in enumerate(
            ((tissue_in, tissue), (gain_in, gain), (volt_in, volt), (pot_in, pot), (factor_in, factor)))
    ]
    for copy in takes:
        copy.start()
    for copy in takes:
        copy.wait()

    lane = lax.broadcasted_iota(jnp.int32, (1, COLS), 1)
    first, last = lane == 0, lane == COLS - 1
    k_in = [coup[0, n] for n in range(9)]
    k_ex = [coup[1, n] for n in range(9)]

    def neighbour(a, b):
        ok = (gx + a >= 0) & (gx + a < GX) & (gy + b >= 0) & (gy + b < GY)
        return ok, (gx + a, gy + b)

    def send_halo(ref, d, depth, sems_s, sems_r, stacked):
        a, b = DIRECTIONS[d]
        zs, zd = z_range(a, depth)
        ys, yd = y_range(b)
        src = ref.at[:, zs, ys, :] if stacked else ref.at[zs, ys, :]
        dst = ref.at[:, zd, yd, :] if stacked else ref.at[zd, yd, :]
        return pltpu.make_async_remote_copy(
            src_ref=src, dst_ref=dst, send_sem=sems_s.at[d], recv_sem=sems_r.at[d],
            device_id=(gx + a, gy + b), device_id_type=MESH)

    def each_halo(act, ref, depth, sems_s, sems_r, stacked, receive=False):
        for d, (a, b) in enumerate(DIRECTIONS):
            ok, _ = neighbour(-a, -b) if receive else neighbour(a, b)

            @pl.when(ok)
            def _():
                act(send_halo(ref, d, depth, sems_s, sems_r, stacked))

    def deep_conduct(d):
        a, b = DIRECTIONS[d]
        ys, yd = y_range(b)
        if a > 0:
            zs, zd = pl.ds(HALO, PLANES - 1), pl.ds(0, HALO - 1)
        else:
            zs, zd = pl.ds(HALO + 1, PLANES - 1), pl.ds(HALO + PLANES + 1, HALO - 1)
        return pltpu.make_async_remote_copy(
            src_ref=fields.at[1, zs, ys, :], dst_ref=fields.at[1, zd, yd, :],
            send_sem=s_cond.at[d], recv_sem=r_cond.at[d],
            device_id=(gx + a, gy + b), device_id_type=MESH)

    def each_deep(act, receive=False):
        for d, (a, b) in enumerate(DIRECTIONS):
            if a == 0:
                continue
            ok, _ = neighbour(-a, -b) if receive else neighbour(a, b)

            @pl.when(ok)
            def _():
                act(deep_conduct(d))

    def start(copy):
        copy.start()

    def wait_recv(copy):
        copy.wait_recv()

    def wait_send(copy):
        copy.wait_send()

    own_group = own_gy == gy

    def scatter_rows(stage, rows_ref, n):
        def one(t, _):
            to_gx, to_gy = owner(gy * ROWS + t)

            @pl.when((to_gx != gx) | (to_gy != gy))
            def _():
                pltpu.make_async_remote_copy(
                    src_ref=stage.at[t], dst_ref=rows_ref.at[1 + gx],
                    send_sem=s_rows.at[n], recv_sem=r_rows.at[n],
                    device_id=(to_gx, to_gy), device_id_type=MESH).start()
            return 0

        lax.fori_loop(0, ROWS, one, 0, unroll=4)

        @pl.when(own_group)
        def _():
            rows_ref[1 + gx] = stage[own_t]

    def wait_rows(stage, rows_ref, n):
        @pl.when(own_group)
        def _():
            part_ref = rows_ref.at[pl.ds(1, TILES - 1)]
            pltpu.make_async_copy(part_ref, part_ref, r_rows.at[n]).wait()

        @pl.when(jnp.logical_not(own_group))
        def _():
            part_ref = rows_ref.at[pl.ds(1, TILES)]
            pltpu.make_async_copy(part_ref, part_ref, r_rows.at[n]).wait()

    def wait_rows_sent(stage, n):
        @pl.when(own_group)
        def _():
            part_ref = stage.at[pl.ds(0, ROWS - 1)]
            pltpu.make_async_copy(part_ref, part_ref, s_rows.at[n]).wait()

        @pl.when(jnp.logical_not(own_group))
        def _():
            pltpu.make_async_copy(stage, stage, s_rows.at[n]).wait()

    def send_back(n):
        two = pl.ds(2 * n, 2)

        def one(i, _):
            @pl.when((i != gx) | (own_gy != gy))
            def _():
                pltpu.make_async_remote_copy(
                    src_ref=lines.at[two, 1 + i], dst_ref=back.at[two, own_t],
                    send_sem=s_back.at[n], recv_sem=r_back.at[n],
                    device_id=(i, own_gy), device_id_type=MESH).start()
            return 0

        lax.fori_loop(0, GX, one, 0, unroll=4)

        @pl.when(own_group)
        def _():
            for k in (2 * n, 2 * n + 1):
                back[k, own_t] = lines[k, 1 + gx]

    def wait_back(n):
        two = pl.ds(2 * n, 2)

        @pl.when(own_group)
        def _():
            got = back.at[two, pl.ds(0, ROWS - 1)]
            pltpu.make_async_copy(got, got, r_back.at[n]).wait()
            pltpu.make_async_copy(got, got, s_back.at[n]).wait()

        @pl.when(jnp.logical_not(own_group))
        def _():
            got = back.at[two]
            pltpu.make_async_copy(got, got, r_back.at[n]).wait()
            pltpu.make_async_copy(got, got, s_back.at[n]).wait()

    inner = pl.ds(1, TILES)

    def edge(src, dst, n, side):
        to_gx, to_gy = owner(row + (1 if side == 0 else -1))
        return pltpu.make_async_remote_copy(
            src_ref=src.at[inner], dst_ref=dst.at[inner],
            send_sem=s_edge.at[n, side], recv_sem=r_edge.at[n, side],
            device_id=(to_gx, to_gy), device_id_type=MESH)

    has_next, has_prev = row < WHOLE_Y - 1, row > 0

    def edges_start(src, prev, nxt, n):
        @pl.when(has_next)
        def _():
            edge(src, prev, n, 0).start()

        @pl.when(has_prev)
        def _():
            edge(src, nxt, n, 1).start()

    def edges_wait(src, prev, nxt, n):
        @pl.when(has_prev)
        def _():
            edge(src, prev, n, 0).wait_recv()

        @pl.when(has_next)
        def _():
            edge(src, nxt, n, 1).wait_recv()

    def edges_sent(src, prev, nxt, n):
        @pl.when(has_next)
        def _():
            edge(src, prev, n, 0).wait_send()

        @pl.when(has_prev)
        def _():
            edge(src, nxt, n, 1).wait_send()

    own_y = pl.ds(HALO, ROWS)
    conduct = tissue[...].astype(jnp.float32) * gain[...]
    own = (pl.ds(HALO, PLANES), own_y, slice(None))
    fields[0, *own] = volt[...] + pot[...]
    fields[1, *own] = conduct
    fields[2, *own] = pot[...]
    pl.semaphore_wait(barrier, 25)
    near = fields.at[pl.ds(0, 2)]
    each_halo(start, near, 1, s_fields, r_fields, True)
    each_deep(start)
    each_halo(start, fields.at[2], 1, s_pot, r_pot, False)
    for d in range(1, 8):
        greet(far, at_z(lax.rem(chip_z + d, 8)))
    for d in range(1, 4):
        greet(far, at_y(lax.rem(chip_y + d, 4)))
    v = volt[...]
    ionic = tissue[...].astype(jnp.float32) * v * (v - onset_level) * (v - 1.0)
    own_term[...] = -ionic_rate * ionic

    for d, (a, b) in enumerate(DIRECTIONS):
        ok, _ = neighbour(-a, -b)

        @pl.when(jnp.logical_not(ok))
        def _():
            zd = z_range(a, HALO)[1]
            yd = y_range(b)[1]
            shape = (zd.size, yd.size, COLS)
            for n in range(3):
                fields[n, zd, yd, :] = jnp.zeros(shape, jnp.float32)
            resid[zd, yd, :] = jnp.zeros(shape, jnp.float32)
    stage_cond[...] = jnp.swapaxes(conduct, 0, 1)
    tile = jnp.zeros((8, COLS), jnp.float32)
    for ref in (row_cond, row_res, cond_prev, cond_next):
        ref[0] = tile
        ref[TILES + 1] = tile
    for k in range(BASIS):
        for ref in (lines, line_prev, line_next):
            ref[k, 0] = tile
            ref[k, TILES + 1] = tile
    blank = jnp.zeros((TILES, 8, COLS), jnp.float32)

    @pl.when(jnp.logical_not(has_prev))
    def _():
        cond_prev[pl.ds(1, TILES)] = blank
        for k in range(BASIS):
            line_prev[k, pl.ds(1, TILES)] = blank

    @pl.when(jnp.logical_not(has_next))
    def _():
        cond_next[pl.ds(1, TILES)] = blank
        for k in range(BASIS):
            line_next[k, pl.ds(1, TILES)] = blank

    whole = lax.dot_general(
        factor[...], factor[...], (((0,), (0,)), ((), ())), precision=HIGHEST,
        preferred_element_type=jnp.float32)
    in_sum = k_in[0]
    ex_sum = k_ex[0]
    for n in range(1, 9):
        in_sum = in_sum + k_in[n]
        ex_sum = ex_sum + k_ex[n]
    reach = jnp.max(jnp.sum(jnp.abs(whole), axis=1, keepdims=True), axis=0, keepdims=True)
    bound = reach * (4.0 * gain_top * in_sum + 4.0 * ex_sum)
    matrix[...] = whole * (1.0 / bound)
    eye = lax.broadcasted_iota(jnp.int32, whole.shape, 0) == lax.broadcasted_iota(jnp.int32, whole.shape, 1)
    mean = jnp.sum(jnp.sum(jnp.where(eye, whole, 0.0), axis=1, keepdims=True), axis=0, keepdims=True) / WHOLE_Z
    shift = SHIFT * mean * (2.0 * in_sum + 2.0 * ex_sum) / bound

    top = 1.0 + time_step * 4.0 * gain_top * in_sum
    ones = jnp.ones((1, COLS), jnp.float32)
    top = ones * top
    centre = (top + 1.0) / 2.0
    half = (top - 1.0) / 2.0
    ratio = centre / half
    weight = 1.0 / ratio

    each_halo(wait_recv, near, 1, s_fields, r_fields, True, receive=True)

    def first_plane(z, _):
        s = stencil(fields[1, z - 1], fields[1, z], fields[1, z + 1], k_in, first, last)
        diag[z] = s
        w = [fields[1, z + n] * fields[0, z + n] for n in (-1, 0, 1)]
        ki = fields[1, z] * (s * fields[0, z] - stencil(*w, k_in, first, last))
        resid[z, own_y, :] = own_term[z - HALO] - time_step * ki[HALO : HALO + ROWS]
        return 0

    lax.fori_loop(HALO, HALO + PLANES, first_plane, 0)
    each_halo(start, resid, HALO, s_resid, r_resid, False)

    each_deep(wait_recv, receive=True)

    def diag_plane(z, _):
        diag[z] = stencil(fields[1, z - 1], fields[1, z], fields[1, z + 1], k_in, first, last)
        return 0

    lax.fori_loop(1, HALO, diag_plane, 0)
    lax.fori_loop(HALO + PLANES, EXT_Z - 1, diag_plane, 0)
    each_halo(wait_recv, fields.at[2], 1, s_pot, r_pot, False, receive=True)
    ex_total = 2.0 * ex_sum

    def extra_plane(z, _):
        p = [fields[2, z + m] for m in (-1, 0, 1)]
        ke = stencil(*p, k_ex, first, last) - ex_total * p[1]
        own_term[z - HALO] = ke[HALO : HALO + ROWS]
        return 0

    lax.fori_loop(HALO, HALO + PLANES, extra_plane, 0)
    each_halo(wait_send, near, 1, s_fields, r_fields, True)
    pl.semaphore_wait(far, 10)
    each_halo(wait_recv, resid, HALO, s_resid, r_resid, False, receive=True)

    scatter_rows(stage_cond, row_cond, 0)

    inv_centre = 1.0 / centre

    def first_update(z, _):
        u = resid[z] * inv_centre
        upd[0, z] = u
        estimate[z] = u
        return 0

    lax.fori_loop(0, EXT_Z, first_update, 0)

    def sweep(n, weight):
        old = lax.rem(n + 1, 2)
        new = lax.rem(n, 2)
        weight_next = 1.0 / (2.0 * ratio - weight)
        keep = weight_next * weight
        gain_r = 2.0 * weight_next / half

        def pair(i, _):
            z = n + 2 * i
            c = [fields[1, z + m] for m in (-1, 0, 1, 2)]
            u = [upd[old, z + m] for m in (-1, 0, 1, 2)]
            w = [a * b for a, b in zip(c, u)]
            for m in (1, 2):
                ki = c[m] * (diag[z + m - 1] * u[m] - stencil(*w[m - 1 : m + 2], k_in, first, last))
                r = resid[z + m - 1] - (u[m] + time_step * ki)
                resid[z + m - 1] = r
                fresh = keep * u[m] + gain_r * r
                upd[new, z + m - 1] = fresh
                estimate[z + m - 1] = estimate[z + m - 1] + fresh
            return 0

        lax.fori_loop(0, EXT_Z // 2 - n, pair, 0)
        return weight_next

    each_halo(wait_send, resid, HALO, s_resid, r_resid, False)
    weight = lax.fori_loop(1, CHEB - 2, sweep, weight)
    wait_rows(stage_cond, row_cond, 0)
    edges_start(row_cond, cond_prev, cond_next, BASIS)
    lax.fori_loop(CHEB - 2, CHEB, sweep, weight)

    def total_plane(z, _):
        fields[0, z] = fields[0, z] + estimate[z]
        return 0

    lax.fori_loop(HALO - 1, HALO + PLANES + 1, total_plane, 0)

    def elliptic_plane(z, _):
        w = [fields[1, z + m] * fields[0, z + m] for m in (-1, 0, 1)]
        ki = fields[1, z] * (diag[z] * fields[0, z] - stencil(*w, k_in, first, last))
        own_term[z - HALO] = own_term[z - HALO] - ki[HALO : HALO + ROWS]
        return 0

    lax.fori_loop(HALO, HALO + PLANES, elliptic_plane, 0)
    stage_res[...] = jnp.swapaxes(own_term[...], 0, 1)
    scatter_rows(stage_res, row_res, 1)

    new_volt[...] = volt[...] + estimate[pl.ds(HALO, PLANES), own_y, :]
    wait_rows(stage_res, row_res, 1)

    def apply_matrix(src, k, shift=None):
        out = jnp.dot(matrix[...], src.reshape(WHOLE_Z, COLS), precision=HIGHEST,
                      preferred_element_type=jnp.float32)
        out = out.reshape(TILES, 8, COLS)
        if shift is not None:
            out = out - shift * lines[k - 1, inner]
        lines[k, inner] = out

    sums = jnp.zeros((1, COLS), jnp.float32)

    def product(sums, e, a, b):
        total = jnp.sum((a * b).reshape(4, TILES // 4, 8, COLS), axis=0)
        total = jnp.sum(jnp.sum(total, axis=0), axis=0, keepdims=True)
        return sums + jnp.where(lane == e, jnp.sum(total, axis=1, keepdims=True), 0.0)

    CHUNK = 8

    def chunk(ref, at):
        return ref[pl.ds(at, CHUNK + 2)].reshape((CHUNK + 2) * 8, COLS)

    def put(ref, at, value):
        ref[pl.ds(at, CHUNK)] = value[8 : 8 + CHUNK * 8].reshape(CHUNK, 8, COLS)

    def operate(k):
        def one(i, _):
            at = i * CHUNK
            c = [chunk(r, at) for r in (cond_prev, row_cond, cond_next)]
            s = [chunk(r, at) for r in (line_prev.at[k], lines.at[k], line_next.at[k])]
            w = [a * b for a, b in zip(c, s)]
            ki = c[1] * (chunk(row_diag, at) * s[1] - stencil(*w, k_in, first, last, True))
            ke = ex_total * s[1] - stencil(*s, k_ex, first, last, True)
            put(image.at[k], at, ki + ke)
            return 0

        lax.fori_loop(0, TILES // CHUNK, one, 0)

    def line_diag(i, _):
        at = i * CHUNK
        c = [chunk(r, at) for r in (cond_prev, row_cond, cond_next)]
        row_diag[pl.ds(at + 1, CHUNK)] = stencil(*c, k_in, first, last, True)[8 : 8 + CHUNK * 8].reshape(
            CHUNK, 8, COLS)
        return 0

    apply_matrix(row_res[inner], 0)
    edges_start(lines.at[0], line_prev.at[0], line_next.at[0], 0)
    edges_wait(row_cond, cond_prev, cond_next, BASIS)
    row_diag[0] = tile
    row_diag[TILES + 1] = tile
    lax.fori_loop(0, TILES // CHUNK, line_diag, 0)
    sums = product(sums, 0, lines[0, inner], row_res[inner])

    at = BASIS
    for k in range(BASIS):
        edges_wait(lines.at[k], line_prev.at[k], line_next.at[k], k)
        operate(k)
        if k < BASIS - 1:
            apply_matrix(image[k], k + 1, shift)
            edges_start(lines.at[k + 1], line_prev.at[k + 1], line_next.at[k + 1], k + 1)
            if k % 2 == 0:
                send_back(k // 2)
            sums = product(sums, k + 1, lines[k + 1, inner], row_res[inner])
            for m in range(k + 1):
                sums = product(sums, at, lines[m, inner], image[k])
                at += 1
            if k == BASIS - 2:
                for m in range(k + 1):
                    sums = product(sums, at, lines[k + 1, inner], image[m])
                    at += 1
        else:
            sums = product(sums, at, lines[k, inner], image[k])

    def sum_over(sums, buf, n, me, peers):
        part[...] = sums
        buf[me] = sums
        for to in peers:
            pltpu.make_async_remote_copy(
                src_ref=part, dst_ref=buf.at[me], send_sem=s_sum.at[n], recv_sem=r_sum.at[n],
                device_id=to, device_id_type=MESH).start()
        got = buf.at[pl.ds(0, 15)]
        pltpu.make_async_copy(got, got, r_sum.at[n]).wait()
        pltpu.make_async_copy(got, got, s_sum.at[n]).wait()
        return jnp.sum(buf[...], axis=0)

    def hops(d, n):
        return min(d, n - d)

    chip_x, core = spot // 2, spot % 2
    steps = sorted(((x, y) for x in range(4) for y in range(4) if (x, y) != (0, 0)),
                   key=lambda p: (-hops(p[0], 4) - hops(p[1], 4), p))
    sums = sum_over(sums, gather_a, 0, chip_x * 4 + chip_y, [
        ((gx // 8) * 8 + lax.rem(chip_x + x, 4) * 2 + core, lax.rem(chip_y + y, 4) * 2 + gy % 2)
        for x, y in steps])
    steps = sorted(((z, c) for z in range(8) for c in range(2) if (z, c) != (0, 0)),
                   key=lambda p: (-hops(p[0], 8) - 0.5 * p[1], p))
    peers = []
    for z, c in steps:
        to_z = lax.rem(chip_z + z, 8)
        peers.append(((to_z // 2) * 8 + chip_x * 2 + (core + c) % 2, chip_y * 2 + to_z % 2))
    sums = sum_over(sums, gather_b, 1, chip_z * 2 + core, peers)

    value = [jnp.sum(jnp.where(lane == e, sums, 0.0), axis=1, keepdims=True) for e in range(14)]
    rhs = value[:BASIS]
    gram = {}
    at = BASIS
    for k in range(BASIS):
        for m in range(k + 1):
            gram[m, k] = value[at]
            at += 1

    low, pivot = {}, {}
    for j in range(BASIS):
        d = gram[j, j]
        for m in range(j):
            d = d - low[j, m] * low[j, m] * pivot[m]
        pivot[j] = d
        for i in range(j + 1, BASIS):
            e = gram[j, i]
            for m in range(j):
                e = e - low[i, m] * low[j, m] * pivot[m]
            low[i, j] = e / d
    sol = list(rhs)
    for i in range(BASIS):
        for m in range(i):
            sol[i] = sol[i] - low[i, m] * sol[m]
    sol = [a / pivot[i] for i, a in enumerate(sol)]
    for i in reversed(range(BASIS)):
        for m in range(i + 1, BASIS):
            sol[i] = sol[i] - low[m, i] * sol[m]

    for n in range(2):
        wait_back(n)
    total = sol[0] * back[0]
    for k in range(1, BASIS):
        total = total + sol[k] * back[k]
    new_pot[...] = pot[...] + jnp.swapaxes(total, 0, 1)

    each_deep(wait_send)
    each_halo(wait_send, fields.at[2], 1, s_pot, r_pot, False)
    wait_rows_sent(stage_cond, 0)
    wait_rows_sent(stage_res, 1)
    edges_sent(row_cond, cond_prev, cond_next, BASIS)
    for k in range(BASIS):
        edges_sent(lines.at[k], line_prev.at[k], line_next.at[k], k)


def body(voltage, potential, tissue, gain, couplings, line_factor):
    f32 = jnp.float32
    block = jax.ShapeDtypeStruct((PLANES, ROWS, COLS), f32)
    vmem = pl.BlockSpec(memory_space=pltpu.VMEM)
    line = (TILES + 2, 8, COLS)
    dma = pltpu.SemaphoreType.DMA
    return pl.pallas_call(
        kernel,
        name="bidomain",
        out_shape=(block, block),
        in_specs=[pl.BlockSpec(memory_space=pltpu.SMEM)] + [pl.BlockSpec(memory_space=pl.ANY)] * 5,
        out_specs=(vmem, vmem),
        scratch_shapes=[
            pltpu.VMEM((PLANES, ROWS, COLS), f32),
            pltpu.VMEM((PLANES, ROWS, COLS), f32),
            pltpu.VMEM((PLANES, ROWS, COLS), jnp.int32),
            pltpu.VMEM((PLANES, ROWS, COLS), f32),
            pltpu.VMEM((WHOLE_Z, WHOLE_Z), f32),
            pltpu.VMEM((3, EXT_Z, EXT_Y, COLS), f32),
            pltpu.VMEM((EXT_Z, EXT_Y, COLS), f32),
            pltpu.VMEM((2, EXT_Z, EXT_Y, COLS), f32),
            pltpu.VMEM((EXT_Z, EXT_Y, COLS), f32),
            pltpu.VMEM((EXT_Z, EXT_Y, COLS), f32),
            pltpu.VMEM((PLANES, ROWS, COLS), f32),
            pltpu.VMEM((WHOLE_Z, WHOLE_Z), f32),
            pltpu.VMEM((ROWS, PLANES, COLS), f32),
            pltpu.VMEM((ROWS, PLANES, COLS), f32),
            pltpu.VMEM(line, f32),
            pltpu.VMEM(line, f32),
            pltpu.VMEM((BASIS, *line), f32),
            pltpu.VMEM((BASIS, *line), f32),
            pltpu.VMEM((BASIS, *line), f32),
            pltpu.VMEM(line, f32),
            pltpu.VMEM(line, f32),
            pltpu.VMEM((BASIS, TILES, 8, COLS), f32),
            pltpu.VMEM(line, f32),
            pltpu.VMEM((BASIS, ROWS, PLANES, COLS), f32),
            pltpu.VMEM((1, COLS), f32),
            pltpu.VMEM((16, 1, COLS), f32),
            pltpu.VMEM((16, 1, COLS), f32),
            dma((8,)), dma((8,)), dma((8,)), dma((8,)), dma((8,)), dma((8,)), dma((8,)), dma((8,)),
            dma((2,)), dma((2,)), dma((BASIS + 1, 2)), dma((BASIS + 1, 2)),
            dma((2,)), dma((2,)), dma((2,)), dma((2,)), dma((5,)), pltpu.SemaphoreType.REGULAR,
        ],
        compiler_params=pltpu.CompilerParams(
            collective_id=0, has_side_effects=True, vmem_limit_bytes=48 * 2**20),
    )(couplings, voltage, potential, tissue, gain, line_factor)


def solution(mesh):
    block = P("gx", "gy", None)
    return jax.shard_map(
        body, mesh=mesh, in_specs=(block, block, block, block, P(), P()),
        out_specs=(block, block), check_vma=False)
```

```python
import jax
import jax.numpy as jnp
from jax import lax
from jax.experimental import pallas as pl
from jax.experimental.pallas import tpu as pltpu
from jax.sharding import PartitionSpec as P

CHEB = 8
SHIFT = 1.3
BASIS = 4
MESH = pl.DeviceIdType.MESH
HIGHEST = lax.Precision.HIGHEST
time_step = 2.0
ionic_rate = 0.5
onset_level = 0.2
gain_top = 3.0625

PLANES, ROWS, COLS = 8, 32, 128
HALO = 8
EXT_Z, EXT_Y = PLANES + 2 * HALO, ROWS + 2 * HALO
PAD_Y = EXT_Y + 16
OWN = 8 + HALO
EXT = pl.ds(8, EXT_Y)
GX, GY = 32, 8
WHOLE_Z = GX * PLANES
WHOLE_Y = GY * ROWS
TILES = WHOLE_Z // 8
LINE = WHOLE_Z + 16
LINES = pl.ds(8, WHOLE_Z)
DIRECTIONS = tuple((a, b) for a in (-1, 0, 1) for b in (-1, 0, 1) if (a, b) != (0, 0))


def z_range(a, depth):
    if a == 0:
        return pl.ds(HALO, PLANES), pl.ds(HALO, PLANES)
    if a > 0:
        return pl.ds(HALO + PLANES - depth, depth), pl.ds(HALO - depth, depth)
    return pl.ds(HALO, depth), pl.ds(HALO + PLANES, depth)


def y_range(b):
    if b == 0:
        return pl.ds(OWN, ROWS), pl.ds(OWN, ROWS)
    if b > 0:
        return pl.ds(OWN + ROWS - 8, 8), pl.ds(OWN - 8, 8)
    return pl.ds(OWN, 8), pl.ds(OWN + ROWS, 8)


def combine(k, lead, sub, lane, lead_sub, lead_lane, sub_lane, scale=1.0):
    half = 0.5 * scale
    return dict(
        lead=scale * k[lead], sub=scale * k[sub], lane=scale * k[lane],
        both=scale * k[lead_sub], cross=scale * k[lead_sub + 1],
        lead_sum=half * (k[lead_lane] + k[lead_lane + 1]), lead_diff=half * (k[lead_lane] - k[lead_lane + 1]),
        sub_sum=half * (k[sub_lane] + k[sub_lane + 1]), sub_diff=half * (k[sub_lane] - k[sub_lane + 1]))


def stencil(read, k, first, last):
    here, plus, minus = read(0, 0), read(1, 0), read(-1, 0)
    up, down = read(0, 1), read(0, -1)
    total, diff = plus + minus, plus - minus
    rows, row_diff = up + down, up - down
    even = k["lane"] * here + k["lead_sum"] * total + k["sub_sum"] * rows
    odd = k["lead_diff"] * diff + k["sub_diff"] * row_diff
    out = k["lead"] * total + k["sub"] * rows
    out = out + k["both"] * (read(1, 1) + read(-1, -1)) + k["cross"] * (read(1, -1) + read(-1, 1))
    out = out + jnp.where(last, 0.0, pltpu.roll(even + odd, COLS - 1, 1))
    return out + jnp.where(first, 0.0, pltpu.roll(even - odd, 1, 1))


def owner(row):
    chip_y = row // 64
    along = row % 64
    along = along + (chip_y % 2) * (63 - 2 * along)
    chip_z = along // 8
    spot = along % 8
    spot = spot + (chip_z % 2) * (7 - 2 * spot)
    return (chip_z // 2) * 8 + spot, chip_y * 2 + chip_z % 2


def own_row(gx, gy):
    chip_y = gy // 2
    chip_z = (gx // 8) * 2 + gy % 2
    spot = gx % 8
    spot = spot + (chip_z % 2) * (7 - 2 * spot)
    along = chip_z * 8 + spot
    return chip_y * 64 + along + (chip_y % 2) * (63 - 2 * along)


def kernel(
    coup, volt_in, pot_in, tissue_in, gain_in, factor_in, new_volt, new_pot,
    volt, pot, tissue, gain, factor,
    fields, resid, upd, diag, estimate, weighted, own_term, matrix,
    stage_cond, stage_res,
    row_cond, row_res, lines, line_prev, line_next, cond_prev, cond_next,
    line_weighted, image, row_diag, back, part, gather_a, gather_b,
    s_fields, r_fields, s_cond, r_cond, s_pot, r_pot, s_resid, r_resid,
    s_rows, r_rows, s_edge, r_edge, s_back, r_back, s_sum, r_sum, s_take, far,
):
    gx = lax.axis_index("gx")
    gy = lax.axis_index("gy")
    row = own_row(gx, gy)
    own_gy = row // ROWS
    own_t = row % ROWS
    chip_z = (gx // 8) * 2 + gy % 2
    chip_y = gy // 2
    spot = gx % 8

    def at_z(z):
        return (z // 2) * 8 + spot, chip_y * 2 + z % 2

    def at_y(y):
        return gx, y * 2 + gy % 2

    takes = [
        pltpu.make_async_copy(src, dst, s_take.at[n])
        for n, (src, dst) in enumerate(
            ((tissue_in, tissue), (gain_in, gain), (volt_in, volt), (pot_in, pot), (factor_in, factor)))
    ]
    for copy in takes:
        copy.start()
    barrier = pltpu.get_barrier_semaphore()

    def greet(sem, to):
        pl.semaphore_signal(sem, inc=1, device_id=to, device_id_type=MESH)

    for a, b in DIRECTIONS:
        greet(barrier, (lax.rem(gx + a + GX, GX), lax.rem(gy + b + GY, GY)))
    for d in range(1, 8):
        greet(barrier, at_z(lax.rem(chip_z + d, 8)))
        greet(barrier, ((gx // 8) * 8 + lax.rem(spot + d, 8), gy))
    for d in range(1, 4):
        greet(barrier, at_y(lax.rem(chip_y + d, 4)))
    for copy in takes:
        copy.wait()

    lane = lax.broadcasted_iota(jnp.int32, (1, COLS), 1)
    first, last = lane == 0, lane == COLS - 1
    k_in = [coup[0, n] for n in range(9)]
    k_ex = [coup[1, n] for n in range(9)]
    z_twice = combine(k_in, 0, 1, 2, 3, 5, 7, time_step)
    z_extra = combine(k_ex, 0, 1, 2, 3, 5, 7)
    line_in = combine(k_in, 1, 0, 2, 3, 7, 5)
    line_ex = combine(k_ex, 1, 0, 2, 3, 7, 5)

    def neighbour(a, b):
        ok = (gx + a >= 0) & (gx + a < GX) & (gy + b >= 0) & (gy + b < GY)
        return ok, (gx + a, gy + b)

    def send_halo(ref, d, depth, sems_s, sems_r, stacked):
        a, b = DIRECTIONS[d]
        zs, zd = z_range(a, depth)
        ys, yd = y_range(b)
        src = ref.at[:, zs, ys, :] if stacked else ref.at[zs, ys, :]
        dst = ref.at[:, zd, yd, :] if stacked else ref.at[zd, yd, :]
        return pltpu.make_async_remote_copy(
            src_ref=src, dst_ref=dst, send_sem=sems_s.at[d], recv_sem=sems_r.at[d],
            device_id=(gx + a, gy + b), device_id_type=MESH)

    def each_halo(act, ref, depth, sems_s, sems_r, stacked, receive=False):
        for d, (a, b) in enumerate(DIRECTIONS):
            ok, _ = neighbour(-a, -b) if receive else neighbour(a, b)

            @pl.when(ok)
            def _():
                act(send_halo(ref, d, depth, sems_s, sems_r, stacked))

    def deep_conduct(d):
        a, b = DIRECTIONS[d]
        ys, yd = y_range(b)
        if a > 0:
            zs, zd = pl.ds(HALO, PLANES - 1), pl.ds(0, HALO - 1)
        else:
            zs, zd = pl.ds(HALO + 1, PLANES - 1), pl.ds(HALO + PLANES + 1, HALO - 1)
        return pltpu.make_async_remote_copy(
            src_ref=fields.at[1, zs, ys, :], dst_ref=fields.at[1, zd, yd, :],
            send_sem=s_cond.at[d], recv_sem=r_cond.at[d],
            device_id=(gx + a, gy + b), device_id_type=MESH)

    def each_deep(act, receive=False):
        for d, (a, b) in enumerate(DIRECTIONS):
            if a == 0:
                continue
            ok, _ = neighbour(-a, -b) if receive else neighbour(a, b)

            @pl.when(ok)
            def _():
                act(deep_conduct(d))

    def start(copy):
        copy.start()

    def wait_recv(copy):
        copy.wait_recv()

    def wait_send(copy):
        copy.wait_send()

    own_group = own_gy == gy

    def row_tile(i):
        return pl.ds(pl.multiple_of(8 + 8 * i, 8), 8)

    turned = chip_y % 2
    upper = gy % 2 + turned * (1 - 2 * (gy % 2))

    def scatter_rows(stage, rows_ref, n):
        for z in range(4):
            for q in range(8):
                m = z * 8 + (q if z % 2 == 0 else 7 - q)
                t = m + turned * (31 - 2 * m)
                to_gx, to_gy = upper * 16 + (z // 2) * 8 + q, chip_y * 2 + z % 2

                @pl.when((to_gx != gx) | (to_gy != gy))
                def _():
                    pltpu.make_async_remote_copy(
                        src_ref=stage.at[t], dst_ref=rows_ref.at[row_tile(gx)],
                        send_sem=s_rows.at[n], recv_sem=r_rows.at[n],
                        device_id=(to_gx, to_gy), device_id_type=MESH).start()

        @pl.when(own_group)
        def _():
            rows_ref[row_tile(gx)] = stage[own_t]

    def wait_rows(stage, rows_ref, n):
        @pl.when(own_group)
        def _():
            part_ref = rows_ref.at[pl.ds(8, WHOLE_Z - 8)]
            pltpu.make_async_copy(part_ref, part_ref, r_rows.at[n]).wait()

        @pl.when(jnp.logical_not(own_group))
        def _():
            part_ref = rows_ref.at[LINES]
            pltpu.make_async_copy(part_ref, part_ref, r_rows.at[n]).wait()

    def wait_rows_sent(stage, n):
        @pl.when(own_group)
        def _():
            part_ref = stage.at[pl.ds(0, ROWS - 1)]
            pltpu.make_async_copy(part_ref, part_ref, s_rows.at[n]).wait()

        @pl.when(jnp.logical_not(own_group))
        def _():
            pltpu.make_async_copy(stage, stage, s_rows.at[n]).wait()

    def send_back(k):
        def one(i, _):
            @pl.when((i != gx) | (own_gy != gy))
            def _():
                pltpu.make_async_remote_copy(
                    src_ref=lines.at[k, row_tile(i)], dst_ref=back.at[k, own_t],
                    send_sem=s_back.at[k], recv_sem=r_back.at[k],
                    device_id=(i, own_gy), device_id_type=MESH).start()
            return 0

        lax.fori_loop(0, GX, one, 0, unroll=4)

        @pl.when(own_group)
        def _():
            back[k, own_t] = lines[k, row_tile(gx)]

    def wait_back(k):
        @pl.when(own_group)
        def _():
            got = back.at[k, pl.ds(0, ROWS - 1)]
            pltpu.make_async_copy(got, got, r_back.at[k]).wait()
            pltpu.make_async_copy(got, got, s_back.at[k]).wait()

        @pl.when(jnp.logical_not(own_group))
        def _():
            pltpu.make_async_copy(back.at[k], back.at[k], r_back.at[k]).wait()
            pltpu.make_async_copy(back.at[k], back.at[k], s_back.at[k]).wait()

    inner = LINES

    def edge(src, dst, n, side):
        to_gx, to_gy = owner(row + (1 if side == 0 else -1))
        return pltpu.make_async_remote_copy(
            src_ref=src.at[inner], dst_ref=dst.at[inner],
            send_sem=s_edge.at[n, side], recv_sem=r_edge.at[n, side],
            device_id=(to_gx, to_gy), device_id_type=MESH)

    has_next, has_prev = row < WHOLE_Y - 1, row > 0

    def edges_start(src, prev, nxt, n):
        @pl.when(has_next)
        def _():
            edge(src, prev, n, 0).start()

        @pl.when(has_prev)
        def _():
            edge(src, nxt, n, 1).start()

    def edges_wait(src, prev, nxt, n):
        @pl.when(has_prev)
        def _():
            edge(src, prev, n, 0).wait_recv()

        @pl.when(has_next)
        def _():
            edge(src, nxt, n, 1).wait_recv()

    def edges_sent(src, prev, nxt, n):
        @pl.when(has_next)
        def _():
            edge(src, prev, n, 0).wait_send()

        @pl.when(has_prev)
        def _():
            edge(src, nxt, n, 1).wait_send()

    own_y = pl.ds(OWN, ROWS)
    conduct = tissue[...].astype(jnp.float32) * gain[...]
    own = (pl.ds(HALO, PLANES), own_y, slice(None))
    fields[0, *own] = volt[...] + pot[...]
    fields[1, *own] = conduct
    fields[2, *own] = pot[...]
    pl.semaphore_wait(barrier, 25)
    near = fields.at[pl.ds(0, 2)]
    each_halo(start, near, 1, s_fields, r_fields, True)
    each_halo(start, fields.at[2], 1, s_pot, r_pot, False)
    each_deep(start)
    for d in range(1, 8):
        greet(far, at_z(lax.rem(chip_z + d, 8)))
    for d in range(1, 4):
        greet(far, at_y(lax.rem(chip_y + d, 4)))
    v = volt[...]
    ionic = tissue[...].astype(jnp.float32) * v * (v - onset_level) * (v - 1.0)
    own_term[...] = -ionic_rate * ionic

    for d, (a, b) in enumerate(DIRECTIONS):
        ok, _ = neighbour(-a, -b)

        @pl.when(jnp.logical_not(ok))
        def _():
            zd = z_range(a, HALO)[1]
            yd = y_range(b)[1]
            shape = (zd.size, yd.size, COLS)
            for n in range(3):
                fields[n, zd, yd, :] = jnp.zeros(shape, jnp.float32)
            resid[zd, yd, :] = jnp.zeros(shape, jnp.float32)
    stage_cond[...] = jnp.swapaxes(conduct, 0, 1)
    tile = jnp.zeros((8, COLS), jnp.float32)
    beyond = (pl.ds(0, 8), pl.ds(PAD_Y - 8, 8))

    def blank_rows(z, _):
        for rows in beyond:
            fields[1, z, rows, :] = tile
            weighted[0, z, rows, :] = tile
            weighted[1, z, rows, :] = tile
        return 0

    lax.fori_loop(0, EXT_Z, blank_rows, 0)
    ends = (pl.ds(0, 8), pl.ds(LINE - 8, 8))
    for rows in ends:
        for ref in (row_cond, row_res, cond_prev, cond_next):
            ref[rows] = tile
        for k in range(BASIS):
            for ref in (lines, line_prev, line_next):
                ref[k, rows] = tile
    blank = jnp.zeros((WHOLE_Z, COLS), jnp.float32)

    @pl.when(jnp.logical_not(has_prev))
    def _():
        cond_prev[LINES] = blank
        for k in range(BASIS):
            line_prev[k, LINES] = blank

    @pl.when(jnp.logical_not(has_next))
    def _():
        cond_next[LINES] = blank
        for k in range(BASIS):
            line_next[k, LINES] = blank

    whole = lax.dot_general(
        factor[...], factor[...], (((0,), (0,)), ((), ())), precision=HIGHEST,
        preferred_element_type=jnp.float32)
    in_sum = k_in[0]
    ex_sum = k_ex[0]
    for n in range(1, 9):
        in_sum = in_sum + k_in[n]
        ex_sum = ex_sum + k_ex[n]
    reach = jnp.max(jnp.sum(jnp.abs(whole), axis=1, keepdims=True), axis=0, keepdims=True)
    bound = reach * (4.0 * gain_top * in_sum + 4.0 * ex_sum)
    matrix[...] = whole * (1.0 / bound)
    eye = lax.broadcasted_iota(jnp.int32, whole.shape, 0) == lax.broadcasted_iota(jnp.int32, whole.shape, 1)
    mean = jnp.sum(jnp.sum(jnp.where(eye, whole, 0.0), axis=1, keepdims=True), axis=0, keepdims=True) / WHOLE_Z
    shift = SHIFT * mean * (2.0 * in_sum + 2.0 * ex_sum) / bound

    top = 1.0 + time_step * 4.0 * gain_top * in_sum
    ones = jnp.ones((1, COLS), jnp.float32)
    top = ones * top
    centre = (top + 1.0) / 2.0
    half = (top - 1.0) / 2.0
    ratio = centre / half
    weight = 1.0 / ratio

    each_halo(wait_recv, near, 1, s_fields, r_fields, True, receive=True)

    def moved(ref, z, at, rows):
        return lambda i, j: ref[z + i, pl.ds(at + j, rows), :]

    cond = fields.at[1]

    def weigh(z, _):
        weighted[0, z, EXT, :] = cond[z, EXT, :] * (fields[0, z, EXT, :])
        return 0

    lax.fori_loop(HALO - 1, HALO + PLANES + 1, weigh, 0)

    def first_plane(z, _):
        s = stencil(moved(cond, z, OWN, ROWS), z_twice, first, last)
        flux = s * fields[0, z, own_y, :] - stencil(moved(weighted.at[0], z, OWN, ROWS), z_twice, first, last)
        resid[z, own_y, :] = own_term[z - HALO] - cond[z, own_y, :] * flux
        return 0

    lax.fori_loop(HALO, HALO + PLANES, first_plane, 0)
    each_halo(start, resid, HALO, s_resid, r_resid, False)

    each_halo(wait_recv, fields.at[2], 1, s_pot, r_pot, False, receive=True)
    ex_total = 2.0 * ex_sum

    def extra_plane(z, _):
        ke = stencil(moved(fields.at[2], z, OWN, ROWS), z_extra, first, last)
        own_term[z - HALO] = ke - ex_total * fields[2, z, own_y, :]
        return 0

    lax.fori_loop(HALO, HALO + PLANES, extra_plane, 0)
    each_deep(wait_recv, receive=True)

    def diag_plane(z, _):
        diag[z, EXT, :] = 1.0 + cond[z, EXT, :] * stencil(moved(cond, z, 8, EXT_Y), z_twice, first, last)
        return 0

    lax.fori_loop(1, EXT_Z - 1, diag_plane, 0)
    each_halo(wait_send, near, 1, s_fields, r_fields, True)
    pl.semaphore_wait(far, 10)
    scatter_rows(stage_cond, row_cond, 0)
    each_halo(wait_recv, resid, HALO, s_resid, r_resid, False, receive=True)

    inv_centre = 1.0 / centre

    def first_update(z, _):
        u = resid[z, EXT, :] * inv_centre
        upd[z, EXT, :] = u
        estimate[z, EXT, :] = u
        weighted[0, z, EXT, :] = cond[z, EXT, :] * u
        return 0

    lax.fori_loop(0, EXT_Z, first_update, 0)

    def sweep(n, weight):
        old = weighted.at[lax.rem(n + 1, 2)]
        new = lax.rem(n, 2)
        weight_next = 1.0 / (2.0 * ratio - weight)
        keep = weight_next * weight
        gain_r = 2.0 * weight_next / half

        def one(z):
            u = upd[z, EXT, :]
            c = cond[z, EXT, :]
            r = resid[z, EXT, :] - diag[z, EXT, :] * u + c * stencil(moved(old, z, 8, EXT_Y), z_twice, first, last)
            resid[z, EXT, :] = r
            fresh = keep * u + gain_r * r
            upd[z, EXT, :] = fresh
            estimate[z, EXT, :] = estimate[z, EXT, :] + fresh
            weighted[new, z, EXT, :] = c * fresh

        def pair(i, _):
            one(n + 2 * i)
            one(n + 2 * i + 1)
            return 0

        lax.fori_loop(0, EXT_Z // 2 - n, pair, 0)
        return weight_next

    each_halo(wait_send, resid, HALO, s_resid, r_resid, False)
    weight = lax.fori_loop(1, CHEB - 2, sweep, weight)
    wait_rows(stage_cond, row_cond, 0)
    edges_start(row_cond, cond_prev, cond_next, BASIS)
    lax.fori_loop(CHEB - 2, CHEB, sweep, weight)

    def total_plane(z, _):
        total = fields[0, z, EXT, :] + estimate[z, EXT, :]
        fields[0, z, EXT, :] = total
        weighted[0, z, EXT, :] = cond[z, EXT, :] * total
        return 0

    lax.fori_loop(HALO - 1, HALO + PLANES + 1, total_plane, 0)

    def elliptic_plane(z, _):
        twice = (diag[z, own_y, :] - 1.0) * fields[0, z, own_y, :]
        twice = twice - cond[z, own_y, :] * stencil(moved(weighted.at[0], z, OWN, ROWS), z_twice, first, last)
        own_term[z - HALO] = own_term[z - HALO] - twice / time_step
        return 0

    lax.fori_loop(HALO, HALO + PLANES, elliptic_plane, 0)
    stage_res[...] = jnp.swapaxes(own_term[...], 0, 1)
    scatter_rows(stage_res, row_res, 1)

    new_volt[...] = volt[...] + estimate[pl.ds(HALO, PLANES), own_y, :]
    wait_rows(stage_res, row_res, 1)

    def apply_matrix(src, k, shift=None):
        out = jnp.dot(matrix[...], src, precision=HIGHEST, preferred_element_type=jnp.float32)
        if shift is not None:
            out = out - shift * lines[k - 1, LINES]
        lines[k, LINES] = out

    sums = jnp.zeros((1, COLS), jnp.float32)

    def product(sums, e, a, b):
        total = jnp.sum((a * b).reshape(4, TILES // 4, 8, COLS), axis=0)
        total = jnp.sum(jnp.sum(total, axis=0), axis=0, keepdims=True)
        return sums + jnp.where(lane == e, jnp.sum(total, axis=1, keepdims=True), 0.0)

    CHUNK = 64

    def near_rows(refs, at):
        return lambda i, j: refs[i + 1][pl.ds(at + j, CHUNK), :]

    weigh_refs = [line_weighted.at[n] for n in range(3)]
    cond_refs = [cond_prev, row_cond, cond_next]

    def operate(k):
        basis = [line_prev.at[k], lines.at[k], line_next.at[k]]
        for n in (0, 2):
            weigh_refs[n][...] = cond_refs[n][...] * basis[n][...]
        for at in range(8, 8 + WHOLE_Z, CHUNK):
            rows = pl.ds(at, CHUNK)
            s = lines[k, rows]
            ki = row_diag[rows] * s - row_cond[rows] * stencil(near_rows(weigh_refs, at), line_in, first, last)
            image[k, pl.ds(at - 8, CHUNK)] = ki - stencil(near_rows(basis, at), line_ex, first, last)

    def line_diag():
        for at in range(8, 8 + WHOLE_Z, CHUNK):
            rows = pl.ds(at, CHUNK)
            row_diag[rows] = ex_total + row_cond[rows] * stencil(near_rows(cond_refs, at), line_in, first, last)

    apply_matrix(row_res[inner], 0)
    edges_start(lines.at[0], line_prev.at[0], line_next.at[0], 0)
    send_back(0)
    weigh_refs[1][...] = row_cond[...] * lines[0]
    edges_wait(row_cond, cond_prev, cond_next, BASIS)
    line_diag()
    sums = product(sums, 0, lines[0, inner], row_res[inner])

    at = BASIS
    for k in range(BASIS):
        edges_wait(lines.at[k], line_prev.at[k], line_next.at[k], k)
        operate(k)
        if k < BASIS - 1:
            apply_matrix(image[k], k + 1, shift)
            edges_start(lines.at[k + 1], line_prev.at[k + 1], line_next.at[k + 1], k + 1)
            send_back(k + 1)
            weigh_refs[1][...] = row_cond[...] * lines[k + 1]
            sums = product(sums, k + 1, lines[k + 1, inner], row_res[inner])
            for m in range(k + 1):
                sums = product(sums, at, lines[m, inner], image[k])
                at += 1
            if k == BASIS - 2:
                for m in range(k + 1):
                    sums = product(sums, at, lines[k + 1, inner], image[m])
                    at += 1
        else:
            sums = product(sums, at, lines[k, inner], image[k])

    def sum_over(sums, buf, n, me, peers):
        part[...] = sums
        buf[me] = sums
        for to in peers:
            pltpu.make_async_remote_copy(
                src_ref=part, dst_ref=buf.at[me], send_sem=s_sum.at[n], recv_sem=r_sum.at[n],
                device_id=to, device_id_type=MESH).start()
        got = buf.at[pl.ds(0, 15)]
        pltpu.make_async_copy(got, got, r_sum.at[n]).wait()
        pltpu.make_async_copy(got, got, s_sum.at[n]).wait()
        return jnp.sum(buf[...], axis=0)

    def hops(d, n):
        return min(d, n - d)

    chip_x, core = spot // 2, spot % 2
    steps = sorted(((x, y) for x in range(4) for y in range(4) if (x, y) != (0, 0)),
                   key=lambda p: (-hops(p[0], 4) - hops(p[1], 4), p))
    sums = sum_over(sums, gather_a, 0, chip_x * 4 + chip_y, [
        ((gx // 8) * 8 + lax.rem(chip_x + x, 4) * 2 + core, lax.rem(chip_y + y, 4) * 2 + gy % 2)
        for x, y in steps])
    steps = sorted(((z, c) for z in range(8) for c in range(2) if (z, c) != (0, 0)),
                   key=lambda p: (-hops(p[0], 8) - 0.5 * p[1], p))
    peers = []
    for z, c in steps:
        to_z = lax.rem(chip_z + z, 8)
        peers.append(((to_z // 2) * 8 + chip_x * 2 + (core + c) % 2, chip_y * 2 + to_z % 2))
    sums = sum_over(sums, gather_b, 1, chip_z * 2 + core, peers)

    value = [jnp.sum(jnp.where(lane == e, sums, 0.0), axis=1, keepdims=True) for e in range(14)]
    rhs = value[:BASIS]
    gram = {}
    at = BASIS
    for k in range(BASIS):
        for m in range(k + 1):
            gram[m, k] = value[at]
            at += 1

    low, pivot = {}, {}
    for j in range(BASIS):
        d = gram[j, j]
        for m in range(j):
            d = d - low[j, m] * low[j, m] * pivot[m]
        pivot[j] = d
        for i in range(j + 1, BASIS):
            e = gram[j, i]
            for m in range(j):
                e = e - low[i, m] * low[j, m] * pivot[m]
            low[i, j] = e / d
    sol = list(rhs)
    for i in range(BASIS):
        for m in range(i):
            sol[i] = sol[i] - low[i, m] * sol[m]
    sol = [a / pivot[i] for i, a in enumerate(sol)]
    for i in reversed(range(BASIS)):
        for m in range(i + 1, BASIS):
            sol[i] = sol[i] - low[m, i] * sol[m]

    for k in range(BASIS):
        wait_back(k)
    total = sol[0] * back[0]
    for k in range(1, BASIS):
        total = total + sol[k] * back[k]
    new_pot[...] = pot[...] + jnp.swapaxes(total, 0, 1)

    each_deep(wait_send)
    each_halo(wait_send, fields.at[2], 1, s_pot, r_pot, False)
    wait_rows_sent(stage_cond, 0)
    wait_rows_sent(stage_res, 1)
    edges_sent(row_cond, cond_prev, cond_next, BASIS)
    for k in range(BASIS):
        edges_sent(lines.at[k], line_prev.at[k], line_next.at[k], k)


def body(voltage, potential, tissue, gain, couplings, line_factor):
    f32 = jnp.float32
    block = jax.ShapeDtypeStruct((PLANES, ROWS, COLS), f32)
    vmem = pl.BlockSpec(memory_space=pltpu.VMEM)
    line = (LINE, COLS)
    dma = pltpu.SemaphoreType.DMA
    return pl.pallas_call(
        kernel,
        name="bidomain",
        out_shape=(block, block),
        in_specs=[pl.BlockSpec(memory_space=pltpu.SMEM)] + [pl.BlockSpec(memory_space=pl.ANY)] * 5,
        out_specs=(vmem, vmem),
        scratch_shapes=[
            pltpu.VMEM((PLANES, ROWS, COLS), f32),
            pltpu.VMEM((PLANES, ROWS, COLS), f32),
            pltpu.VMEM((PLANES, ROWS, COLS), jnp.int32),
            pltpu.VMEM((PLANES, ROWS, COLS), f32),
            pltpu.VMEM((WHOLE_Z, WHOLE_Z), f32),
            pltpu.VMEM((3, EXT_Z, PAD_Y, COLS), f32),
            pltpu.VMEM((EXT_Z, PAD_Y, COLS), f32),
            pltpu.VMEM((EXT_Z, PAD_Y, COLS), f32),
            pltpu.VMEM((EXT_Z, PAD_Y, COLS), f32),
            pltpu.VMEM((EXT_Z, PAD_Y, COLS), f32),
            pltpu.VMEM((2, EXT_Z, PAD_Y, COLS), f32),
            pltpu.VMEM((PLANES, ROWS, COLS), f32),
            pltpu.VMEM((WHOLE_Z, WHOLE_Z), f32),
            pltpu.VMEM((ROWS, PLANES, COLS), f32),
            pltpu.VMEM((ROWS, PLANES, COLS), f32),
            pltpu.VMEM(line, f32),
            pltpu.VMEM(line, f32),
            pltpu.VMEM((BASIS, *line), f32),
            pltpu.VMEM((BASIS, *line), f32),
            pltpu.VMEM((BASIS, *line), f32),
            pltpu.VMEM(line, f32),
            pltpu.VMEM(line, f32),
            pltpu.VMEM((3, *line), f32),
            pltpu.VMEM((BASIS, WHOLE_Z, COLS), f32),
            pltpu.VMEM(line, f32),
            pltpu.VMEM((BASIS, ROWS, PLANES, COLS), f32),
            pltpu.VMEM((1, COLS), f32),
            pltpu.VMEM((16, 1, COLS), f32),
            pltpu.VMEM((16, 1, COLS), f32),
            dma((8,)), dma((8,)), dma((8,)), dma((8,)), dma((8,)), dma((8,)), dma((8,)), dma((8,)),
            dma((2,)), dma((2,)), dma((BASIS + 1, 2)), dma((BASIS + 1, 2)),
            dma((BASIS,)), dma((BASIS,)), dma((2,)), dma((2,)), dma((5,)), pltpu.SemaphoreType.REGULAR,
        ],
        compiler_params=pltpu.CompilerParams(
            collective_id=0, has_side_effects=True, vmem_limit_bytes=48 * 2**20),
    )(couplings, voltage, potential, tissue, gain, line_factor)


def solution(mesh):
    block = P("gx", "gy", None)
    return jax.shard_map(
        body, mesh=mesh, in_specs=(block, block, block, block, P(), P()),
        out_specs=(block, block), check_vma=False)
```

```python
import jax
import jax.numpy as jnp
from jax import lax
from jax.experimental import pallas as pl
from jax.experimental.pallas import tpu as pltpu
from jax.sharding import PartitionSpec as P

CHEB = 8
SHIFT = 1.3
BASIS = 4
MESH = pl.DeviceIdType.MESH
HIGHEST = lax.Precision.HIGHEST
time_step = 2.0
ionic_rate = 0.5
onset_level = 0.2
gain_top = 3.0625

PLANES, ROWS, COLS = 8, 32, 128
HALO = 8
EXT_Z, EXT_Y = PLANES + 2 * HALO, ROWS + 2 * HALO
PAD_Y = EXT_Y + 16
OWN = 8 + HALO
EXT = pl.ds(8, EXT_Y)
GX, GY = 32, 8
WHOLE_Z = GX * PLANES
WHOLE_Y = GY * ROWS
TILES = WHOLE_Z // 8
LINE = WHOLE_Z + 16
LINES = pl.ds(8, WHOLE_Z)
DIRECTIONS = tuple((a, b) for a in (-1, 0, 1) for b in (-1, 0, 1) if (a, b) != (0, 0))


def z_range(a, depth):
    if a == 0:
        return pl.ds(HALO, PLANES), pl.ds(HALO, PLANES)
    if a > 0:
        return pl.ds(HALO + PLANES - depth, depth), pl.ds(HALO - depth, depth)
    return pl.ds(HALO, depth), pl.ds(HALO + PLANES, depth)


def y_range(b):
    if b == 0:
        return pl.ds(OWN, ROWS), pl.ds(OWN, ROWS)
    if b > 0:
        return pl.ds(OWN + ROWS - 8, 8), pl.ds(OWN - 8, 8)
    return pl.ds(OWN, 8), pl.ds(OWN + ROWS, 8)


def combine(k, lead, sub, lane, lead_sub, lead_lane, sub_lane, scale=1.0):
    half = 0.5 * scale
    return dict(
        lead=scale * k[lead], sub=scale * k[sub], lane=scale * k[lane],
        both=scale * k[lead_sub], cross=scale * k[lead_sub + 1],
        lead_sum=half * (k[lead_lane] + k[lead_lane + 1]), lead_diff=half * (k[lead_lane] - k[lead_lane + 1]),
        sub_sum=half * (k[sub_lane] + k[sub_lane + 1]), sub_diff=half * (k[sub_lane] - k[sub_lane + 1]))


def shift_lanes(even, odd, first, last):
    right = jnp.where(last, 0.0, pltpu.roll(even + odd, COLS - 1, 1))
    return right + jnp.where(first, 0.0, pltpu.roll(even - odd, 1, 1))


def stencil_here(read, k, first, last):
    up, down = read(0, 1), read(0, -1)
    rows = up + down
    even = k["lane"] * read(0, 0) + k["sub_sum"] * rows
    return k["sub"] * rows + shift_lanes(even, k["sub_diff"] * (up - down), first, last)


def stencil_beside(read, k, first, last):
    plus, minus = read(1, 0), read(-1, 0)
    total = plus + minus
    out = k["lead"] * total
    out = out + k["both"] * (read(1, 1) + read(-1, -1)) + k["cross"] * (read(1, -1) + read(-1, 1))
    return out + shift_lanes(k["lead_sum"] * total, k["lead_diff"] * (plus - minus), first, last)


def stencil(read, k, first, last):
    here, plus, minus = read(0, 0), read(1, 0), read(-1, 0)
    up, down = read(0, 1), read(0, -1)
    total, diff = plus + minus, plus - minus
    rows, row_diff = up + down, up - down
    even = k["lane"] * here + k["lead_sum"] * total + k["sub_sum"] * rows
    odd = k["lead_diff"] * diff + k["sub_diff"] * row_diff
    out = k["lead"] * total + k["sub"] * rows
    out = out + k["both"] * (read(1, 1) + read(-1, -1)) + k["cross"] * (read(1, -1) + read(-1, 1))
    return out + shift_lanes(even, odd, first, last)


def owner(row):
    chip_y = row // 64
    along = row % 64
    along = along + (chip_y % 2) * (63 - 2 * along)
    chip_z = along // 8
    spot = along % 8
    spot = spot + (chip_z % 2) * (7 - 2 * spot)
    return (chip_z // 2) * 8 + spot, chip_y * 2 + chip_z % 2


def own_row(gx, gy):
    chip_y = gy // 2
    chip_z = (gx // 8) * 2 + gy % 2
    spot = gx % 8
    spot = spot + (chip_z % 2) * (7 - 2 * spot)
    along = chip_z * 8 + spot
    return chip_y * 64 + along + (chip_y % 2) * (63 - 2 * along)


def kernel(
    coup, volt_in, pot_in, tissue_in, gain_in, factor_in, new_volt, new_pot,
    volt, pot, tissue, gain, factor,
    fields, resid, upd, diag, estimate, weighted, own_term, matrix,
    stage_cond, stage_res,
    row_cond, row_res, lines, line_prev, line_next, cond_prev, cond_next,
    line_weighted, image, row_diag, back, part, gather_a, gather_b,
    s_fields, r_fields, s_cond, r_cond, s_pot, r_pot, s_resid, r_resid,
    s_rows, r_rows, s_edge, r_edge, s_back, r_back, s_sum, r_sum, s_take, far,
):
    gx = lax.axis_index("gx")
    gy = lax.axis_index("gy")
    row = own_row(gx, gy)
    own_gy = row // ROWS
    own_t = row % ROWS
    chip_z = (gx // 8) * 2 + gy % 2
    chip_y = gy // 2
    spot = gx % 8

    def at_z(z):
        return (z // 2) * 8 + spot, chip_y * 2 + z % 2

    def at_y(y):
        return gx, y * 2 + gy % 2

    takes = [
        pltpu.make_async_copy(src, dst, s_take.at[n])
        for n, (src, dst) in enumerate(
            ((tissue_in, tissue), (gain_in, gain), (volt_in, volt), (pot_in, pot), (factor_in, factor)))
    ]
    for copy in takes:
        copy.start()
    barrier = pltpu.get_barrier_semaphore()

    def greet(sem, to):
        pl.semaphore_signal(sem, inc=1, device_id=to, device_id_type=MESH)

    for a, b in DIRECTIONS:
        greet(barrier, (lax.rem(gx + a + GX, GX), lax.rem(gy + b + GY, GY)))
    for d in range(1, 8):
        greet(barrier, at_z(lax.rem(chip_z + d, 8)))
        greet(barrier, ((gx // 8) * 8 + lax.rem(spot + d, 8), gy))
    for d in range(1, 4):
        greet(barrier, at_y(lax.rem(chip_y + d, 4)))
    for copy in takes:
        copy.wait()

    lane = lax.broadcasted_iota(jnp.int32, (1, COLS), 1)
    first, last = lane == 0, lane == COLS - 1
    k_in = [coup[0, n] for n in range(9)]
    k_ex = [coup[1, n] for n in range(9)]
    z_twice = combine(k_in, 0, 1, 2, 3, 5, 7, time_step)
    z_extra = combine(k_ex, 0, 1, 2, 3, 5, 7)
    line_in = combine(k_in, 1, 0, 2, 3, 7, 5)
    line_ex = combine(k_ex, 1, 0, 2, 3, 7, 5)

    def neighbour(a, b):
        ok = (gx + a >= 0) & (gx + a < GX) & (gy + b >= 0) & (gy + b < GY)
        return ok, (gx + a, gy + b)

    def send_halo(ref, d, depth, sems_s, sems_r, stacked):
        a, b = DIRECTIONS[d]
        zs, zd = z_range(a, depth)
        ys, yd = y_range(b)
        src = ref.at[:, zs, ys, :] if stacked else ref.at[zs, ys, :]
        dst = ref.at[:, zd, yd, :] if stacked else ref.at[zd, yd, :]
        return pltpu.make_async_remote_copy(
            src_ref=src, dst_ref=dst, send_sem=sems_s.at[d], recv_sem=sems_r.at[d],
            device_id=(gx + a, gy + b), device_id_type=MESH)

    def each_halo(act, ref, depth, sems_s, sems_r, stacked, receive=False):
        for d, (a, b) in enumerate(DIRECTIONS):
            ok, _ = neighbour(-a, -b) if receive else neighbour(a, b)

            @pl.when(ok)
            def _():
                act(send_halo(ref, d, depth, sems_s, sems_r, stacked))

    def deep_conduct(d):
        a, b = DIRECTIONS[d]
        ys, yd = y_range(b)
        if a > 0:
            zs, zd = pl.ds(HALO, PLANES - 1), pl.ds(0, HALO - 1)
        else:
            zs, zd = pl.ds(HALO + 1, PLANES - 1), pl.ds(HALO + PLANES + 1, HALO - 1)
        return pltpu.make_async_remote_copy(
            src_ref=fields.at[1, zs, ys, :], dst_ref=fields.at[1, zd, yd, :],
            send_sem=s_cond.at[d], recv_sem=r_cond.at[d],
            device_id=(gx + a, gy + b), device_id_type=MESH)

    def each_deep(act, receive=False):
        for d, (a, b) in enumerate(DIRECTIONS):
            if a == 0:
                continue
            ok, _ = neighbour(-a, -b) if receive else neighbour(a, b)

            @pl.when(ok)
            def _():
                act(deep_conduct(d))

    def start(copy):
        copy.start()

    def wait_recv(copy):
        copy.wait_recv()

    def wait_send(copy):
        copy.wait_send()

    own_group = own_gy == gy

    def row_tile(i):
        return pl.ds(pl.multiple_of(8 + 8 * i, 8), 8)

    turned = chip_y % 2
    upper = gy % 2 + turned * (1 - 2 * (gy % 2))

    def scatter_rows(stage, rows_ref, n):
        for z in range(4):
            for q in range(8):
                m = z * 8 + (q if z % 2 == 0 else 7 - q)
                t = m + turned * (31 - 2 * m)
                to_gx, to_gy = upper * 16 + (z // 2) * 8 + q, chip_y * 2 + z % 2

                @pl.when((to_gx != gx) | (to_gy != gy))
                def _():
                    pltpu.make_async_remote_copy(
                        src_ref=stage.at[t], dst_ref=rows_ref.at[row_tile(gx)],
                        send_sem=s_rows.at[n], recv_sem=r_rows.at[n],
                        device_id=(to_gx, to_gy), device_id_type=MESH).start()

        @pl.when(own_group)
        def _():
            rows_ref[row_tile(gx)] = stage[own_t]

    def wait_rows(stage, rows_ref, n):
        @pl.when(own_group)
        def _():
            part_ref = rows_ref.at[pl.ds(8, WHOLE_Z - 8)]
            pltpu.make_async_copy(part_ref, part_ref, r_rows.at[n]).wait()

        @pl.when(jnp.logical_not(own_group))
        def _():
            part_ref = rows_ref.at[LINES]
            pltpu.make_async_copy(part_ref, part_ref, r_rows.at[n]).wait()

    def wait_rows_sent(stage, n):
        @pl.when(own_group)
        def _():
            part_ref = stage.at[pl.ds(0, ROWS - 1)]
            pltpu.make_async_copy(part_ref, part_ref, s_rows.at[n]).wait()

        @pl.when(jnp.logical_not(own_group))
        def _():
            pltpu.make_async_copy(stage, stage, s_rows.at[n]).wait()

    def send_back(k):
        def one(i, _):
            @pl.when((i != gx) | (own_gy != gy))
            def _():
                pltpu.make_async_remote_copy(
                    src_ref=lines.at[k, row_tile(i)], dst_ref=back.at[k, own_t],
                    send_sem=s_back.at[k], recv_sem=r_back.at[k],
                    device_id=(i, own_gy), device_id_type=MESH).start()
            return 0

        lax.fori_loop(0, GX, one, 0, unroll=4)

        @pl.when(own_group)
        def _():
            back[k, own_t] = lines[k, row_tile(gx)]

    def wait_back(k):
        @pl.when(own_group)
        def _():
            got = back.at[k, pl.ds(0, ROWS - 1)]
            pltpu.make_async_copy(got, got, r_back.at[k]).wait()
            pltpu.make_async_copy(got, got, s_back.at[k]).wait()

        @pl.when(jnp.logical_not(own_group))
        def _():
            pltpu.make_async_copy(back.at[k], back.at[k], r_back.at[k]).wait()
            pltpu.make_async_copy(back.at[k], back.at[k], s_back.at[k]).wait()

    inner = LINES

    def edge(src, dst, n, side):
        to_gx, to_gy = owner(row + (1 if side == 0 else -1))
        return pltpu.make_async_remote_copy(
            src_ref=src.at[inner], dst_ref=dst.at[inner],
            send_sem=s_edge.at[n, side], recv_sem=r_edge.at[n, side],
            device_id=(to_gx, to_gy), device_id_type=MESH)

    has_next, has_prev = row < WHOLE_Y - 1, row > 0

    def edges_start(src, prev, nxt, n):
        @pl.when(has_next)
        def _():
            edge(src, prev, n, 0).start()

        @pl.when(has_prev)
        def _():
            edge(src, nxt, n, 1).start()

    def edges_wait(src, prev, nxt, n):
        @pl.when(has_prev)
        def _():
            edge(src, prev, n, 0).wait_recv()

        @pl.when(has_next)
        def _():
            edge(src, nxt, n, 1).wait_recv()

    def edges_sent(src, prev, nxt, n):
        @pl.when(has_next)
        def _():
            edge(src, prev, n, 0).wait_send()

        @pl.when(has_prev)
        def _():
            edge(src, nxt, n, 1).wait_send()

    own_y = pl.ds(OWN, ROWS)
    conduct = tissue[...].astype(jnp.float32) * gain[...]
    own = (pl.ds(HALO, PLANES), own_y, slice(None))
    fields[0, *own] = volt[...] + pot[...]
    fields[1, *own] = conduct
    fields[2, *own] = pot[...]
    pl.semaphore_wait(barrier, 25)
    near = fields.at[pl.ds(0, 2)]
    each_halo(start, near, 1, s_fields, r_fields, True)
    each_halo(start, fields.at[2], 1, s_pot, r_pot, False)
    each_deep(start)
    for d in range(1, 8):
        greet(far, at_z(lax.rem(chip_z + d, 8)))
    for d in range(1, 4):
        greet(far, at_y(lax.rem(chip_y + d, 4)))
    v = volt[...]
    ionic = tissue[...].astype(jnp.float32) * v * (v - onset_level) * (v - 1.0)
    own_term[...] = -ionic_rate * ionic

    for d, (a, b) in enumerate(DIRECTIONS):
        ok, _ = neighbour(-a, -b)

        @pl.when(jnp.logical_not(ok))
        def _():
            zd = z_range(a, HALO)[1]
            yd = y_range(b)[1]
            shape = (zd.size, yd.size, COLS)
            for n in range(3):
                fields[n, zd, yd, :] = jnp.zeros(shape, jnp.float32)
            resid[zd, yd, :] = jnp.zeros(shape, jnp.float32)
    stage_cond[...] = jnp.swapaxes(conduct, 0, 1)
    tile = jnp.zeros((8, COLS), jnp.float32)
    beyond = (pl.ds(0, 8), pl.ds(PAD_Y - 8, 8))

    def blank_rows(z, _):
        for rows in beyond:
            fields[1, z, rows, :] = tile
            weighted[0, z, rows, :] = tile
            weighted[1, z, rows, :] = tile
        return 0

    lax.fori_loop(0, EXT_Z, blank_rows, 0)
    ends = (pl.ds(0, 8), pl.ds(LINE - 8, 8))
    for rows in ends:
        for ref in (row_cond, row_res, cond_prev, cond_next):
            ref[rows] = tile
        for k in range(BASIS):
            for ref in (lines, line_prev, line_next):
                ref[k, rows] = tile
    blank = jnp.zeros((WHOLE_Z, COLS), jnp.float32)

    @pl.when(jnp.logical_not(has_prev))
    def _():
        cond_prev[LINES] = blank
        for k in range(BASIS):
            line_prev[k, LINES] = blank

    @pl.when(jnp.logical_not(has_next))
    def _():
        cond_next[LINES] = blank
        for k in range(BASIS):
            line_next[k, LINES] = blank

    whole = lax.dot_general(
        factor[...], factor[...], (((0,), (0,)), ((), ())), precision=HIGHEST,
        preferred_element_type=jnp.float32)
    in_sum = k_in[0]
    ex_sum = k_ex[0]
    for n in range(1, 9):
        in_sum = in_sum + k_in[n]
        ex_sum = ex_sum + k_ex[n]
    reach = jnp.max(jnp.sum(jnp.abs(whole), axis=1, keepdims=True), axis=0, keepdims=True)
    bound = reach * (4.0 * gain_top * in_sum + 4.0 * ex_sum)
    scaled = whole * (1.0 / bound)
    coarse = scaled.astype(jnp.bfloat16)
    matrix[0] = coarse
    matrix[1] = (scaled - coarse.astype(jnp.float32)).astype(jnp.bfloat16)
    eye = lax.broadcasted_iota(jnp.int32, whole.shape, 0) == lax.broadcasted_iota(jnp.int32, whole.shape, 1)
    mean = jnp.sum(jnp.sum(jnp.where(eye, whole, 0.0), axis=1, keepdims=True), axis=0, keepdims=True) / WHOLE_Z
    shift = SHIFT * mean * (2.0 * in_sum + 2.0 * ex_sum) / bound

    top = 1.0 + time_step * 4.0 * gain_top * in_sum
    ones = jnp.ones((1, COLS), jnp.float32)
    top = ones * top
    centre = (top + 1.0) / 2.0
    half = (top - 1.0) / 2.0
    ratio = centre / half
    weight = 1.0 / ratio

    each_halo(wait_recv, near, 1, s_fields, r_fields, True, receive=True)

    def moved(ref, z, at, rows):
        return lambda i, j: ref[z + i, pl.ds(at + j, rows), :]

    cond = fields.at[1]

    def weigh(z, _):
        weighted[0, z, EXT, :] = cond[z, EXT, :] * (fields[0, z, EXT, :])
        return 0

    lax.fori_loop(HALO - 1, HALO + PLANES + 1, weigh, 0)

    def first_plane(z, _):
        s = stencil(moved(cond, z, OWN, ROWS), z_twice, first, last)
        flux = s * fields[0, z, own_y, :] - stencil(moved(weighted.at[0], z, OWN, ROWS), z_twice, first, last)
        resid[z, own_y, :] = own_term[z - HALO] - cond[z, own_y, :] * flux
        return 0

    lax.fori_loop(HALO, HALO + PLANES, first_plane, 0)
    each_halo(start, resid, HALO, s_resid, r_resid, False)

    each_halo(wait_recv, fields.at[2], 1, s_pot, r_pot, False, receive=True)
    ex_total = 2.0 * ex_sum

    def extra_plane(z, _):
        ke = stencil(moved(fields.at[2], z, OWN, ROWS), z_extra, first, last)
        own_term[z - HALO] = ke - ex_total * fields[2, z, own_y, :]
        return 0

    lax.fori_loop(HALO, HALO + PLANES, extra_plane, 0)
    each_deep(wait_recv, receive=True)

    def diag_plane(z, _):
        diag[z, EXT, :] = 1.0 + cond[z, EXT, :] * stencil(moved(cond, z, 8, EXT_Y), z_twice, first, last)
        return 0

    lax.fori_loop(1, EXT_Z - 1, diag_plane, 0)
    each_halo(wait_send, near, 1, s_fields, r_fields, True)
    pl.semaphore_wait(far, 10)
    scatter_rows(stage_cond, row_cond, 0)
    each_halo(wait_recv, resid, HALO, s_resid, r_resid, False, receive=True)

    inv_centre = 1.0 / centre

    def first_update(z, _):
        u = resid[z, EXT, :] * inv_centre
        upd[z, EXT, :] = u
        estimate[z, EXT, :] = u
        weighted[0, z, EXT, :] = cond[z, EXT, :] * u
        return 0

    lax.fori_loop(0, EXT_Z, first_update, 0)

    def sweep(n, weight):
        old = weighted.at[lax.rem(n + 1, 2)]
        new = lax.rem(n, 2)
        weight_next = 1.0 / (2.0 * ratio - weight)
        keep = weight_next * weight
        gain_r = 2.0 * weight_next / half

        def one(z):
            u = upd[z, EXT, :]
            c = cond[z, EXT, :]
            r = resid[z, EXT, :] - diag[z, EXT, :] * u + c * stencil(moved(old, z, 8, EXT_Y), z_twice, first, last)
            fresh = keep * u + gain_r * r
            return r, fresh, estimate[z, EXT, :] + fresh, c * fresh

        def pair(i, _):
            planes = [n + 2 * i, n + 2 * i + 1]
            for z, (r, fresh, total, flux) in zip(planes, [one(z) for z in planes]):
                resid[z, EXT, :] = r
                upd[z, EXT, :] = fresh
                estimate[z, EXT, :] = total
                weighted[new, z, EXT, :] = flux
            return 0

        lax.fori_loop(0, EXT_Z // 2 - n, pair, 0)
        return weight_next

    each_halo(wait_send, resid, HALO, s_resid, r_resid, False)
    weight = lax.fori_loop(1, CHEB - 2, sweep, weight)
    wait_rows(stage_cond, row_cond, 0)
    edges_start(row_cond, cond_prev, cond_next, BASIS)
    lax.fori_loop(CHEB - 2, CHEB, sweep, weight)

    def total_plane(z, _):
        total = fields[0, z, EXT, :] + estimate[z, EXT, :]
        fields[0, z, EXT, :] = total
        weighted[0, z, EXT, :] = cond[z, EXT, :] * total
        return 0

    lax.fori_loop(HALO - 1, HALO + PLANES + 1, total_plane, 0)

    def elliptic_plane(z, _):
        twice = (diag[z, own_y, :] - 1.0) * fields[0, z, own_y, :]
        twice = twice - cond[z, own_y, :] * stencil(moved(weighted.at[0], z, OWN, ROWS), z_twice, first, last)
        own_term[z - HALO] = own_term[z - HALO] - twice / time_step
        return 0

    lax.fori_loop(HALO, HALO + PLANES, elliptic_plane, 0)
    stage_res[...] = jnp.swapaxes(own_term[...], 0, 1)
    scatter_rows(stage_res, row_res, 1)

    new_volt[...] = volt[...] + estimate[pl.ds(HALO, PLANES), own_y, :]
    wait_rows(stage_res, row_res, 1)

    def apply_matrix(src, k, shift=None):
        coarse = src.astype(jnp.bfloat16)
        fine = (src - coarse.astype(jnp.float32)).astype(jnp.bfloat16)

        def dot(a, b):
            return jnp.dot(a, b, preferred_element_type=jnp.float32)

        out = dot(matrix[0], fine) + dot(matrix[1], coarse) + dot(matrix[0], coarse)
        if shift is not None:
            out = out - shift * lines[k - 1, LINES]
        lines[k, LINES] = out

    sums = jnp.zeros((1, COLS), jnp.float32)

    def product(sums, e, a, b):
        total = jnp.sum((a * b).reshape(4, TILES // 4, 8, COLS), axis=0)
        total = jnp.sum(jnp.sum(total, axis=0), axis=0, keepdims=True)
        return sums + jnp.where(lane == e, jnp.sum(total, axis=1, keepdims=True), 0.0)

    CHUNK = 64

    def near_rows(refs, at):
        return lambda i, j: refs[i + 1][pl.ds(at + j, CHUNK), :]

    weigh_refs = [line_weighted.at[n] for n in range(3)]
    cond_refs = [cond_prev, row_cond, cond_next]

    def operate_here(k):
        basis = [None, lines.at[k], None]
        for at in range(8, 8 + WHOLE_Z, CHUNK):
            rows = pl.ds(at, CHUNK)
            ki = row_diag[rows] * lines[k, rows]
            ki = ki - row_cond[rows] * stencil_here(near_rows(weigh_refs, at), line_in, first, last)
            image[k, pl.ds(at - 8, CHUNK)] = ki - stencil_here(near_rows(basis, at), line_ex, first, last)

    def operate_beside(k):
        basis = [line_prev.at[k], None, line_next.at[k]]
        for n in (0, 2):
            weigh_refs[n][...] = cond_refs[n][...] * basis[n][...]
        for at in range(8, 8 + WHOLE_Z, CHUNK):
            rows = pl.ds(at, CHUNK)
            ki = row_cond[rows] * stencil_beside(near_rows(weigh_refs, at), line_in, first, last)
            ki = ki + stencil_beside(near_rows(basis, at), line_ex, first, last)
            image[k, pl.ds(at - 8, CHUNK)] = image[k, pl.ds(at - 8, CHUNK)] - ki

    def line_diag():
        for at in range(8, 8 + WHOLE_Z, CHUNK):
            rows = pl.ds(at, CHUNK)
            row_diag[rows] = ex_total + row_cond[rows] * stencil(near_rows(cond_refs, at), line_in, first, last)

    apply_matrix(row_res[inner], 0)
    edges_start(lines.at[0], line_prev.at[0], line_next.at[0], 0)
    weigh_refs[1][...] = row_cond[...] * lines[0]
    edges_wait(row_cond, cond_prev, cond_next, BASIS)
    line_diag()
    operate_here(0)
    sums = product(sums, 0, lines[0, inner], row_res[inner])

    at = BASIS
    for k in range(BASIS):
        edges_wait(lines.at[k], line_prev.at[k], line_next.at[k], k)
        operate_beside(k)
        if k < BASIS - 1:
            apply_matrix(image[k], k + 1, shift)
            edges_start(lines.at[k + 1], line_prev.at[k + 1], line_next.at[k + 1], k + 1)
            send_back(k)
            weigh_refs[1][...] = row_cond[...] * lines[k + 1]
            operate_here(k + 1)
            sums = product(sums, k + 1, lines[k + 1, inner], row_res[inner])
            for m in range(k + 1):
                sums = product(sums, at, lines[m, inner], image[k])
                at += 1
            if k == BASIS - 2:
                for m in range(k + 1):
                    sums = product(sums, at, lines[k + 1, inner], image[m])
                    at += 1
        else:
            sums = product(sums, at, lines[k, inner], image[k])

    def sum_over(sums, buf, n, me, peers, meanwhile=None):
        part[...] = sums
        buf[me] = sums
        for to in peers:
            pltpu.make_async_remote_copy(
                src_ref=part, dst_ref=buf.at[me], send_sem=s_sum.at[n], recv_sem=r_sum.at[n],
                device_id=to, device_id_type=MESH).start()
        if meanwhile is not None:
            meanwhile()
        got = buf.at[pl.ds(0, 15)]
        pltpu.make_async_copy(got, got, r_sum.at[n]).wait()
        pltpu.make_async_copy(got, got, s_sum.at[n]).wait()
        return jnp.sum(buf[...], axis=0)

    def hops(d, n):
        return min(d, n - d)

    chip_x, core = spot // 2, spot % 2
    steps = sorted(((x, y) for x in range(4) for y in range(4) if (x, y) != (0, 0)),
                   key=lambda p: (-hops(p[0], 4) - hops(p[1], 4), p))
    sums = sum_over(sums, gather_a, 0, chip_x * 4 + chip_y, [
        ((gx // 8) * 8 + lax.rem(chip_x + x, 4) * 2 + core, lax.rem(chip_y + y, 4) * 2 + gy % 2)
        for x, y in steps], lambda: send_back(BASIS - 1))
    steps = sorted(((z, c) for z in range(8) for c in range(2) if (z, c) != (0, 0)),
                   key=lambda p: (-hops(p[0], 8) - 0.5 * p[1], p))
    peers = []
    for z, c in steps:
        to_z = lax.rem(chip_z + z, 8)
        peers.append(((to_z // 2) * 8 + chip_x * 2 + (core + c) % 2, chip_y * 2 + to_z % 2))
    sums = sum_over(sums, gather_b, 1, chip_z * 2 + core, peers)

    value = [jnp.sum(jnp.where(lane == e, sums, 0.0), axis=1, keepdims=True) for e in range(14)]
    rhs = value[:BASIS]
    gram = {}
    at = BASIS
    for k in range(BASIS):
        for m in range(k + 1):
            gram[m, k] = value[at]
            at += 1

    low, pivot = {}, {}
    for j in range(BASIS):
        d = gram[j, j]
        for m in range(j):
            d = d - low[j, m] * low[j, m] * pivot[m]
        pivot[j] = d
        for i in range(j + 1, BASIS):
            e = gram[j, i]
            for m in range(j):
                e = e - low[i, m] * low[j, m] * pivot[m]
            low[i, j] = e / d
    sol = list(rhs)
    for i in range(BASIS):
        for m in range(i):
            sol[i] = sol[i] - low[i, m] * sol[m]
    sol = [a / pivot[i] for i, a in enumerate(sol)]
    for i in reversed(range(BASIS)):
        for m in range(i + 1, BASIS):
            sol[i] = sol[i] - low[m, i] * sol[m]

    for k in range(BASIS):
        wait_back(k)
    total = sol[0] * back[0]
    for k in range(1, BASIS):
        total = total + sol[k] * back[k]
    new_pot[...] = pot[...] + jnp.swapaxes(total, 0, 1)

    each_deep(wait_send)
    each_halo(wait_send, fields.at[2], 1, s_pot, r_pot, False)
    wait_rows_sent(stage_cond, 0)
    wait_rows_sent(stage_res, 1)
    edges_sent(row_cond, cond_prev, cond_next, BASIS)
    for k in range(BASIS):
        edges_sent(lines.at[k], line_prev.at[k], line_next.at[k], k)


def body(voltage, potential, tissue, gain, couplings, line_factor):
    f32 = jnp.float32
    block = jax.ShapeDtypeStruct((PLANES, ROWS, COLS), f32)
    vmem = pl.BlockSpec(memory_space=pltpu.VMEM)
    line = (LINE, COLS)
    dma = pltpu.SemaphoreType.DMA
    return pl.pallas_call(
        kernel,
        name="bidomain",
        out_shape=(block, block),
        in_specs=[pl.BlockSpec(memory_space=pltpu.SMEM)] + [pl.BlockSpec(memory_space=pl.ANY)] * 5,
        out_specs=(vmem, vmem),
        scratch_shapes=[
            pltpu.VMEM((PLANES, ROWS, COLS), f32),
            pltpu.VMEM((PLANES, ROWS, COLS), f32),
            pltpu.VMEM((PLANES, ROWS, COLS), jnp.int32),
            pltpu.VMEM((PLANES, ROWS, COLS), f32),
            pltpu.VMEM((WHOLE_Z, WHOLE_Z), f32),
            pltpu.VMEM((3, EXT_Z, PAD_Y, COLS), f32),
            pltpu.VMEM((EXT_Z, PAD_Y, COLS), f32),
            pltpu.VMEM((EXT_Z, PAD_Y, COLS), f32),
            pltpu.VMEM((EXT_Z, PAD_Y, COLS), f32),
            pltpu.VMEM((EXT_Z, PAD_Y, COLS), f32),
            pltpu.VMEM((2, EXT_Z, PAD_Y, COLS), f32),
            pltpu.VMEM((PLANES, ROWS, COLS), f32),
            pltpu.VMEM((2, WHOLE_Z, WHOLE_Z), jnp.bfloat16),
            pltpu.VMEM((ROWS, PLANES, COLS), f32),
            pltpu.VMEM((ROWS, PLANES, COLS), f32),
            pltpu.VMEM(line, f32),
            pltpu.VMEM(line, f32),
            pltpu.VMEM((BASIS, *line), f32),
            pltpu.VMEM((BASIS, *line), f32),
            pltpu.VMEM((BASIS, *line), f32),
            pltpu.VMEM(line, f32),
            pltpu.VMEM(line, f32),
            pltpu.VMEM((3, *line), f32),
            pltpu.VMEM((BASIS, WHOLE_Z, COLS), f32),
            pltpu.VMEM(line, f32),
            pltpu.VMEM((BASIS, ROWS, PLANES, COLS), f32),
            pltpu.VMEM((1, COLS), f32),
            pltpu.VMEM((16, 1, COLS), f32),
            pltpu.VMEM((16, 1, COLS), f32),
            dma((8,)), dma((8,)), dma((8,)), dma((8,)), dma((8,)), dma((8,)), dma((8,)), dma((8,)),
            dma((2,)), dma((2,)), dma((BASIS + 1, 2)), dma((BASIS + 1, 2)),
            dma((BASIS,)), dma((BASIS,)), dma((2,)), dma((2,)), dma((5,)), pltpu.SemaphoreType.REGULAR,
        ],
        compiler_params=pltpu.CompilerParams(
            collective_id=0, has_side_effects=True, vmem_limit_bytes=67043328),
    )(couplings, voltage, potential, tissue, gain, line_factor)


def solution(mesh):
    block = P("gx", "gy", None)
    return jax.shard_map(
        body, mesh=mesh, in_specs=(block, block, block, block, P(), P()),
        out_specs=(block, block), check_vma=False)
```

```python
import jax
import jax.numpy as jnp
from jax import lax
from jax.experimental import pallas as pl
from jax.experimental.pallas import tpu as pltpu
from jax.sharding import PartitionSpec as P

CHEB = 8
SHIFT = 1.3
BASIS = 4
MESH = pl.DeviceIdType.MESH
HIGHEST = lax.Precision.HIGHEST
time_step = 2.0
ionic_rate = 0.5
onset_level = 0.2
gain_top = 3.0625

PLANES, ROWS, COLS = 8, 32, 128
HALO = 8
EXT_Z, EXT_Y = PLANES + 2 * HALO, ROWS + 2 * HALO
PAD_Y = EXT_Y + 16
OWN = 8 + HALO
EXT = pl.ds(8, EXT_Y)
GX, GY = 32, 8
WHOLE_Z = GX * PLANES
WHOLE_Y = GY * ROWS
TILES = WHOLE_Z // 8
LINE = WHOLE_Z + 16
LINES = pl.ds(8, WHOLE_Z)
DIRECTIONS = tuple((a, b) for a in (-1, 0, 1) for b in (-1, 0, 1) if (a, b) != (0, 0))


def z_range(a, depth):
    if a == 0:
        return pl.ds(HALO, PLANES), pl.ds(HALO, PLANES)
    if a > 0:
        return pl.ds(HALO + PLANES - depth, depth), pl.ds(HALO - depth, depth)
    return pl.ds(HALO, depth), pl.ds(HALO + PLANES, depth)


def y_range(b):
    if b == 0:
        return pl.ds(OWN, ROWS), pl.ds(OWN, ROWS)
    if b > 0:
        return pl.ds(OWN + ROWS - 8, 8), pl.ds(OWN - 8, 8)
    return pl.ds(OWN, 8), pl.ds(OWN + ROWS, 8)


def combine(k, lead, sub, lane, lead_sub, lead_lane, sub_lane, scale=1.0):
    half = 0.5 * scale
    return dict(
        lead=scale * k[lead], sub=scale * k[sub], lane=scale * k[lane],
        both=scale * k[lead_sub], cross=scale * k[lead_sub + 1],
        lead_sum=half * (k[lead_lane] + k[lead_lane + 1]), lead_diff=half * (k[lead_lane] - k[lead_lane + 1]),
        sub_sum=half * (k[sub_lane] + k[sub_lane + 1]), sub_diff=half * (k[sub_lane] - k[sub_lane + 1]))


def shift_lanes(even, odd, first, last):
    right = jnp.where(last, 0.0, pltpu.roll(even + odd, COLS - 1, 1))
    return right + jnp.where(first, 0.0, pltpu.roll(even - odd, 1, 1))


def stencil_here(read, k, first, last):
    up, down = read(0, 1), read(0, -1)
    rows = up + down
    even = k["lane"] * read(0, 0) + k["sub_sum"] * rows
    return k["sub"] * rows + shift_lanes(even, k["sub_diff"] * (up - down), first, last)


def stencil_beside(read, k, first, last):
    plus, minus = read(1, 0), read(-1, 0)
    total = plus + minus
    out = k["lead"] * total
    out = out + k["both"] * (read(1, 1) + read(-1, -1)) + k["cross"] * (read(1, -1) + read(-1, 1))
    return out + shift_lanes(k["lead_sum"] * total, k["lead_diff"] * (plus - minus), first, last)


def stencil_before(read, k, first, last):
    minus = read(-1, 0)
    out = k["lead"] * minus + k["both"] * read(-1, -1) + k["cross"] * read(-1, 1)
    return out + shift_lanes(k["lead_sum"] * minus, -(k["lead_diff"] * minus), first, last)


def stencil(read, k, first, last):
    here, plus, minus = read(0, 0), read(1, 0), read(-1, 0)
    up, down = read(0, 1), read(0, -1)
    total, diff = plus + minus, plus - minus
    rows, row_diff = up + down, up - down
    even = k["lane"] * here + k["lead_sum"] * total + k["sub_sum"] * rows
    odd = k["lead_diff"] * diff + k["sub_diff"] * row_diff
    out = k["lead"] * total + k["sub"] * rows
    out = out + k["both"] * (read(1, 1) + read(-1, -1)) + k["cross"] * (read(1, -1) + read(-1, 1))
    return out + shift_lanes(even, odd, first, last)


def owner(row):
    chip_y = row // 64
    along = row % 64
    along = along + (chip_y % 2) * (63 - 2 * along)
    chip_z = along // 8
    spot = along % 8
    spot = spot + (chip_z % 2) * (7 - 2 * spot)
    return (chip_z // 2) * 8 + spot, chip_y * 2 + chip_z % 2


def own_row(gx, gy):
    chip_y = gy // 2
    chip_z = (gx // 8) * 2 + gy % 2
    spot = gx % 8
    spot = spot + (chip_z % 2) * (7 - 2 * spot)
    along = chip_z * 8 + spot
    return chip_y * 64 + along + (chip_y % 2) * (63 - 2 * along)


def kernel(
    coup, volt_in, pot_in, tissue_in, gain_in, factor_in, new_volt, new_pot,
    volt, pot, tissue, gain, factor,
    fields, resid, upd, diag, estimate, weighted, own_term, matrix,
    stage_cond, stage_res,
    row_cond, row_res, lines, line_prev, line_next, cond_prev, cond_next,
    line_weighted, image, row_diag, back, part, gather_a, gather_b,
    s_fields, r_fields, s_cond, r_cond, s_pot, r_pot, s_resid, r_resid,
    s_rows, r_rows, s_edge, r_edge, s_back, r_back, s_sum, r_sum, s_take, far,
):
    gx = lax.axis_index("gx")
    gy = lax.axis_index("gy")
    row = own_row(gx, gy)
    own_gy = row // ROWS
    own_t = row % ROWS
    chip_z = (gx // 8) * 2 + gy % 2
    chip_y = gy // 2
    spot = gx % 8

    def at_z(z):
        return (z // 2) * 8 + spot, chip_y * 2 + z % 2

    def at_y(y):
        return gx, y * 2 + gy % 2

    takes = [
        pltpu.make_async_copy(src, dst, s_take.at[n])
        for n, (src, dst) in enumerate(
            ((tissue_in, tissue), (gain_in, gain), (volt_in, volt), (pot_in, pot), (factor_in, factor)))
    ]
    for copy in takes:
        copy.start()
    barrier = pltpu.get_barrier_semaphore()

    def greet(sem, to):
        pl.semaphore_signal(sem, inc=1, device_id=to, device_id_type=MESH)

    for a, b in DIRECTIONS:
        greet(barrier, (lax.rem(gx + a + GX, GX), lax.rem(gy + b + GY, GY)))
    for d in range(1, 8):
        greet(barrier, at_z(lax.rem(chip_z + d, 8)))
        greet(barrier, ((gx // 8) * 8 + lax.rem(spot + d, 8), gy))
    for d in range(1, 4):
        greet(barrier, at_y(lax.rem(chip_y + d, 4)))
    for copy in takes:
        copy.wait()

    lane = lax.broadcasted_iota(jnp.int32, (1, COLS), 1)
    first, last = lane == 0, lane == COLS - 1
    k_in = [coup[0, n] for n in range(9)]
    k_ex = [coup[1, n] for n in range(9)]
    z_twice = combine(k_in, 0, 1, 2, 3, 5, 7, time_step)
    z_extra = combine(k_ex, 0, 1, 2, 3, 5, 7)
    line_in = combine(k_in, 1, 0, 2, 3, 7, 5)
    line_ex = combine(k_ex, 1, 0, 2, 3, 7, 5)

    def neighbour(a, b):
        ok = (gx + a >= 0) & (gx + a < GX) & (gy + b >= 0) & (gy + b < GY)
        return ok, (gx + a, gy + b)

    def send_halo(ref, d, depth, sems_s, sems_r, stacked):
        a, b = DIRECTIONS[d]
        zs, zd = z_range(a, depth)
        ys, yd = y_range(b)
        src = ref.at[:, zs, ys, :] if stacked else ref.at[zs, ys, :]
        dst = ref.at[:, zd, yd, :] if stacked else ref.at[zd, yd, :]
        return pltpu.make_async_remote_copy(
            src_ref=src, dst_ref=dst, send_sem=sems_s.at[d], recv_sem=sems_r.at[d],
            device_id=(gx + a, gy + b), device_id_type=MESH)

    def each_halo(act, ref, depth, sems_s, sems_r, stacked, receive=False):
        for d, (a, b) in enumerate(DIRECTIONS):
            ok, _ = neighbour(-a, -b) if receive else neighbour(a, b)

            @pl.when(ok)
            def _():
                act(send_halo(ref, d, depth, sems_s, sems_r, stacked))

    def deep_conduct(d):
        a, b = DIRECTIONS[d]
        ys, yd = y_range(b)
        if a > 0:
            zs, zd = pl.ds(HALO, PLANES - 1), pl.ds(0, HALO - 1)
        else:
            zs, zd = pl.ds(HALO + 1, PLANES - 1), pl.ds(HALO + PLANES + 1, HALO - 1)
        return pltpu.make_async_remote_copy(
            src_ref=fields.at[1, zs, ys, :], dst_ref=fields.at[1, zd, yd, :],
            send_sem=s_cond.at[d], recv_sem=r_cond.at[d],
            device_id=(gx + a, gy + b), device_id_type=MESH)

    def each_deep(act, receive=False):
        for d, (a, b) in enumerate(DIRECTIONS):
            if a == 0:
                continue
            ok, _ = neighbour(-a, -b) if receive else neighbour(a, b)

            @pl.when(ok)
            def _():
                act(deep_conduct(d))

    def start(copy):
        copy.start()

    def wait_recv(copy):
        copy.wait_recv()

    def wait_send(copy):
        copy.wait_send()

    own_group = own_gy == gy

    def row_tile(i):
        return pl.ds(pl.multiple_of(8 + 8 * i, 8), 8)

    turned = chip_y % 2
    upper = gy % 2 + turned * (1 - 2 * (gy % 2))

    def scatter_rows(stage, rows_ref, n):
        def one(d, _):
            m = lax.rem(gx + d, 32)
            z, q = m // 8, lax.rem(m, 8)
            z_odd = lax.rem(z, 2)
            to_gx = upper * 16 + (z // 2) * 8 + q + z_odd * (7 - 2 * q)
            to_gy = chip_y * 2 + z_odd
            t = m + turned * (31 - 2 * m)

            @pl.when((to_gx != gx) | (to_gy != gy))
            def _():
                pltpu.make_async_remote_copy(
                    src_ref=stage.at[t], dst_ref=rows_ref.at[row_tile(gx)],
                    send_sem=s_rows.at[n], recv_sem=r_rows.at[n],
                    device_id=(to_gx, to_gy), device_id_type=MESH).start()
            return 0

        lax.fori_loop(0, ROWS, one, 0, unroll=4)

        @pl.when(own_group)
        def _():
            rows_ref[row_tile(gx)] = stage[own_t]

    def wait_rows(stage, rows_ref, n):
        @pl.when(own_group)
        def _():
            part_ref = rows_ref.at[pl.ds(8, WHOLE_Z - 8)]
            pltpu.make_async_copy(part_ref, part_ref, r_rows.at[n]).wait()

        @pl.when(jnp.logical_not(own_group))
        def _():
            part_ref = rows_ref.at[LINES]
            pltpu.make_async_copy(part_ref, part_ref, r_rows.at[n]).wait()

    def wait_rows_sent(stage, n):
        @pl.when(own_group)
        def _():
            part_ref = stage.at[pl.ds(0, ROWS - 1)]
            pltpu.make_async_copy(part_ref, part_ref, s_rows.at[n]).wait()

        @pl.when(jnp.logical_not(own_group))
        def _():
            pltpu.make_async_copy(stage, stage, s_rows.at[n]).wait()

    def send_back(k):
        def one(d, _):
            i = lax.rem(gx + d, GX)

            @pl.when((i != gx) | (own_gy != gy))
            def _():
                pltpu.make_async_remote_copy(
                    src_ref=lines.at[k, row_tile(i)], dst_ref=back.at[k, own_t],
                    send_sem=s_back.at[k], recv_sem=r_back.at[k],
                    device_id=(i, own_gy), device_id_type=MESH).start()
            return 0

        lax.fori_loop(0, GX, one, 0, unroll=4)

        @pl.when(own_group)
        def _():
            back[k, own_t] = lines[k, row_tile(gx)]

    def wait_back(k):
        @pl.when(own_group)
        def _():
            got = back.at[k, pl.ds(0, ROWS - 1)]
            pltpu.make_async_copy(got, got, r_back.at[k]).wait()
            pltpu.make_async_copy(got, got, s_back.at[k]).wait()

        @pl.when(jnp.logical_not(own_group))
        def _():
            pltpu.make_async_copy(back.at[k], back.at[k], r_back.at[k]).wait()
            pltpu.make_async_copy(back.at[k], back.at[k], s_back.at[k]).wait()

    inner = LINES

    HALF = WHOLE_Z // 2

    def edge(src, dst, n, side, part):
        to_gx, to_gy = owner(row + (1 if side == 0 else -1))
        rows = pl.ds(8 + part * HALF, HALF)
        return pltpu.make_async_remote_copy(
            src_ref=src.at[rows], dst_ref=dst.at[rows],
            send_sem=s_edge.at[n, side, part], recv_sem=r_edge.at[n, side, part],
            device_id=(to_gx, to_gy), device_id_type=MESH)

    has_next, has_prev = row < WHOLE_Y - 1, row > 0

    def edges_start(src, prev, nxt, n, part):
        @pl.when(has_next)
        def _():
            edge(src, prev, n, 0, part).start()

        if n != BASIS - 1:
            @pl.when(has_prev)
            def _():
                edge(src, nxt, n, 1, part).start()

    def edges_wait(src, prev, nxt, n, part):
        @pl.when(has_prev)
        def _():
            edge(src, prev, n, 0, part).wait_recv()

        if n != BASIS - 1:
            @pl.when(has_next)
            def _():
                edge(src, nxt, n, 1, part).wait_recv()

    def edges_sent(src, prev, nxt, n, part):
        @pl.when(has_next)
        def _():
            edge(src, prev, n, 0, part).wait_send()

        if n != BASIS - 1:
            @pl.when(has_prev)
            def _():
                edge(src, nxt, n, 1, part).wait_send()

    own_y = pl.ds(OWN, ROWS)
    conduct = tissue[...].astype(jnp.float32) * gain[...]
    own = (pl.ds(HALO, PLANES), own_y, slice(None))
    fields[0, *own] = volt[...] + pot[...]
    fields[1, *own] = conduct
    fields[2, *own] = pot[...]
    pl.semaphore_wait(barrier, 25)
    near = fields.at[pl.ds(0, 2)]
    each_halo(start, near, 1, s_fields, r_fields, True)
    each_halo(start, fields.at[2], 1, s_pot, r_pot, False)
    each_deep(start)
    for d in range(1, 8):
        greet(far, at_z(lax.rem(chip_z + d, 8)))
    for d in range(1, 4):
        greet(far, at_y(lax.rem(chip_y + d, 4)))
    v = volt[...]
    ionic = tissue[...].astype(jnp.float32) * v * (v - onset_level) * (v - 1.0)
    own_term[...] = -ionic_rate * ionic

    for d, (a, b) in enumerate(DIRECTIONS):
        ok, _ = neighbour(-a, -b)

        @pl.when(jnp.logical_not(ok))
        def _():
            zd = z_range(a, HALO)[1]
            yd = y_range(b)[1]
            shape = (zd.size, yd.size, COLS)
            for n in range(3):
                fields[n, zd, yd, :] = jnp.zeros(shape, jnp.float32)
            resid[zd, yd, :] = jnp.zeros(shape, jnp.float32)
    stage_cond[...] = jnp.swapaxes(conduct, 0, 1)
    tile = jnp.zeros((8, COLS), jnp.float32)
    beyond = (pl.ds(0, 8), pl.ds(PAD_Y - 8, 8))

    def blank_rows(z, _):
        for rows in beyond:
            fields[1, z, rows, :] = tile
            weighted[0, z, rows, :] = tile
            weighted[1, z, rows, :] = tile
        return 0

    lax.fori_loop(0, EXT_Z, blank_rows, 0)
    ends = (pl.ds(0, 8), pl.ds(LINE - 8, 8))
    for rows in ends:
        for ref in (row_cond, row_res, cond_prev, cond_next):
            ref[rows] = tile
        for k in range(BASIS):
            for ref in (lines, line_prev, line_next):
                ref[k, rows] = tile
    blank = jnp.zeros((WHOLE_Z, COLS), jnp.float32)

    @pl.when(jnp.logical_not(has_prev))
    def _():
        cond_prev[LINES] = blank
        for k in range(BASIS):
            line_prev[k, LINES] = blank

    @pl.when(jnp.logical_not(has_next))
    def _():
        cond_next[LINES] = blank
        for k in range(BASIS):
            line_next[k, LINES] = blank

    whole = lax.dot_general(
        factor[...], factor[...], (((0,), (0,)), ((), ())), precision=HIGHEST,
        preferred_element_type=jnp.float32)
    in_sum = k_in[0]
    ex_sum = k_ex[0]
    for n in range(1, 9):
        in_sum = in_sum + k_in[n]
        ex_sum = ex_sum + k_ex[n]
    reach = jnp.max(jnp.sum(jnp.abs(whole), axis=1, keepdims=True), axis=0, keepdims=True)
    bound = reach * (4.0 * gain_top * in_sum + 4.0 * ex_sum)
    scaled = whole * (1.0 / bound)
    coarse = scaled.astype(jnp.bfloat16)
    matrix[0] = coarse
    matrix[1] = (scaled - coarse.astype(jnp.float32)).astype(jnp.bfloat16)
    eye = lax.broadcasted_iota(jnp.int32, whole.shape, 0) == lax.broadcasted_iota(jnp.int32, whole.shape, 1)
    mean = jnp.sum(jnp.sum(jnp.where(eye, whole, 0.0), axis=1, keepdims=True), axis=0, keepdims=True) / WHOLE_Z
    shift = SHIFT * mean * (2.0 * in_sum + 2.0 * ex_sum) / bound

    top = 1.0 + time_step * 4.0 * gain_top * in_sum
    ones = jnp.ones((1, COLS), jnp.float32)
    top = ones * top
    centre = (top + 1.0) / 2.0
    half = (top - 1.0) / 2.0
    ratio = centre / half
    weight = 1.0 / ratio

    each_halo(wait_recv, near, 1, s_fields, r_fields, True, receive=True)

    def moved(ref, z, at, rows):
        return lambda i, j: ref[z + i, pl.ds(at + j, rows), :]

    cond = fields.at[1]

    def weigh(z, _):
        weighted[0, z, EXT, :] = cond[z, EXT, :] * (fields[0, z, EXT, :])
        return 0

    lax.fori_loop(HALO - 1, HALO + PLANES + 1, weigh, 0)

    def first_plane(z, _):
        s = stencil(moved(cond, z, OWN, ROWS), z_twice, first, last)
        flux = s * fields[0, z, own_y, :] - stencil(moved(weighted.at[0], z, OWN, ROWS), z_twice, first, last)
        resid[z, own_y, :] = own_term[z - HALO] - cond[z, own_y, :] * flux
        return 0

    lax.fori_loop(HALO, HALO + PLANES, first_plane, 0)
    each_halo(start, resid, HALO, s_resid, r_resid, False)

    each_halo(wait_recv, fields.at[2], 1, s_pot, r_pot, False, receive=True)
    ex_total = 2.0 * ex_sum

    def extra_plane(z, _):
        ke = stencil(moved(fields.at[2], z, OWN, ROWS), z_extra, first, last)
        own_term[z - HALO] = ke - ex_total * fields[2, z, own_y, :]
        return 0

    lax.fori_loop(HALO, HALO + PLANES, extra_plane, 0)
    each_deep(wait_recv, receive=True)

    def diag_plane(z, _):
        diag[z, EXT, :] = 1.0 + cond[z, EXT, :] * stencil(moved(cond, z, 8, EXT_Y), z_twice, first, last)
        return 0

    lax.fori_loop(1, EXT_Z - 1, diag_plane, 0)
    each_halo(wait_send, near, 1, s_fields, r_fields, True)
    pl.semaphore_wait(far, 10)
    scatter_rows(stage_cond, row_cond, 0)
    each_halo(wait_recv, resid, HALO, s_resid, r_resid, False, receive=True)

    inv_centre = 1.0 / centre

    def first_update(z, _):
        u = resid[z, EXT, :] * inv_centre
        upd[z, EXT, :] = u
        estimate[z, EXT, :] = u
        weighted[0, z, EXT, :] = cond[z, EXT, :] * u
        return 0

    lax.fori_loop(0, EXT_Z, first_update, 0)

    def sweep(n, weight, margin):
        old = weighted.at[lax.rem(n + 1, 2)]
        new = lax.rem(n, 2)
        weight_next = 1.0 / (2.0 * ratio - weight)
        keep = weight_next * weight
        gain_r = 2.0 * weight_next / half
        at, count = OWN - margin, ROWS + 2 * margin
        rows = pl.ds(at, count)

        def one(z):
            u = upd[z, rows, :]
            c = cond[z, rows, :]
            r = resid[z, rows, :] - diag[z, rows, :] * u + c * stencil(moved(old, z, at, count), z_twice, first, last)
            fresh = keep * u + gain_r * r
            return r, fresh, estimate[z, rows, :] + fresh, c * fresh

        def pair(i, _):
            planes = [n + 2 * i, n + 2 * i + 1]
            for z, (r, fresh, total, flux) in zip(planes, [one(z) for z in planes]):
                resid[z, rows, :] = r
                upd[z, rows, :] = fresh
                estimate[z, rows, :] = total
                weighted[new, z, rows, :] = flux
            return 0

        lax.fori_loop(0, EXT_Z // 2 - n, pair, 0)
        return weight_next

    each_halo(wait_send, resid, HALO, s_resid, r_resid, False)
    weight = lax.fori_loop(1, 4, lambda n, w: sweep(n, w, 8), weight)
    weight = lax.fori_loop(4, CHEB - 2, lambda n, w: sweep(n, w, 4), weight)
    wait_rows(stage_cond, row_cond, 0)
    for half_line in range(2):
        edges_start(row_cond, cond_prev, cond_next, BASIS, half_line)
    lax.fori_loop(CHEB - 2, CHEB, lambda n, w: sweep(n, w, 4), weight)

    def total_plane(z, _):
        total = fields[0, z, EXT, :] + estimate[z, EXT, :]
        fields[0, z, EXT, :] = total
        weighted[0, z, EXT, :] = cond[z, EXT, :] * total
        return 0

    lax.fori_loop(HALO - 1, HALO + PLANES + 1, total_plane, 0)

    def elliptic_plane(z, _):
        twice = (diag[z, own_y, :] - 1.0) * fields[0, z, own_y, :]
        twice = twice - cond[z, own_y, :] * stencil(moved(weighted.at[0], z, OWN, ROWS), z_twice, first, last)
        own_term[z - HALO] = own_term[z - HALO] - twice / time_step
        return 0

    lax.fori_loop(HALO, HALO + PLANES, elliptic_plane, 0)
    stage_res[...] = jnp.swapaxes(own_term[...], 0, 1)
    scatter_rows(stage_res, row_res, 1)

    gain[...] = volt[...] + estimate[pl.ds(HALO, PLANES), own_y, :]
    early = pltpu.make_async_copy(gain, new_volt, s_take.at[0])
    early.start()
    wait_rows(stage_res, row_res, 1)

    def apply_matrix(src, k, shift=None):
        coarse = src.astype(jnp.bfloat16)
        fine = (src - coarse.astype(jnp.float32)).astype(jnp.bfloat16)

        def dot(a, b):
            return jnp.dot(a, b, preferred_element_type=jnp.float32)

        for part in range(2):
            rows = pl.ds(part * HALF, HALF)
            out = dot(matrix[0, rows], fine) + dot(matrix[1, rows], coarse) + dot(matrix[0, rows], coarse)
            if shift is not None:
                out = out - shift * lines[k - 1, pl.ds(8 + part * HALF, HALF)]
            lines[k, pl.ds(8 + part * HALF, HALF)] = out
            edges_start(lines.at[k], line_prev.at[k], line_next.at[k], k, part)

    sums = jnp.zeros((1, COLS), jnp.float32)

    def product(sums, e, a, b):
        total = jnp.sum((a * b).reshape(4, TILES // 4, 8, COLS), axis=0)
        total = jnp.sum(jnp.sum(total, axis=0), axis=0, keepdims=True)
        return sums + jnp.where(lane == e, jnp.sum(total, axis=1, keepdims=True), 0.0)

    CHUNK = 64

    def near_rows(refs, at):
        return lambda i, j: refs[i + 1][pl.ds(at + j, CHUNK), :]

    weigh_refs = [line_weighted.at[n] for n in range(3)]
    cond_refs = [cond_prev, row_cond, cond_next]

    def operate_here(k):
        basis = [None, lines.at[k], None]
        for at in range(8, 8 + WHOLE_Z, CHUNK):
            rows = pl.ds(at, CHUNK)
            ki = row_diag[rows] * lines[k, rows]
            ki = ki - row_cond[rows] * stencil_here(near_rows(weigh_refs, at), line_in, first, last)
            image[k, pl.ds(at - 8, CHUNK)] = ki - stencil_here(near_rows(basis, at), line_ex, first, last)

    def operate_beside(k):
        basis = [line_prev.at[k], None, line_next.at[k]]
        split = 8 + HALF
        for part, lined in enumerate((pl.ds(0, split), pl.ds(split, LINE - split))):
            edges_wait(lines.at[k], line_prev.at[k], line_next.at[k], k, part)
            for n in (0, 2) if k < BASIS - 1 else (0,):
                weigh_refs[n][lined] = cond_refs[n][lined] * basis[n][lined]
            for at in (range(8, split - CHUNK, CHUNK) if part == 0 else range(split - CHUNK, 8 + WHOLE_Z, CHUNK)):
                rows = pl.ds(at, CHUNK)
                beside = stencil_beside if k < BASIS - 1 else stencil_before
                ki = row_cond[rows] * beside(near_rows(weigh_refs, at), line_in, first, last)
                ki = ki + beside(near_rows(basis, at), line_ex, first, last)
                if k == BASIS - 1:
                    ki = 2.0 * ki
                image[k, pl.ds(at - 8, CHUNK)] = image[k, pl.ds(at - 8, CHUNK)] - ki

    def line_diag():
        for at in range(8, 8 + WHOLE_Z, CHUNK):
            rows = pl.ds(at, CHUNK)
            row_diag[rows] = ex_total + row_cond[rows] * stencil(near_rows(cond_refs, at), line_in, first, last)

    apply_matrix(row_res[inner], 0)
    send_back(0)
    weigh_refs[1][...] = row_cond[...] * lines[0]
    for half_line in range(2):
        edges_wait(row_cond, cond_prev, cond_next, BASIS, half_line)
    line_diag()
    operate_here(0)
    sums = product(sums, 0, lines[0, inner], row_res[inner])

    at = BASIS
    for k in range(BASIS):
        operate_beside(k)
        if k < BASIS - 1:
            apply_matrix(image[k], k + 1, shift)
            send_back(k + 1)
            weigh_refs[1][...] = row_cond[...] * lines[k + 1]
            operate_here(k + 1)
            sums = product(sums, k + 1, lines[k + 1, inner], row_res[inner])
            for m in range(k + 1):
                sums = product(sums, at, lines[m, inner], image[k])
                at += 1
            if k == BASIS - 2:
                for m in range(k + 1):
                    sums = product(sums, at, lines[k + 1, inner], image[m])
                    at += 1
        else:
            sums = product(sums, at, lines[k, inner], image[k])

    def sum_over(sums, buf, n, me, peers):
        part[...] = sums
        buf[me] = sums
        for to in peers:
            pltpu.make_async_remote_copy(
                src_ref=part, dst_ref=buf.at[me], send_sem=s_sum.at[n], recv_sem=r_sum.at[n],
                device_id=to, device_id_type=MESH).start()
        got = buf.at[pl.ds(0, 15)]
        pltpu.make_async_copy(got, got, r_sum.at[n]).wait()
        pltpu.make_async_copy(got, got, s_sum.at[n]).wait()
        return jnp.sum(buf[...], axis=0)

    def hops(d, n):
        return min(d, n - d)

    chip_x, core = spot // 2, spot % 2
    steps = sorted(((x, y) for x in range(4) for y in range(4) if (x, y) != (0, 0)),
                   key=lambda p: (-hops(p[0], 4) - hops(p[1], 4), p))
    sums = sum_over(sums, gather_a, 0, chip_x * 4 + chip_y, [
        ((gx // 8) * 8 + lax.rem(chip_x + x, 4) * 2 + core, lax.rem(chip_y + y, 4) * 2 + gy % 2)
        for x, y in steps])
    steps = sorted(((z, c) for z in range(8) for c in range(2) if (z, c) != (0, 0)),
                   key=lambda p: (-hops(p[0], 8) - 0.5 * p[1], p))
    peers = []
    for z, c in steps:
        to_z = lax.rem(chip_z + z, 8)
        peers.append(((to_z // 2) * 8 + chip_x * 2 + (core + c) % 2, chip_y * 2 + to_z % 2))
    sums = sum_over(sums, gather_b, 1, chip_z * 2 + core, peers)

    value = [jnp.sum(jnp.where(lane == e, sums, 0.0), axis=1, keepdims=True) for e in range(14)]
    rhs = value[:BASIS]
    gram = {}
    at = BASIS
    for k in range(BASIS):
        for m in range(k + 1):
            gram[m, k] = value[at]
            at += 1

    low, pivot = {}, {}
    for j in range(BASIS):
        d = gram[j, j]
        for m in range(j):
            d = d - low[j, m] * low[j, m] * pivot[m]
        pivot[j] = d
        for i in range(j + 1, BASIS):
            e = gram[j, i]
            for m in range(j):
                e = e - low[i, m] * low[j, m] * pivot[m]
            low[i, j] = e / d
    sol = list(rhs)
    for i in range(BASIS):
        for m in range(i):
            sol[i] = sol[i] - low[i, m] * sol[m]
    sol = [a / pivot[i] for i, a in enumerate(sol)]
    for i in reversed(range(BASIS)):
        for m in range(i + 1, BASIS):
            sol[i] = sol[i] - low[m, i] * sol[m]

    for k in range(BASIS):
        wait_back(k)
    total = sol[0] * back[0]
    for k in range(1, BASIS):
        total = total + sol[k] * back[k]
    new_pot[...] = pot[...] + jnp.swapaxes(total, 0, 1)

    early.wait()
    each_deep(wait_send)
    each_halo(wait_send, fields.at[2], 1, s_pot, r_pot, False)
    wait_rows_sent(stage_cond, 0)
    wait_rows_sent(stage_res, 1)
    for half_line in range(2):
        edges_sent(row_cond, cond_prev, cond_next, BASIS, half_line)
        for k in range(BASIS):
            edges_sent(lines.at[k], line_prev.at[k], line_next.at[k], k, half_line)


def body(voltage, potential, tissue, gain, couplings, line_factor):
    f32 = jnp.float32
    block = jax.ShapeDtypeStruct((PLANES, ROWS, COLS), f32)
    vmem = pl.BlockSpec(memory_space=pltpu.VMEM)
    line = (LINE, COLS)
    dma = pltpu.SemaphoreType.DMA
    return pl.pallas_call(
        kernel,
        name="bidomain",
        out_shape=(block, block),
        in_specs=[pl.BlockSpec(memory_space=pltpu.SMEM)] + [pl.BlockSpec(memory_space=pl.ANY)] * 5,
        out_specs=(pl.BlockSpec(memory_space=pl.ANY), vmem),
        scratch_shapes=[
            pltpu.VMEM((PLANES, ROWS, COLS), f32),
            pltpu.VMEM((PLANES, ROWS, COLS), f32),
            pltpu.VMEM((PLANES, ROWS, COLS), jnp.int32),
            pltpu.VMEM((PLANES, ROWS, COLS), f32),
            pltpu.VMEM((WHOLE_Z, WHOLE_Z), f32),
            pltpu.VMEM((3, EXT_Z, PAD_Y, COLS), f32),
            pltpu.VMEM((EXT_Z, PAD_Y, COLS), f32),
            pltpu.VMEM((EXT_Z, PAD_Y, COLS), f32),
            pltpu.VMEM((EXT_Z, PAD_Y, COLS), f32),
            pltpu.VMEM((EXT_Z, PAD_Y, COLS), f32),
            pltpu.VMEM((2, EXT_Z, PAD_Y, COLS), f32),
            pltpu.VMEM((PLANES, ROWS, COLS), f32),
            pltpu.VMEM((2, WHOLE_Z, WHOLE_Z), jnp.bfloat16),
            pltpu.VMEM((ROWS, PLANES, COLS), f32),
            pltpu.VMEM((ROWS, PLANES, COLS), f32),
            pltpu.VMEM(line, f32),
            pltpu.VMEM(line, f32),
            pltpu.VMEM((BASIS, *line), f32),
            pltpu.VMEM((BASIS, *line), f32),
            pltpu.VMEM((BASIS, *line), f32),
            pltpu.VMEM(line, f32),
            pltpu.VMEM(line, f32),
            pltpu.VMEM((3, *line), f32),
            pltpu.VMEM((BASIS, WHOLE_Z, COLS), f32),
            pltpu.VMEM(line, f32),
            pltpu.VMEM((BASIS, ROWS, PLANES, COLS), f32),
            pltpu.VMEM((1, COLS), f32),
            pltpu.VMEM((16, 1, COLS), f32),
            pltpu.VMEM((16, 1, COLS), f32),
            dma((8,)), dma((8,)), dma((8,)), dma((8,)), dma((8,)), dma((8,)), dma((8,)), dma((8,)),
            dma((2,)), dma((2,)), dma((BASIS + 1, 2, 2)), dma((BASIS + 1, 2, 2)),
            dma((BASIS,)), dma((BASIS,)), dma((2,)), dma((2,)), dma((5,)), pltpu.SemaphoreType.REGULAR,
        ],
        compiler_params=pltpu.CompilerParams(
            collective_id=0, has_side_effects=True, vmem_limit_bytes=67043328),
    )(couplings, voltage, potential, tissue, gain, line_factor)


def solution(mesh):
    block = P("gx", "gy", None)
    return jax.shard_map(
        body, mesh=mesh, in_specs=(block, block, block, block, P(), P()),
        out_specs=(block, block), check_vma=False)
```

```python
import jax
import jax.numpy as jnp
from jax import lax
from jax.experimental import pallas as pl
from jax.experimental.pallas import tpu as pltpu
from jax.sharding import PartitionSpec as P

CHEB = 8
SHIFT = 1.3
BASIS = 4
MESH = pl.DeviceIdType.MESH
HIGHEST = lax.Precision.HIGHEST
time_step = 2.0
ionic_rate = 0.5
onset_level = 0.2
gain_top = 3.0625

PLANES, ROWS, COLS = 8, 32, 128
HALO = 8
EXT_Z, EXT_Y = PLANES + 2 * HALO, ROWS + 2 * HALO
PAD_Y = EXT_Y + 16
OWN = 8 + HALO
EXT = pl.ds(8, EXT_Y)
GX, GY = 32, 8
WHOLE_Z = GX * PLANES
WHOLE_Y = GY * ROWS
TILES = WHOLE_Z // 8
LINE = WHOLE_Z + 16
LINES = pl.ds(8, WHOLE_Z)
DIRECTIONS = tuple((a, b) for a in (-1, 0, 1) for b in (-1, 0, 1) if (a, b) != (0, 0))


def z_range(a, depth):
    if a == 0:
        return pl.ds(HALO, PLANES), pl.ds(HALO, PLANES)
    if a > 0:
        return pl.ds(HALO + PLANES - depth, depth), pl.ds(HALO - depth, depth)
    return pl.ds(HALO, depth), pl.ds(HALO + PLANES, depth)


def y_range(b):
    if b == 0:
        return pl.ds(OWN, ROWS), pl.ds(OWN, ROWS)
    if b > 0:
        return pl.ds(OWN + ROWS - 8, 8), pl.ds(OWN - 8, 8)
    return pl.ds(OWN, 8), pl.ds(OWN + ROWS, 8)


def combine(k, lead, sub, lane, lead_sub, lead_lane, sub_lane, scale=1.0):
    half = 0.5 * scale
    return dict(
        lead=scale * k[lead], sub=scale * k[sub], lane=scale * k[lane],
        both=scale * k[lead_sub], cross=scale * k[lead_sub + 1],
        lead_sum=half * (k[lead_lane] + k[lead_lane + 1]), lead_diff=half * (k[lead_lane] - k[lead_lane + 1]),
        sub_sum=half * (k[sub_lane] + k[sub_lane + 1]), sub_diff=half * (k[sub_lane] - k[sub_lane + 1]))


def shift_lanes(even, odd, first, last):
    right = jnp.where(last, 0.0, pltpu.roll(even + odd, COLS - 1, 1))
    return right + jnp.where(first, 0.0, pltpu.roll(even - odd, 1, 1))


def stencil_here(read, k, first, last):
    up, down = read(0, 1), read(0, -1)
    rows = up + down
    even = k["lane"] * read(0, 0) + k["sub_sum"] * rows
    return k["sub"] * rows + shift_lanes(even, k["sub_diff"] * (up - down), first, last)


def stencil_beside(read, k, first, last):
    plus, minus = read(1, 0), read(-1, 0)
    total = plus + minus
    out = k["lead"] * total
    out = out + k["both"] * (read(1, 1) + read(-1, -1)) + k["cross"] * (read(1, -1) + read(-1, 1))
    return out + shift_lanes(k["lead_sum"] * total, k["lead_diff"] * (plus - minus), first, last)


def stencil_before(read, k, first, last):
    minus = read(-1, 0)
    out = k["lead"] * minus + k["both"] * read(-1, -1) + k["cross"] * read(-1, 1)
    return out + shift_lanes(k["lead_sum"] * minus, -(k["lead_diff"] * minus), first, last)


def stencil(read, k, first, last):
    here, plus, minus = read(0, 0), read(1, 0), read(-1, 0)
    up, down = read(0, 1), read(0, -1)
    total, diff = plus + minus, plus - minus
    rows, row_diff = up + down, up - down
    even = k["lane"] * here + k["lead_sum"] * total + k["sub_sum"] * rows
    odd = k["lead_diff"] * diff + k["sub_diff"] * row_diff
    out = k["lead"] * total + k["sub"] * rows
    out = out + k["both"] * (read(1, 1) + read(-1, -1)) + k["cross"] * (read(1, -1) + read(-1, 1))
    return out + shift_lanes(even, odd, first, last)


def owner(row):
    chip_y = row // 64
    along = row % 64
    along = along + (chip_y % 2) * (63 - 2 * along)
    chip_z = along // 8
    spot = along % 8
    spot = spot + (chip_z % 2) * (7 - 2 * spot)
    return (chip_z // 2) * 8 + spot, chip_y * 2 + chip_z % 2


def own_row(gx, gy):
    chip_y = gy // 2
    chip_z = (gx // 8) * 2 + gy % 2
    spot = gx % 8
    spot = spot + (chip_z % 2) * (7 - 2 * spot)
    along = chip_z * 8 + spot
    return chip_y * 64 + along + (chip_y % 2) * (63 - 2 * along)


def kernel(
    coup, volt_in, pot_in, tissue_in, gain_in, factor_in, new_volt, new_pot,
    volt, pot, tissue, gain, factor,
    fields, resid, upd, diag, estimate, weighted, own_term, matrix,
    stage_cond, stage_res,
    row_cond, row_res, lines, line_prev, line_next, cond_prev, cond_next,
    line_weighted, image, row_diag, back, part, gather_a, gather_b,
    s_fields, r_fields, s_cond, r_cond, s_pot, r_pot, s_resid, r_resid,
    s_rows, r_rows, s_edge, r_edge, s_back, r_back, s_sum, r_sum, s_take, far,
):
    gx = lax.axis_index("gx")
    gy = lax.axis_index("gy")
    row = own_row(gx, gy)
    own_gy = row // ROWS
    own_t = row % ROWS
    chip_z = (gx // 8) * 2 + gy % 2
    chip_y = gy // 2
    spot = gx % 8

    def at_z(z):
        return (z // 2) * 8 + spot, chip_y * 2 + z % 2

    def at_y(y):
        return gx, y * 2 + gy % 2

    takes = [
        pltpu.make_async_copy(src, dst, s_take.at[n])
        for n, (src, dst) in enumerate(
            ((tissue_in, tissue), (gain_in, gain), (volt_in, volt), (pot_in, pot), (factor_in, factor)))
    ]
    for copy in takes:
        copy.start()
    barrier = pltpu.get_barrier_semaphore()

    def greet(sem, to):
        pl.semaphore_signal(sem, inc=1, device_id=to, device_id_type=MESH)

    for a, b in DIRECTIONS:
        greet(barrier, (lax.rem(gx + a + GX, GX), lax.rem(gy + b + GY, GY)))
    for d in range(1, 8):
        greet(barrier, at_z(lax.rem(chip_z + d, 8)))
        greet(barrier, ((gx // 8) * 8 + lax.rem(spot + d, 8), gy))
    for d in range(1, 4):
        greet(barrier, at_y(lax.rem(chip_y + d, 4)))
    for copy in takes:
        copy.wait()

    lane = lax.broadcasted_iota(jnp.int32, (1, COLS), 1)
    first, last = lane == 0, lane == COLS - 1
    k_in = [coup[0, n] for n in range(9)]
    k_ex = [coup[1, n] for n in range(9)]
    z_twice = combine(k_in, 0, 1, 2, 3, 5, 7, time_step)
    z_extra = combine(k_ex, 0, 1, 2, 3, 5, 7)
    line_in = combine(k_in, 1, 0, 2, 3, 7, 5)
    line_ex = combine(k_ex, 1, 0, 2, 3, 7, 5)

    def neighbour(a, b):
        ok = (gx + a >= 0) & (gx + a < GX) & (gy + b >= 0) & (gy + b < GY)
        return ok, (gx + a, gy + b)

    def send_halo(ref, d, depth, sems_s, sems_r, stacked):
        a, b = DIRECTIONS[d]
        zs, zd = z_range(a, depth)
        ys, yd = y_range(b)
        src = ref.at[:, zs, ys, :] if stacked else ref.at[zs, ys, :]
        dst = ref.at[:, zd, yd, :] if stacked else ref.at[zd, yd, :]
        return pltpu.make_async_remote_copy(
            src_ref=src, dst_ref=dst, send_sem=sems_s.at[d], recv_sem=sems_r.at[d],
            device_id=(gx + a, gy + b), device_id_type=MESH)

    def each_halo(act, ref, depth, sems_s, sems_r, stacked, receive=False):
        for d, (a, b) in enumerate(DIRECTIONS):
            ok, _ = neighbour(-a, -b) if receive else neighbour(a, b)

            @pl.when(ok)
            def _():
                act(send_halo(ref, d, depth, sems_s, sems_r, stacked))

    def deep_conduct(d):
        a, b = DIRECTIONS[d]
        ys, yd = y_range(b)
        if a > 0:
            zs, zd = pl.ds(HALO, PLANES - 1), pl.ds(0, HALO - 1)
        else:
            zs, zd = pl.ds(HALO + 1, PLANES - 1), pl.ds(HALO + PLANES + 1, HALO - 1)
        return pltpu.make_async_remote_copy(
            src_ref=fields.at[1, zs, ys, :], dst_ref=fields.at[1, zd, yd, :],
            send_sem=s_cond.at[d], recv_sem=r_cond.at[d],
            device_id=(gx + a, gy + b), device_id_type=MESH)

    def each_deep(act, receive=False):
        for d, (a, b) in enumerate(DIRECTIONS):
            if a == 0:
                continue
            ok, _ = neighbour(-a, -b) if receive else neighbour(a, b)

            @pl.when(ok)
            def _():
                act(deep_conduct(d))

    def start(copy):
        copy.start()

    def wait_recv(copy):
        copy.wait_recv()

    def wait_send(copy):
        copy.wait_send()

    own_group = own_gy == gy

    def row_tile(i):
        return pl.ds(pl.multiple_of(8 + 8 * i, 8), 8)

    turned = chip_y % 2
    upper = gy % 2 + turned * (1 - 2 * (gy % 2))

    def scatter_rows(stage, rows_ref, n):
        def one(d, _):
            m = lax.rem(gx + d, 32)
            z, q = m // 8, lax.rem(m, 8)
            z_odd = lax.rem(z, 2)
            to_gx = upper * 16 + (z // 2) * 8 + q + z_odd * (7 - 2 * q)
            to_gy = chip_y * 2 + z_odd
            t = m + turned * (31 - 2 * m)

            @pl.when((to_gx != gx) | (to_gy != gy))
            def _():
                pltpu.make_async_remote_copy(
                    src_ref=stage.at[t], dst_ref=rows_ref.at[row_tile(gx)],
                    send_sem=s_rows.at[n], recv_sem=r_rows.at[n],
                    device_id=(to_gx, to_gy), device_id_type=MESH).start()
            return 0

        lax.fori_loop(0, ROWS, one, 0, unroll=4)

        @pl.when(own_group)
        def _():
            rows_ref[row_tile(gx)] = stage[own_t]

    def wait_rows(stage, rows_ref, n):
        @pl.when(own_group)
        def _():
            part_ref = rows_ref.at[pl.ds(8, WHOLE_Z - 8)]
            pltpu.make_async_copy(part_ref, part_ref, r_rows.at[n]).wait()

        @pl.when(jnp.logical_not(own_group))
        def _():
            part_ref = rows_ref.at[LINES]
            pltpu.make_async_copy(part_ref, part_ref, r_rows.at[n]).wait()

    def wait_rows_sent(stage, n):
        @pl.when(own_group)
        def _():
            part_ref = stage.at[pl.ds(0, ROWS - 1)]
            pltpu.make_async_copy(part_ref, part_ref, s_rows.at[n]).wait()

        @pl.when(jnp.logical_not(own_group))
        def _():
            pltpu.make_async_copy(stage, stage, s_rows.at[n]).wait()

    def send_back(k):
        def one(d, _):
            i = lax.rem(gx + d, GX)

            @pl.when((i != gx) | (own_gy != gy))
            def _():
                pltpu.make_async_remote_copy(
                    src_ref=lines.at[k, row_tile(i)], dst_ref=back.at[k, own_t],
                    send_sem=s_back.at[k], recv_sem=r_back.at[k],
                    device_id=(i, own_gy), device_id_type=MESH).start()
            return 0

        lax.fori_loop(0, GX, one, 0, unroll=4)

        @pl.when(own_group)
        def _():
            back[k, own_t] = lines[k, row_tile(gx)]

    def wait_back(k):
        @pl.when(own_group)
        def _():
            got = back.at[k, pl.ds(0, ROWS - 1)]
            pltpu.make_async_copy(got, got, r_back.at[k]).wait()
            pltpu.make_async_copy(got, got, s_back.at[k]).wait()

        @pl.when(jnp.logical_not(own_group))
        def _():
            pltpu.make_async_copy(back.at[k], back.at[k], r_back.at[k]).wait()
            pltpu.make_async_copy(back.at[k], back.at[k], s_back.at[k]).wait()

    inner = LINES

    HALF = WHOLE_Z // 2

    def edge(src, dst, n, side, part):
        to_gx, to_gy = owner(row + (1 if side == 0 else -1))
        rows = pl.ds(8 + part * HALF, HALF)
        return pltpu.make_async_remote_copy(
            src_ref=src.at[rows], dst_ref=dst.at[rows],
            send_sem=s_edge.at[n, side, part], recv_sem=r_edge.at[n, side, part],
            device_id=(to_gx, to_gy), device_id_type=MESH)

    has_next, has_prev = row < WHOLE_Y - 1, row > 0

    def edges_start(src, prev, nxt, n, part):
        @pl.when(has_next)
        def _():
            edge(src, prev, n, 0, part).start()

        if n != BASIS - 1:
            @pl.when(has_prev)
            def _():
                edge(src, nxt, n, 1, part).start()

    def edges_wait(src, prev, nxt, n, part):
        @pl.when(has_prev)
        def _():
            edge(src, prev, n, 0, part).wait_recv()

        if n != BASIS - 1:
            @pl.when(has_next)
            def _():
                edge(src, nxt, n, 1, part).wait_recv()

    def edges_sent(src, prev, nxt, n, part):
        @pl.when(has_next)
        def _():
            edge(src, prev, n, 0, part).wait_send()

        if n != BASIS - 1:
            @pl.when(has_prev)
            def _():
                edge(src, nxt, n, 1, part).wait_send()

    own_y = pl.ds(OWN, ROWS)
    conduct = tissue[...].astype(jnp.float32) * gain[...]
    own = (pl.ds(HALO, PLANES), own_y, slice(None))
    fields[0, *own] = volt[...] + pot[...]
    fields[1, *own] = conduct
    fields[2, *own] = pot[...]
    pl.semaphore_wait(barrier, 25)
    near = fields.at[pl.ds(0, 2)]
    each_halo(start, near, 1, s_fields, r_fields, True)
    each_halo(start, fields.at[2], 1, s_pot, r_pot, False)
    each_deep(start)
    for d in range(1, 8):
        greet(far, at_z(lax.rem(chip_z + d, 8)))
    for d in range(1, 4):
        greet(far, at_y(lax.rem(chip_y + d, 4)))
    v = volt[...]
    ionic = tissue[...].astype(jnp.float32) * v * (v - onset_level) * (v - 1.0)
    own_term[...] = -ionic_rate * ionic

    for d, (a, b) in enumerate(DIRECTIONS):
        ok, _ = neighbour(-a, -b)

        @pl.when(jnp.logical_not(ok))
        def _():
            zd = z_range(a, HALO)[1]
            yd = y_range(b)[1]
            shape = (zd.size, yd.size, COLS)
            for n in range(3):
                fields[n, zd, yd, :] = jnp.zeros(shape, jnp.float32)
            resid[zd, yd, :] = jnp.zeros(shape, jnp.float32)
    stage_cond[...] = jnp.swapaxes(conduct, 0, 1)
    tile = jnp.zeros((8, COLS), jnp.float32)
    beyond = (pl.ds(0, 8), pl.ds(PAD_Y - 8, 8))

    def blank_rows(z, _):
        for rows in beyond:
            fields[1, z, rows, :] = tile
            weighted[0, z, rows, :] = tile
            weighted[1, z, rows, :] = tile
        return 0

    lax.fori_loop(0, EXT_Z, blank_rows, 0)
    ends = (pl.ds(0, 8), pl.ds(LINE - 8, 8))
    for rows in ends:
        for ref in (row_cond, row_res, cond_prev, cond_next):
            ref[rows] = tile
        for k in range(BASIS):
            for ref in (lines, line_prev, line_next):
                ref[k, rows] = tile
    blank = jnp.zeros((WHOLE_Z, COLS), jnp.float32)

    @pl.when(jnp.logical_not(has_prev))
    def _():
        cond_prev[LINES] = blank
        for k in range(BASIS):
            line_prev[k, LINES] = blank

    @pl.when(jnp.logical_not(has_next))
    def _():
        cond_next[LINES] = blank
        for k in range(BASIS):
            line_next[k, LINES] = blank

    whole = lax.dot_general(
        factor[...], factor[...], (((0,), (0,)), ((), ())), precision=HIGHEST,
        preferred_element_type=jnp.float32)
    in_sum = k_in[0]
    ex_sum = k_ex[0]
    for n in range(1, 9):
        in_sum = in_sum + k_in[n]
        ex_sum = ex_sum + k_ex[n]
    reach = jnp.max(jnp.sum(jnp.abs(whole), axis=1, keepdims=True), axis=0, keepdims=True)
    bound = reach * (4.0 * gain_top * in_sum + 4.0 * ex_sum)
    scaled = whole * (1.0 / bound)
    coarse = scaled.astype(jnp.bfloat16)
    matrix[0] = coarse
    matrix[1] = (scaled - coarse.astype(jnp.float32)).astype(jnp.bfloat16)
    eye = lax.broadcasted_iota(jnp.int32, whole.shape, 0) == lax.broadcasted_iota(jnp.int32, whole.shape, 1)
    mean = jnp.sum(jnp.sum(jnp.where(eye, whole, 0.0), axis=1, keepdims=True), axis=0, keepdims=True) / WHOLE_Z
    shift = SHIFT * mean * (2.0 * in_sum + 2.0 * ex_sum) / bound

    top = 1.0 + time_step * 4.0 * gain_top * in_sum
    ones = jnp.ones((1, COLS), jnp.float32)
    top = ones * top
    centre = (top + 1.0) / 2.0
    half = (top - 1.0) / 2.0
    ratio = centre / half
    weight = 1.0 / ratio

    each_halo(wait_recv, near, 1, s_fields, r_fields, True, receive=True)

    def moved(ref, z, at, rows):
        return lambda i, j: ref[z + i, pl.ds(at + j, rows), :]

    cond = fields.at[1]

    def weigh(z, _):
        weighted[0, z, EXT, :] = cond[z, EXT, :] * (fields[0, z, EXT, :])
        return 0

    lax.fori_loop(HALO - 1, HALO + PLANES + 1, weigh, 0)

    def first_plane(z, _):
        s = stencil(moved(cond, z, OWN, ROWS), z_twice, first, last)
        flux = s * fields[0, z, own_y, :] - stencil(moved(weighted.at[0], z, OWN, ROWS), z_twice, first, last)
        resid[z, own_y, :] = own_term[z - HALO] - cond[z, own_y, :] * flux
        return 0

    lax.fori_loop(HALO, HALO + PLANES, first_plane, 0)
    each_halo(start, resid, HALO, s_resid, r_resid, False)

    each_halo(wait_recv, fields.at[2], 1, s_pot, r_pot, False, receive=True)
    ex_total = 2.0 * ex_sum

    def extra_plane(z, _):
        ke = stencil(moved(fields.at[2], z, OWN, ROWS), z_extra, first, last)
        own_term[z - HALO] = ke - ex_total * fields[2, z, own_y, :]
        return 0

    lax.fori_loop(HALO, HALO + PLANES, extra_plane, 0)
    pl.semaphore_wait(far, 10)
    scatter_rows(stage_cond, row_cond, 0)
    each_deep(wait_recv, receive=True)

    def diag_plane(z, _):
        diag[z, EXT, :] = 1.0 + cond[z, EXT, :] * stencil(moved(cond, z, 8, EXT_Y), z_twice, first, last)
        return 0

    lax.fori_loop(1, EXT_Z - 1, diag_plane, 0)
    each_halo(wait_send, near, 1, s_fields, r_fields, True)
    each_halo(wait_recv, resid, HALO, s_resid, r_resid, False, receive=True)

    inv_centre = 1.0 / centre

    def first_update(z, _):
        u = resid[z, EXT, :] * inv_centre
        upd[z, EXT, :] = u
        estimate[z, EXT, :] = u
        weighted[0, z, EXT, :] = cond[z, EXT, :] * u
        return 0

    lax.fori_loop(0, EXT_Z, first_update, 0)

    def sweep(n, weight, margin):
        old = weighted.at[lax.rem(n + 1, 2)]
        new = lax.rem(n, 2)
        weight_next = 1.0 / (2.0 * ratio - weight)
        keep = weight_next * weight
        gain_r = 2.0 * weight_next / half
        at, count = OWN - margin, ROWS + 2 * margin
        rows = pl.ds(at, count)

        def one(z):
            u = upd[z, rows, :]
            c = cond[z, rows, :]
            r = resid[z, rows, :] - diag[z, rows, :] * u + c * stencil(moved(old, z, at, count), z_twice, first, last)
            fresh = keep * u + gain_r * r
            return r, fresh, estimate[z, rows, :] + fresh, c * fresh

        def pair(i, _):
            planes = [n + 2 * i, n + 2 * i + 1]
            for z, (r, fresh, total, flux) in zip(planes, [one(z) for z in planes]):
                resid[z, rows, :] = r
                upd[z, rows, :] = fresh
                estimate[z, rows, :] = total
                weighted[new, z, rows, :] = flux
            return 0

        lax.fori_loop(0, EXT_Z // 2 - n, pair, 0)
        return weight_next

    each_halo(wait_send, resid, HALO, s_resid, r_resid, False)
    weight = lax.fori_loop(1, 4, lambda n, w: sweep(n, w, 8), weight)
    weight = lax.fori_loop(4, CHEB - 2, lambda n, w: sweep(n, w, 4), weight)
    wait_rows(stage_cond, row_cond, 0)
    for half_line in range(2):
        edges_start(row_cond, cond_prev, cond_next, BASIS, half_line)
    lax.fori_loop(CHEB - 2, CHEB, lambda n, w: sweep(n, w, 4), weight)

    def total_plane(z, _):
        total = fields[0, z, EXT, :] + estimate[z, EXT, :]
        fields[0, z, EXT, :] = total
        weighted[0, z, EXT, :] = cond[z, EXT, :] * total
        return 0

    lax.fori_loop(HALO - 1, HALO + PLANES + 1, total_plane, 0)

    def elliptic_plane(z, _):
        twice = (diag[z, own_y, :] - 1.0) * fields[0, z, own_y, :]
        twice = twice - cond[z, own_y, :] * stencil(moved(weighted.at[0], z, OWN, ROWS), z_twice, first, last)
        own_term[z - HALO] = own_term[z - HALO] - twice / time_step
        return 0

    lax.fori_loop(HALO, HALO + PLANES, elliptic_plane, 0)
    stage_res[...] = jnp.swapaxes(own_term[...], 0, 1)
    scatter_rows(stage_res, row_res, 1)

    gain[...] = volt[...] + estimate[pl.ds(HALO, PLANES), own_y, :]
    early = pltpu.make_async_copy(gain, new_volt, s_take.at[0])
    early.start()
    wait_rows(stage_res, row_res, 1)

    def apply_matrix(src, k, shift=None):
        coarse = src.astype(jnp.bfloat16)
        fine = (src - coarse.astype(jnp.float32)).astype(jnp.bfloat16)

        def dot(a, b):
            return jnp.dot(a, b, preferred_element_type=jnp.float32)

        for part in range(2):
            rows = pl.ds(part * HALF, HALF)
            out = dot(matrix[0, rows], fine) + dot(matrix[1, rows], coarse) + dot(matrix[0, rows], coarse)
            if shift is not None:
                out = out - shift * lines[k - 1, pl.ds(8 + part * HALF, HALF)]
            lines[k, pl.ds(8 + part * HALF, HALF)] = out
            edges_start(lines.at[k], line_prev.at[k], line_next.at[k], k, part)

    sums = jnp.zeros((1, COLS), jnp.float32)

    def product(sums, e, a, b):
        total = jnp.sum((a * b).reshape(4, TILES // 4, 8, COLS), axis=0)
        total = jnp.sum(jnp.sum(total, axis=0), axis=0, keepdims=True)
        return sums + jnp.where(lane == e, jnp.sum(total, axis=1, keepdims=True), 0.0)

    CHUNK = 64

    def near_rows(refs, at):
        return lambda i, j: refs[i + 1][pl.ds(at + j, CHUNK), :]

    weigh_refs = [line_weighted.at[n] for n in range(3)]
    cond_refs = [cond_prev, row_cond, cond_next]

    def operate_here(k):
        basis = [None, lines.at[k], None]
        for at in range(8, 8 + WHOLE_Z, CHUNK):
            rows = pl.ds(at, CHUNK)
            ki = row_diag[rows] * lines[k, rows]
            ki = ki - row_cond[rows] * stencil_here(near_rows(weigh_refs, at), line_in, first, last)
            image[k, pl.ds(at - 8, CHUNK)] = ki - stencil_here(near_rows(basis, at), line_ex, first, last)

    def operate_beside(k):
        basis = [line_prev.at[k], None, line_next.at[k]]
        split = 8 + HALF
        for part, lined in enumerate((pl.ds(0, split), pl.ds(split, LINE - split))):
            edges_wait(lines.at[k], line_prev.at[k], line_next.at[k], k, part)
            for n in (0, 2) if k < BASIS - 1 else (0,):
                weigh_refs[n][lined] = cond_refs[n][lined] * basis[n][lined]
            for at in (range(8, split - CHUNK, CHUNK) if part == 0 else range(split - CHUNK, 8 + WHOLE_Z, CHUNK)):
                rows = pl.ds(at, CHUNK)
                beside = stencil_beside if k < BASIS - 1 else stencil_before
                ki = row_cond[rows] * beside(near_rows(weigh_refs, at), line_in, first, last)
                ki = ki + beside(near_rows(basis, at), line_ex, first, last)
                if k == BASIS - 1:
                    ki = 2.0 * ki
                image[k, pl.ds(at - 8, CHUNK)] = image[k, pl.ds(at - 8, CHUNK)] - ki

    def line_diag():
        for at in range(8, 8 + WHOLE_Z, CHUNK):
            rows = pl.ds(at, CHUNK)
            row_diag[rows] = ex_total + row_cond[rows] * stencil(near_rows(cond_refs, at), line_in, first, last)

    apply_matrix(row_res[inner], 0)
    send_back(0)
    weigh_refs[1][...] = row_cond[...] * lines[0]
    for half_line in range(2):
        edges_wait(row_cond, cond_prev, cond_next, BASIS, half_line)
    line_diag()
    operate_here(0)
    sums = product(sums, 0, lines[0, inner], row_res[inner])

    at = BASIS
    for k in range(BASIS):
        operate_beside(k)
        if k < BASIS - 1:
            apply_matrix(image[k], k + 1, shift)
            send_back(k + 1)
            weigh_refs[1][...] = row_cond[...] * lines[k + 1]
            operate_here(k + 1)
            sums = product(sums, k + 1, lines[k + 1, inner], row_res[inner])
            for m in range(k + 1):
                sums = product(sums, at, lines[m, inner], image[k])
                at += 1
            if k == BASIS - 2:
                for m in range(k + 1):
                    sums = product(sums, at, lines[k + 1, inner], image[m])
                    at += 1
        else:
            sums = product(sums, at, lines[k, inner], image[k])

    def sum_over(sums, buf, n, me, peers):
        part[...] = sums
        buf[me] = sums
        for to in peers:
            pltpu.make_async_remote_copy(
                src_ref=part, dst_ref=buf.at[me], send_sem=s_sum.at[n], recv_sem=r_sum.at[n],
                device_id=to, device_id_type=MESH).start()
        got = buf.at[pl.ds(0, 15)]
        pltpu.make_async_copy(got, got, r_sum.at[n]).wait()
        pltpu.make_async_copy(got, got, s_sum.at[n]).wait()
        return jnp.sum(buf[...], axis=0)

    def hops(d, n):
        return min(d, n - d)

    chip_x, core = spot // 2, spot % 2
    steps = sorted(((x, y) for x in range(4) for y in range(4) if (x, y) != (0, 0)),
                   key=lambda p: (-hops(p[0], 4) - hops(p[1], 4), p))
    sums = sum_over(sums, gather_a, 0, chip_x * 4 + chip_y, [
        ((gx // 8) * 8 + lax.rem(chip_x + x, 4) * 2 + core, lax.rem(chip_y + y, 4) * 2 + gy % 2)
        for x, y in steps])
    steps = sorted(((z, c) for z in range(8) for c in range(2) if (z, c) != (0, 0)),
                   key=lambda p: (-hops(p[0], 8) - 0.5 * p[1], p))
    peers = []
    for z, c in steps:
        to_z = lax.rem(chip_z + z, 8)
        peers.append(((to_z // 2) * 8 + chip_x * 2 + (core + c) % 2, chip_y * 2 + to_z % 2))
    sums = sum_over(sums, gather_b, 1, chip_z * 2 + core, peers)

    value = [jnp.sum(jnp.where(lane == e, sums, 0.0), axis=1, keepdims=True) for e in range(14)]
    rhs = value[:BASIS]
    gram = {}
    at = BASIS
    for k in range(BASIS):
        for m in range(k + 1):
            gram[m, k] = value[at]
            at += 1

    low, pivot = {}, {}
    for j in range(BASIS):
        d = gram[j, j]
        for m in range(j):
            d = d - low[j, m] * low[j, m] * pivot[m]
        pivot[j] = d
        for i in range(j + 1, BASIS):
            e = gram[j, i]
            for m in range(j):
                e = e - low[i, m] * low[j, m] * pivot[m]
            low[i, j] = e / d
    sol = list(rhs)
    for i in range(BASIS):
        for m in range(i):
            sol[i] = sol[i] - low[i, m] * sol[m]
    sol = [a / pivot[i] for i, a in enumerate(sol)]
    for i in reversed(range(BASIS)):
        for m in range(i + 1, BASIS):
            sol[i] = sol[i] - low[m, i] * sol[m]

    for k in range(BASIS):
        wait_back(k)
    total = sol[0] * back[0]
    for k in range(1, BASIS):
        total = total + sol[k] * back[k]
    new_pot[...] = pot[...] + jnp.swapaxes(total, 0, 1)

    early.wait()
    each_deep(wait_send)
    each_halo(wait_send, fields.at[2], 1, s_pot, r_pot, False)
    wait_rows_sent(stage_cond, 0)
    wait_rows_sent(stage_res, 1)
    for half_line in range(2):
        edges_sent(row_cond, cond_prev, cond_next, BASIS, half_line)
        for k in range(BASIS):
            edges_sent(lines.at[k], line_prev.at[k], line_next.at[k], k, half_line)


def body(voltage, potential, tissue, gain, couplings, line_factor):
    f32 = jnp.float32
    block = jax.ShapeDtypeStruct((PLANES, ROWS, COLS), f32)
    vmem = pl.BlockSpec(memory_space=pltpu.VMEM)
    line = (LINE, COLS)
    dma = pltpu.SemaphoreType.DMA
    return pl.pallas_call(
        kernel,
        name="bidomain",
        out_shape=(block, block),
        in_specs=[pl.BlockSpec(memory_space=pltpu.SMEM)] + [pl.BlockSpec(memory_space=pl.ANY)] * 5,
        out_specs=(pl.BlockSpec(memory_space=pl.ANY), vmem),
        scratch_shapes=[
            pltpu.VMEM((PLANES, ROWS, COLS), f32),
            pltpu.VMEM((PLANES, ROWS, COLS), f32),
            pltpu.VMEM((PLANES, ROWS, COLS), jnp.int32),
            pltpu.VMEM((PLANES, ROWS, COLS), f32),
            pltpu.VMEM((WHOLE_Z, WHOLE_Z), f32),
            pltpu.VMEM((3, EXT_Z, PAD_Y, COLS), f32),
            pltpu.VMEM((EXT_Z, PAD_Y, COLS), f32),
            pltpu.VMEM((EXT_Z, PAD_Y, COLS), f32),
            pltpu.VMEM((EXT_Z, PAD_Y, COLS), f32),
            pltpu.VMEM((EXT_Z, PAD_Y, COLS), f32),
            pltpu.VMEM((2, EXT_Z, PAD_Y, COLS), f32),
            pltpu.VMEM((PLANES, ROWS, COLS), f32),
            pltpu.VMEM((2, WHOLE_Z, WHOLE_Z), jnp.bfloat16),
            pltpu.VMEM((ROWS, PLANES, COLS), f32),
            pltpu.VMEM((ROWS, PLANES, COLS), f32),
            pltpu.VMEM(line, f32),
            pltpu.VMEM(line, f32),
            pltpu.VMEM((BASIS, *line), f32),
            pltpu.VMEM((BASIS, *line), f32),
            pltpu.VMEM((BASIS, *line), f32),
            pltpu.VMEM(line, f32),
            pltpu.VMEM(line, f32),
            pltpu.VMEM((3, *line), f32),
            pltpu.VMEM((BASIS, WHOLE_Z, COLS), f32),
            pltpu.VMEM(line, f32),
            pltpu.VMEM((BASIS, ROWS, PLANES, COLS), f32),
            pltpu.VMEM((1, COLS), f32),
            pltpu.VMEM((16, 1, COLS), f32),
            pltpu.VMEM((16, 1, COLS), f32),
            dma((8,)), dma((8,)), dma((8,)), dma((8,)), dma((8,)), dma((8,)), dma((8,)), dma((8,)),
            dma((2,)), dma((2,)), dma((BASIS + 1, 2, 2)), dma((BASIS + 1, 2, 2)),
            dma((BASIS,)), dma((BASIS,)), dma((2,)), dma((2,)), dma((5,)), pltpu.SemaphoreType.REGULAR,
        ],
        compiler_params=pltpu.CompilerParams(
            collective_id=0, has_side_effects=True, vmem_limit_bytes=67043328),
    )(couplings, voltage, potential, tissue, gain, line_factor)


def solution(mesh):
    block = P("gx", "gy", None)
    return jax.shard_map(
        body, mesh=mesh, in_specs=(block, block, block, block, P(), P()),
        out_specs=(block, block), check_vma=False)
```

```python
import jax
import jax.numpy as jnp
from jax import lax
from jax.experimental import pallas as pl
from jax.experimental.pallas import tpu as pltpu
from jax.sharding import PartitionSpec as P

CHEB = 8
SHIFT = 1.3
BASIS = 4
MESH = pl.DeviceIdType.MESH
HIGHEST = lax.Precision.HIGHEST
time_step = 2.0
ionic_rate = 0.5
onset_level = 0.2
gain_top = 3.0625

PLANES, ROWS, COLS = 8, 32, 128
HALO = 8
EXT_Z, EXT_Y = PLANES + 2 * HALO, ROWS + 2 * HALO
PAD_Y = EXT_Y + 16
OWN = 8 + HALO
EXT = pl.ds(8, EXT_Y)
GX, GY = 32, 8
WHOLE_Z = GX * PLANES
WHOLE_Y = GY * ROWS
TILES = WHOLE_Z // 8
LINE = WHOLE_Z + 16
LINES = pl.ds(8, WHOLE_Z)
DIRECTIONS = tuple((a, b) for a in (-1, 0, 1) for b in (-1, 0, 1) if (a, b) != (0, 0))


def z_range(a, depth):
    if a == 0:
        return pl.ds(HALO, PLANES), pl.ds(HALO, PLANES)
    if a > 0:
        return pl.ds(HALO + PLANES - depth, depth), pl.ds(HALO - depth, depth)
    return pl.ds(HALO, depth), pl.ds(HALO + PLANES, depth)


def y_range(b):
    if b == 0:
        return pl.ds(OWN, ROWS), pl.ds(OWN, ROWS)
    if b > 0:
        return pl.ds(OWN + ROWS - 8, 8), pl.ds(OWN - 8, 8)
    return pl.ds(OWN, 8), pl.ds(OWN + ROWS, 8)


def combine(k, lead, sub, lane, lead_sub, lead_lane, sub_lane, scale=1.0):
    half = 0.5 * scale
    return dict(
        lead=scale * k[lead], sub=scale * k[sub], lane=scale * k[lane],
        both=scale * k[lead_sub], cross=scale * k[lead_sub + 1],
        lead_sum=half * (k[lead_lane] + k[lead_lane + 1]), lead_diff=half * (k[lead_lane] - k[lead_lane + 1]),
        sub_sum=half * (k[sub_lane] + k[sub_lane + 1]), sub_diff=half * (k[sub_lane] - k[sub_lane + 1]))


def shift_lanes(even, odd, first, last):
    right = jnp.where(last, 0.0, pltpu.roll(even + odd, COLS - 1, 1))
    return right + jnp.where(first, 0.0, pltpu.roll(even - odd, 1, 1))


def stencil_here(read, k, first, last):
    up, down = read(0, 1), read(0, -1)
    rows = up + down
    even = k["lane"] * read(0, 0) + k["sub_sum"] * rows
    return k["sub"] * rows + shift_lanes(even, k["sub_diff"] * (up - down), first, last)


def stencil_beside(read, k, first, last):
    plus, minus = read(1, 0), read(-1, 0)
    total = plus + minus
    out = k["lead"] * total
    out = out + k["both"] * (read(1, 1) + read(-1, -1)) + k["cross"] * (read(1, -1) + read(-1, 1))
    return out + shift_lanes(k["lead_sum"] * total, k["lead_diff"] * (plus - minus), first, last)


def stencil_before(read, k, first, last):
    minus = read(-1, 0)
    out = k["lead"] * minus + k["both"] * read(-1, -1) + k["cross"] * read(-1, 1)
    return out + shift_lanes(k["lead_sum"] * minus, -(k["lead_diff"] * minus), first, last)


def stencil(read, k, first, last):
    here, plus, minus = read(0, 0), read(1, 0), read(-1, 0)
    up, down = read(0, 1), read(0, -1)
    total, diff = plus + minus, plus - minus
    rows, row_diff = up + down, up - down
    even = k["lane"] * here + k["lead_sum"] * total + k["sub_sum"] * rows
    odd = k["lead_diff"] * diff + k["sub_diff"] * row_diff
    out = k["lead"] * total + k["sub"] * rows
    out = out + k["both"] * (read(1, 1) + read(-1, -1)) + k["cross"] * (read(1, -1) + read(-1, 1))
    return out + shift_lanes(even, odd, first, last)


def owner(row):
    chip_y = row // 64
    along = row % 64
    along = along + (chip_y % 2) * (63 - 2 * along)
    chip_z = along // 8
    spot = along % 8
    spot = spot + (chip_z % 2) * (7 - 2 * spot)
    return (chip_z // 2) * 8 + spot, chip_y * 2 + chip_z % 2


def own_row(gx, gy):
    chip_y = gy // 2
    chip_z = (gx // 8) * 2 + gy % 2
    spot = gx % 8
    spot = spot + (chip_z % 2) * (7 - 2 * spot)
    along = chip_z * 8 + spot
    return chip_y * 64 + along + (chip_y % 2) * (63 - 2 * along)


def kernel(
    coup, volt_in, pot_in, tissue_in, gain_in, factor_in, new_volt, new_pot,
    volt, pot, tissue, gain, factor,
    fields, resid, upd, diag, estimate, weighted, own_term, matrix,
    stage_cond, stage_res,
    row_cond, row_res, lines, line_prev, line_next, cond_prev, cond_next,
    line_weighted, image, row_diag, back, part, gather_a, gather_b,
    s_fields, r_fields, s_cond, r_cond, s_pot, r_pot, s_resid, r_resid,
    s_rows, r_rows, s_edge, r_edge, s_back, r_back, s_sum, r_sum, s_take, far,
):
    gx = lax.axis_index("gx")
    gy = lax.axis_index("gy")
    row = own_row(gx, gy)
    own_gy = row // ROWS
    own_t = row % ROWS
    chip_z = (gx // 8) * 2 + gy % 2
    chip_y = gy // 2
    spot = gx % 8

    def at_z(z):
        return (z // 2) * 8 + spot, chip_y * 2 + z % 2

    def at_y(y):
        return gx, y * 2 + gy % 2

    takes = [
        pltpu.make_async_copy(src, dst, s_take.at[n])
        for n, (src, dst) in enumerate(
            ((tissue_in, tissue), (gain_in, gain), (volt_in, volt), (pot_in, pot), (factor_in, factor)))
    ]
    for copy in takes:
        copy.start()
    barrier = pltpu.get_barrier_semaphore()

    def greet(sem, to):
        pl.semaphore_signal(sem, inc=1, device_id=to, device_id_type=MESH)

    for a, b in DIRECTIONS:
        greet(barrier, (lax.rem(gx + a + GX, GX), lax.rem(gy + b + GY, GY)))
    for d in range(1, 8):
        greet(barrier, at_z(lax.rem(chip_z + d, 8)))
        greet(barrier, ((gx // 8) * 8 + lax.rem(spot + d, 8), gy))
    for d in range(1, 4):
        greet(barrier, at_y(lax.rem(chip_y + d, 4)))
    for copy in takes:
        copy.wait()

    lane = lax.broadcasted_iota(jnp.int32, (1, COLS), 1)
    first, last = lane == 0, lane == COLS - 1
    k_in = [coup[0, n] for n in range(9)]
    k_ex = [coup[1, n] for n in range(9)]
    z_twice = combine(k_in, 0, 1, 2, 3, 5, 7, time_step)
    z_extra = combine(k_ex, 0, 1, 2, 3, 5, 7)
    line_in = combine(k_in, 1, 0, 2, 3, 7, 5)
    line_ex = combine(k_ex, 1, 0, 2, 3, 7, 5)

    def neighbour(a, b):
        ok = (gx + a >= 0) & (gx + a < GX) & (gy + b >= 0) & (gy + b < GY)
        return ok, (gx + a, gy + b)

    def send_halo(ref, d, depth, sems_s, sems_r, stacked):
        a, b = DIRECTIONS[d]
        zs, zd = z_range(a, depth)
        ys, yd = y_range(b)
        src = ref.at[:, zs, ys, :] if stacked else ref.at[zs, ys, :]
        dst = ref.at[:, zd, yd, :] if stacked else ref.at[zd, yd, :]
        return pltpu.make_async_remote_copy(
            src_ref=src, dst_ref=dst, send_sem=sems_s.at[d], recv_sem=sems_r.at[d],
            device_id=(gx + a, gy + b), device_id_type=MESH)

    def each_halo(act, ref, depth, sems_s, sems_r, stacked, receive=False):
        for d, (a, b) in enumerate(DIRECTIONS):
            ok, _ = neighbour(-a, -b) if receive else neighbour(a, b)

            @pl.when(ok)
            def _():
                act(send_halo(ref, d, depth, sems_s, sems_r, stacked))

    def deep_conduct(d):
        a, b = DIRECTIONS[d]
        ys, yd = y_range(b)
        if a > 0:
            zs, zd = pl.ds(HALO, PLANES - 1), pl.ds(0, HALO - 1)
        else:
            zs, zd = pl.ds(HALO + 1, PLANES - 1), pl.ds(HALO + PLANES + 1, HALO - 1)
        return pltpu.make_async_remote_copy(
            src_ref=fields.at[1, zs, ys, :], dst_ref=fields.at[1, zd, yd, :],
            send_sem=s_cond.at[d], recv_sem=r_cond.at[d],
            device_id=(gx + a, gy + b), device_id_type=MESH)

    def each_deep(act, receive=False):
        for d, (a, b) in enumerate(DIRECTIONS):
            if a == 0:
                continue
            ok, _ = neighbour(-a, -b) if receive else neighbour(a, b)

            @pl.when(ok)
            def _():
                act(deep_conduct(d))

    def start(copy):
        copy.start()

    def wait_recv(copy):
        copy.wait_recv()

    def wait_send(copy):
        copy.wait_send()

    own_group = own_gy == gy

    def row_tile(i):
        return pl.ds(pl.multiple_of(8 + 8 * i, 8), 8)

    turned = chip_y % 2
    upper = gy % 2 + turned * (1 - 2 * (gy % 2))

    def scatter_rows(stage, rows_ref, n):
        def one(d, _):
            m = lax.rem(gx + d, 32)
            z, q = m // 8, lax.rem(m, 8)
            z_odd = lax.rem(z, 2)
            to_gx = upper * 16 + (z // 2) * 8 + q + z_odd * (7 - 2 * q)
            to_gy = chip_y * 2 + z_odd
            t = m + turned * (31 - 2 * m)

            @pl.when((to_gx != gx) | (to_gy != gy))
            def _():
                pltpu.make_async_remote_copy(
                    src_ref=stage.at[t], dst_ref=rows_ref.at[row_tile(gx)],
                    send_sem=s_rows.at[n], recv_sem=r_rows.at[n],
                    device_id=(to_gx, to_gy), device_id_type=MESH).start()
            return 0

        lax.fori_loop(0, ROWS, one, 0, unroll=4)

        @pl.when(own_group)
        def _():
            rows_ref[row_tile(gx)] = stage[own_t]

    def wait_rows(stage, rows_ref, n):
        @pl.when(own_group)
        def _():
            part_ref = rows_ref.at[pl.ds(8, WHOLE_Z - 8)]
            pltpu.make_async_copy(part_ref, part_ref, r_rows.at[n]).wait()

        @pl.when(jnp.logical_not(own_group))
        def _():
            part_ref = rows_ref.at[LINES]
            pltpu.make_async_copy(part_ref, part_ref, r_rows.at[n]).wait()

    def wait_rows_sent(stage, n):
        @pl.when(own_group)
        def _():
            part_ref = stage.at[pl.ds(0, ROWS - 1)]
            pltpu.make_async_copy(part_ref, part_ref, s_rows.at[n]).wait()

        @pl.when(jnp.logical_not(own_group))
        def _():
            pltpu.make_async_copy(stage, stage, s_rows.at[n]).wait()

    def send_back(k):
        def one(d, _):
            i = lax.rem(gx + d, GX)

            @pl.when((i != gx) | (own_gy != gy))
            def _():
                pltpu.make_async_remote_copy(
                    src_ref=lines.at[k, row_tile(i)], dst_ref=back.at[k, own_t],
                    send_sem=s_back.at[k], recv_sem=r_back.at[k],
                    device_id=(i, own_gy), device_id_type=MESH).start()
            return 0

        lax.fori_loop(0, GX, one, 0, unroll=4)

        @pl.when(own_group)
        def _():
            back[k, own_t] = lines[k, row_tile(gx)]

    def wait_back(k):
        @pl.when(own_group)
        def _():
            got = back.at[k, pl.ds(0, ROWS - 1)]
            pltpu.make_async_copy(got, got, r_back.at[k]).wait()
            pltpu.make_async_copy(got, got, s_back.at[k]).wait()

        @pl.when(jnp.logical_not(own_group))
        def _():
            pltpu.make_async_copy(back.at[k], back.at[k], r_back.at[k]).wait()
            pltpu.make_async_copy(back.at[k], back.at[k], s_back.at[k]).wait()

    inner = LINES

    HALF = WHOLE_Z // 2

    def edge(src, dst, n, side, part):
        to_gx, to_gy = owner(row + (1 if side == 0 else -1))
        rows = pl.ds(8 + part * HALF, HALF)
        return pltpu.make_async_remote_copy(
            src_ref=src.at[rows], dst_ref=dst.at[rows],
            send_sem=s_edge.at[n, side, part], recv_sem=r_edge.at[n, side, part],
            device_id=(to_gx, to_gy), device_id_type=MESH)

    has_next, has_prev = row < WHOLE_Y - 1, row > 0

    def edges_start(src, prev, nxt, n, part):
        @pl.when(has_next)
        def _():
            edge(src, prev, n, 0, part).start()

        if n != BASIS - 1:
            @pl.when(has_prev)
            def _():
                edge(src, nxt, n, 1, part).start()

    def edges_wait(src, prev, nxt, n, part):
        @pl.when(has_prev)
        def _():
            edge(src, prev, n, 0, part).wait_recv()

        if n != BASIS - 1:
            @pl.when(has_next)
            def _():
                edge(src, nxt, n, 1, part).wait_recv()

    def edges_sent(src, prev, nxt, n, part):
        @pl.when(has_next)
        def _():
            edge(src, prev, n, 0, part).wait_send()

        if n != BASIS - 1:
            @pl.when(has_prev)
            def _():
                edge(src, nxt, n, 1, part).wait_send()

    own_y = pl.ds(OWN, ROWS)
    conduct = tissue[...].astype(jnp.float32) * gain[...]
    own = (pl.ds(HALO, PLANES), own_y, slice(None))
    fields[0, *own] = volt[...] + pot[...]
    fields[1, *own] = conduct
    fields[2, *own] = pot[...]
    pl.semaphore_wait(barrier, 25)
    near = fields.at[pl.ds(0, 2)]
    each_halo(start, near, 1, s_fields, r_fields, True)
    each_deep(start)
    each_halo(start, fields.at[2], 1, s_pot, r_pot, False)
    for d in range(1, 8):
        greet(far, at_z(lax.rem(chip_z + d, 8)))
    for d in range(1, 4):
        greet(far, at_y(lax.rem(chip_y + d, 4)))
    v = volt[...]
    ionic = tissue[...].astype(jnp.float32) * v * (v - onset_level) * (v - 1.0)
    own_term[...] = -ionic_rate * ionic

    for d, (a, b) in enumerate(DIRECTIONS):
        ok, _ = neighbour(-a, -b)

        @pl.when(jnp.logical_not(ok))
        def _():
            zd = z_range(a, HALO)[1]
            yd = y_range(b)[1]
            shape = (zd.size, yd.size, COLS)
            for n in range(3):
                fields[n, zd, yd, :] = jnp.zeros(shape, jnp.float32)
            resid[zd, yd, :] = jnp.zeros(shape, jnp.float32)
    stage_cond[...] = jnp.swapaxes(conduct, 0, 1)
    tile = jnp.zeros((8, COLS), jnp.float32)
    beyond = (pl.ds(0, 8), pl.ds(PAD_Y - 8, 8))

    def blank_rows(z, _):
        for rows in beyond:
            fields[1, z, rows, :] = tile
            weighted[0, z, rows, :] = tile
            weighted[1, z, rows, :] = tile
        return 0

    lax.fori_loop(0, EXT_Z, blank_rows, 0)
    ends = (pl.ds(0, 8), pl.ds(LINE - 8, 8))
    for rows in ends:
        for ref in (row_cond, row_res, cond_prev, cond_next):
            ref[rows] = tile
        for k in range(BASIS):
            for ref in (lines, line_prev, line_next):
                ref[k, rows] = tile
    blank = jnp.zeros((WHOLE_Z, COLS), jnp.float32)

    @pl.when(jnp.logical_not(has_prev))
    def _():
        cond_prev[LINES] = blank
        for k in range(BASIS):
            line_prev[k, LINES] = blank

    @pl.when(jnp.logical_not(has_next))
    def _():
        cond_next[LINES] = blank
        for k in range(BASIS):
            line_next[k, LINES] = blank

    whole = lax.dot_general(
        factor[...], factor[...], (((0,), (0,)), ((), ())), precision=HIGHEST,
        preferred_element_type=jnp.float32)
    in_sum = k_in[0]
    ex_sum = k_ex[0]
    for n in range(1, 9):
        in_sum = in_sum + k_in[n]
        ex_sum = ex_sum + k_ex[n]
    reach = jnp.max(jnp.sum(jnp.abs(whole), axis=1, keepdims=True), axis=0, keepdims=True)
    bound = reach * (4.0 * gain_top * in_sum + 4.0 * ex_sum)
    scaled = whole * (1.0 / bound)
    coarse = scaled.astype(jnp.bfloat16)
    matrix[0] = coarse
    matrix[1] = (scaled - coarse.astype(jnp.float32)).astype(jnp.bfloat16)
    eye = lax.broadcasted_iota(jnp.int32, whole.shape, 0) == lax.broadcasted_iota(jnp.int32, whole.shape, 1)
    mean = jnp.sum(jnp.sum(jnp.where(eye, whole, 0.0), axis=1, keepdims=True), axis=0, keepdims=True) / WHOLE_Z
    shift = SHIFT * mean * (2.0 * in_sum + 2.0 * ex_sum) / bound

    top = 1.0 + time_step * 4.0 * gain_top * in_sum
    ones = jnp.ones((1, COLS), jnp.float32)
    top = ones * top
    centre = (top + 1.0) / 2.0
    half = (top - 1.0) / 2.0
    ratio = centre / half
    weight = 1.0 / ratio

    each_halo(wait_recv, near, 1, s_fields, r_fields, True, receive=True)

    def moved(ref, z, at, rows):
        return lambda i, j: ref[z + i, pl.ds(at + j, rows), :]

    cond = fields.at[1]

    def weigh(z, _):
        weighted[0, z, EXT, :] = cond[z, EXT, :] * (fields[0, z, EXT, :])
        return 0

    lax.fori_loop(HALO - 1, HALO + PLANES + 1, weigh, 0)

    def first_plane(z, _):
        s = stencil(moved(cond, z, OWN, ROWS), z_twice, first, last)
        flux = s * fields[0, z, own_y, :] - stencil(moved(weighted.at[0], z, OWN, ROWS), z_twice, first, last)
        resid[z, own_y, :] = own_term[z - HALO] - cond[z, own_y, :] * flux
        return 0

    lax.fori_loop(HALO, HALO + PLANES, first_plane, 0)
    each_halo(start, resid, HALO, s_resid, r_resid, False)

    pl.semaphore_wait(far, 10)
    scatter_rows(stage_cond, row_cond, 0)
    each_deep(wait_recv, receive=True)

    def diag_plane(z, _):
        diag[z, EXT, :] = 1.0 + cond[z, EXT, :] * stencil(moved(cond, z, 8, EXT_Y), z_twice, first, last)
        return 0

    lax.fori_loop(1, EXT_Z - 1, diag_plane, 0)
    each_halo(wait_recv, fields.at[2], 1, s_pot, r_pot, False, receive=True)
    ex_total = 2.0 * ex_sum

    def extra_plane(z, _):
        ke = stencil(moved(fields.at[2], z, OWN, ROWS), z_extra, first, last)
        own_term[z - HALO] = ke - ex_total * fields[2, z, own_y, :]
        return 0

    lax.fori_loop(HALO, HALO + PLANES, extra_plane, 0)
    each_halo(wait_send, near, 1, s_fields, r_fields, True)
    each_halo(wait_recv, resid, HALO, s_resid, r_resid, False, receive=True)

    inv_centre = 1.0 / centre

    def first_update(z, _):
        u = resid[z, EXT, :] * inv_centre
        upd[z, EXT, :] = u
        estimate[z, EXT, :] = u
        weighted[0, z, EXT, :] = cond[z, EXT, :] * u
        return 0

    lax.fori_loop(0, EXT_Z, first_update, 0)

    def sweep(n, weight, margin):
        old = weighted.at[lax.rem(n + 1, 2)]
        new = lax.rem(n, 2)
        weight_next = 1.0 / (2.0 * ratio - weight)
        keep = weight_next * weight
        gain_r = 2.0 * weight_next / half
        at, count = OWN - margin, ROWS + 2 * margin
        rows = pl.ds(at, count)

        def one(z):
            u = upd[z, rows, :]
            c = cond[z, rows, :]
            r = resid[z, rows, :] - diag[z, rows, :] * u + c * stencil(moved(old, z, at, count), z_twice, first, last)
            fresh = keep * u + gain_r * r
            return r, fresh, estimate[z, rows, :] + fresh, c * fresh

        def pair(i, _):
            planes = [n + 2 * i, n + 2 * i + 1]
            for z, (r, fresh, total, flux) in zip(planes, [one(z) for z in planes]):
                resid[z, rows, :] = r
                upd[z, rows, :] = fresh
                estimate[z, rows, :] = total
                weighted[new, z, rows, :] = flux
            return 0

        lax.fori_loop(0, EXT_Z // 2 - n, pair, 0)
        return weight_next

    each_halo(wait_send, resid, HALO, s_resid, r_resid, False)
    weight = lax.fori_loop(1, 4, lambda n, w: sweep(n, w, 8), weight)
    weight = lax.fori_loop(4, CHEB - 2, lambda n, w: sweep(n, w, 4), weight)
    wait_rows(stage_cond, row_cond, 0)
    for half_line in range(2):
        edges_start(row_cond, cond_prev, cond_next, BASIS, half_line)
    lax.fori_loop(CHEB - 2, CHEB, lambda n, w: sweep(n, w, 4), weight)

    def total_plane(z, _):
        total = fields[0, z, EXT, :] + estimate[z, EXT, :]
        fields[0, z, EXT, :] = total
        weighted[0, z, EXT, :] = cond[z, EXT, :] * total
        return 0

    lax.fori_loop(HALO - 1, HALO + PLANES + 1, total_plane, 0)

    def elliptic_plane(z, _):
        twice = (diag[z, own_y, :] - 1.0) * fields[0, z, own_y, :]
        twice = twice - cond[z, own_y, :] * stencil(moved(weighted.at[0], z, OWN, ROWS), z_twice, first, last)
        own_term[z - HALO] = own_term[z - HALO] - twice / time_step
        return 0

    lax.fori_loop(HALO, HALO + PLANES, elliptic_plane, 0)
    stage_res[...] = jnp.swapaxes(own_term[...], 0, 1)
    scatter_rows(stage_res, row_res, 1)

    gain[...] = volt[...] + estimate[pl.ds(HALO, PLANES), own_y, :]
    early = pltpu.make_async_copy(gain, new_volt, s_take.at[0])
    early.start()
    wait_rows(stage_res, row_res, 1)

    def apply_matrix(src, k, shift=None):
        coarse = src.astype(jnp.bfloat16)
        fine = (src - coarse.astype(jnp.float32)).astype(jnp.bfloat16)

        def dot(a, b):
            return jnp.dot(a, b, preferred_element_type=jnp.float32)

        for part in range(2):
            rows = pl.ds(part * HALF, HALF)
            out = dot(matrix[0, rows], fine) + dot(matrix[1, rows], coarse) + dot(matrix[0, rows], coarse)
            if shift is not None:
                out = out - shift * lines[k - 1, pl.ds(8 + part * HALF, HALF)]
            lines[k, pl.ds(8 + part * HALF, HALF)] = out
            edges_start(lines.at[k], line_prev.at[k], line_next.at[k], k, part)

    sums = jnp.zeros((1, COLS), jnp.float32)

    def product(sums, e, a, b):
        total = jnp.sum((a * b).reshape(4, TILES // 4, 8, COLS), axis=0)
        total = jnp.sum(jnp.sum(total, axis=0), axis=0, keepdims=True)
        return sums + jnp.where(lane == e, jnp.sum(total, axis=1, keepdims=True), 0.0)

    CHUNK = 64

    def near_rows(refs, at):
        return lambda i, j: refs[i + 1][pl.ds(at + j, CHUNK), :]

    weigh_refs = [line_weighted.at[n] for n in range(3)]
    cond_refs = [cond_prev, row_cond, cond_next]

    def operate_here(k):
        basis = [None, lines.at[k], None]
        for at in range(8, 8 + WHOLE_Z, CHUNK):
            rows = pl.ds(at, CHUNK)
            ki = row_diag[rows] * lines[k, rows]
            ki = ki - row_cond[rows] * stencil_here(near_rows(weigh_refs, at), line_in, first, last)
            image[k, pl.ds(at - 8, CHUNK)] = ki - stencil_here(near_rows(basis, at), line_ex, first, last)

    def operate_beside(k):
        basis = [line_prev.at[k], None, line_next.at[k]]
        split = 8 + HALF
        for part, lined in enumerate((pl.ds(0, split), pl.ds(split, LINE - split))):
            edges_wait(lines.at[k], line_prev.at[k], line_next.at[k], k, part)
            for n in (0, 2) if k < BASIS - 1 else (0,):
                weigh_refs[n][lined] = cond_refs[n][lined] * basis[n][lined]
            for at in (range(8, split - CHUNK, CHUNK) if part == 0 else range(split - CHUNK, 8 + WHOLE_Z, CHUNK)):
                rows = pl.ds(at, CHUNK)
                beside = stencil_beside if k < BASIS - 1 else stencil_before
                ki = row_cond[rows] * beside(near_rows(weigh_refs, at), line_in, first, last)
                ki = ki + beside(near_rows(basis, at), line_ex, first, last)
                if k == BASIS - 1:
                    ki = 2.0 * ki
                image[k, pl.ds(at - 8, CHUNK)] = image[k, pl.ds(at - 8, CHUNK)] - ki

    def line_diag():
        for at in range(8, 8 + WHOLE_Z, CHUNK):
            rows = pl.ds(at, CHUNK)
            row_diag[rows] = ex_total + row_cond[rows] * stencil(near_rows(cond_refs, at), line_in, first, last)

    apply_matrix(row_res[inner], 0)
    send_back(0)
    weigh_refs[1][...] = row_cond[...] * lines[0]
    for half_line in range(2):
        edges_wait(row_cond, cond_prev, cond_next, BASIS, half_line)
    line_diag()
    operate_here(0)
    sums = product(sums, 0, lines[0, inner], row_res[inner])

    at = BASIS
    for k in range(BASIS):
        operate_beside(k)
        if k < BASIS - 1:
            apply_matrix(image[k], k + 1, shift)
            send_back(k + 1)
            weigh_refs[1][...] = row_cond[...] * lines[k + 1]
            operate_here(k + 1)
            sums = product(sums, k + 1, lines[k + 1, inner], row_res[inner])
            for m in range(k + 1):
                sums = product(sums, at, lines[m, inner], image[k])
                at += 1
            if k == BASIS - 2:
                for m in range(k + 1):
                    sums = product(sums, at, lines[k + 1, inner], image[m])
                    at += 1
        else:
            sums = product(sums, at, lines[k, inner], image[k])

    def sum_over(sums, buf, n, me, peers):
        part[...] = sums
        buf[me] = sums
        for to in peers:
            pltpu.make_async_remote_copy(
                src_ref=part, dst_ref=buf.at[me], send_sem=s_sum.at[n], recv_sem=r_sum.at[n],
                device_id=to, device_id_type=MESH).start()
        got = buf.at[pl.ds(0, 15)]
        pltpu.make_async_copy(got, got, r_sum.at[n]).wait()
        pltpu.make_async_copy(got, got, s_sum.at[n]).wait()
        return jnp.sum(buf[...], axis=0)

    def hops(d, n):
        return min(d, n - d)

    chip_x, core = spot // 2, spot % 2
    steps = sorted(((x, y) for x in range(4) for y in range(4) if (x, y) != (0, 0)),
                   key=lambda p: (-hops(p[0], 4) - hops(p[1], 4), p))
    sums = sum_over(sums, gather_a, 0, chip_x * 4 + chip_y, [
        ((gx // 8) * 8 + lax.rem(chip_x + x, 4) * 2 + core, lax.rem(chip_y + y, 4) * 2 + gy % 2)
        for x, y in steps])
    steps = sorted(((z, c) for z in range(8) for c in range(2) if (z, c) != (0, 0)),
                   key=lambda p: (-hops(p[0], 8) - 0.5 * p[1], p))
    peers = []
    for z, c in steps:
        to_z = lax.rem(chip_z + z, 8)
        peers.append(((to_z // 2) * 8 + chip_x * 2 + (core + c) % 2, chip_y * 2 + to_z % 2))
    sums = sum_over(sums, gather_b, 1, chip_z * 2 + core, peers)

    value = [jnp.sum(jnp.where(lane == e, sums, 0.0), axis=1, keepdims=True) for e in range(14)]
    rhs = value[:BASIS]
    gram = {}
    at = BASIS
    for k in range(BASIS):
        for m in range(k + 1):
            gram[m, k] = value[at]
            at += 1

    low, pivot = {}, {}
    for j in range(BASIS):
        d = gram[j, j]
        for m in range(j):
            d = d - low[j, m] * low[j, m] * pivot[m]
        pivot[j] = d
        for i in range(j + 1, BASIS):
            e = gram[j, i]
            for m in range(j):
                e = e - low[i, m] * low[j, m] * pivot[m]
            low[i, j] = e / d
    sol = list(rhs)
    for i in range(BASIS):
        for m in range(i):
            sol[i] = sol[i] - low[i, m] * sol[m]
    sol = [a / pivot[i] for i, a in enumerate(sol)]
    for i in reversed(range(BASIS)):
        for m in range(i + 1, BASIS):
            sol[i] = sol[i] - low[m, i] * sol[m]

    for k in range(BASIS):
        wait_back(k)
    total = sol[0] * back[0]
    for k in range(1, BASIS):
        total = total + sol[k] * back[k]
    new_pot[...] = pot[...] + jnp.swapaxes(total, 0, 1)

    early.wait()
    each_deep(wait_send)
    each_halo(wait_send, fields.at[2], 1, s_pot, r_pot, False)
    wait_rows_sent(stage_cond, 0)
    wait_rows_sent(stage_res, 1)
    for half_line in range(2):
        edges_sent(row_cond, cond_prev, cond_next, BASIS, half_line)
        for k in range(BASIS):
            edges_sent(lines.at[k], line_prev.at[k], line_next.at[k], k, half_line)


def body(voltage, potential, tissue, gain, couplings, line_factor):
    f32 = jnp.float32
    block = jax.ShapeDtypeStruct((PLANES, ROWS, COLS), f32)
    vmem = pl.BlockSpec(memory_space=pltpu.VMEM)
    line = (LINE, COLS)
    dma = pltpu.SemaphoreType.DMA
    return pl.pallas_call(
        kernel,
        name="bidomain",
        out_shape=(block, block),
        in_specs=[pl.BlockSpec(memory_space=pltpu.SMEM)] + [pl.BlockSpec(memory_space=pl.ANY)] * 5,
        out_specs=(pl.BlockSpec(memory_space=pl.ANY), vmem),
        scratch_shapes=[
            pltpu.VMEM((PLANES, ROWS, COLS), f32),
            pltpu.VMEM((PLANES, ROWS, COLS), f32),
            pltpu.VMEM((PLANES, ROWS, COLS), jnp.int32),
            pltpu.VMEM((PLANES, ROWS, COLS), f32),
            pltpu.VMEM((WHOLE_Z, WHOLE_Z), f32),
            pltpu.VMEM((3, EXT_Z, PAD_Y, COLS), f32),
            pltpu.VMEM((EXT_Z, PAD_Y, COLS), f32),
            pltpu.VMEM((EXT_Z, PAD_Y, COLS), f32),
            pltpu.VMEM((EXT_Z, PAD_Y, COLS), f32),
            pltpu.VMEM((EXT_Z, PAD_Y, COLS), f32),
            pltpu.VMEM((2, EXT_Z, PAD_Y, COLS), f32),
            pltpu.VMEM((PLANES, ROWS, COLS), f32),
            pltpu.VMEM((2, WHOLE_Z, WHOLE_Z), jnp.bfloat16),
            pltpu.VMEM((ROWS, PLANES, COLS), f32),
            pltpu.VMEM((ROWS, PLANES, COLS), f32),
            pltpu.VMEM(line, f32),
            pltpu.VMEM(line, f32),
            pltpu.VMEM((BASIS, *line), f32),
            pltpu.VMEM((BASIS, *line), f32),
            pltpu.VMEM((BASIS, *line), f32),
            pltpu.VMEM(line, f32),
            pltpu.VMEM(line, f32),
            pltpu.VMEM((3, *line), f32),
            pltpu.VMEM((BASIS, WHOLE_Z, COLS), f32),
            pltpu.VMEM(line, f32),
            pltpu.VMEM((BASIS, ROWS, PLANES, COLS), f32),
            pltpu.VMEM((1, COLS), f32),
            pltpu.VMEM((16, 1, COLS), f32),
            pltpu.VMEM((16, 1, COLS), f32),
            dma((8,)), dma((8,)), dma((8,)), dma((8,)), dma((8,)), dma((8,)), dma((8,)), dma((8,)),
            dma((2,)), dma((2,)), dma((BASIS + 1, 2, 2)), dma((BASIS + 1, 2, 2)),
            dma((BASIS,)), dma((BASIS,)), dma((2,)), dma((2,)), dma((5,)), pltpu.SemaphoreType.REGULAR,
        ],
        compiler_params=pltpu.CompilerParams(
            collective_id=0, has_side_effects=True, vmem_limit_bytes=67043328),
    )(couplings, voltage, potential, tissue, gain, line_factor)


def solution(mesh):
    block = P("gx", "gy", None)
    return jax.shard_map(
        body, mesh=mesh, in_specs=(block, block, block, block, P(), P()),
        out_specs=(block, block), check_vma=False)
```
